32 devices in a mesh: section: 2 (over core), dom: 8 (over z, x), cls: 2 (over y).
Axes of the slice: x: 2, y: 2, z: 4, core: 2. Of those that a mesh axis runs over, the one named last changes fastest.
Arguments:
- images: bfloat16 [1536, 128, 128], P(('dom', 'cls'), 'section'), may hold values from -6 to 6
- defocus_bin: int32 [1536], P(('dom', 'cls')), may hold values from 0 to 15
- ctf_kernels: float32 [16, 128], replicated, may hold values from -0.25 to 0.25
- band_kernel: float32 [128], replicated, may hold values from -0.25 to 0.25
- references: bfloat16 [200, 3, 128, 128], P('cls'), may hold values from -6 to 6
- rot_index: int32 [200, 3], P('cls'), may hold values from 0 to 3
- class_mask: int32 [1536, 200], P('dom', 'cls'), may hold values from 0 to 1, as said below
- noise_var: float32 [1536], P('dom'), may hold values from 20 to 200
Outputs:
- class_sums: float32 [200, 128, 128], P('cls', ('section', 'dom'))
The draws below stay inside these ranges and needn't reach their ends.
Inputs may be any that keep to these rules, and one draw needn't show every extreme that they name: `class_mask`: every particle may join at least one class.
All inputs are finite; a program needn't handle non-finite values.
Results may differ from the reference program's by a relative error of at most 0.012.
The reference program's roundings to bfloat16 on the way (of `filters`, `column_pass`, `filtered` and `weights`) count: a program that leaves them out, or rounds other values in their place, can miss the bound.
Values may be sent and summed in bfloat16 or wider, within the bound.
No kernel may reach another device: no remote copies, remote signals or barrier semaphores. Data moves between devices by JAX's collectives and lax.ppermute only.
A program may use at most 128 MiB of HBM per device.

```python
import math
import jax
import jax.numpy as jnp
from jax import lax

L = 128
K = 200
NROT = 3
NB = 16
PL = 96
PARTICLES = 1536


def draw_class_mask(key, part):
    first_key, second_key = jax.random.split(jax.random.fold_in(key, 17))
    chosen = jax.random.randint(first_key, (PARTICLES, K), 0, 2) == 0
    forced = jax.random.randint(second_key, (PARTICLES,), 0, K)
    columns = jnp.arange(K, dtype=jnp.int32)[None, :]
    return (chosen | (columns == forced[:, None])).astype(jnp.int32)


def draw_references(key, part):
    value_key = jax.random.fold_in(jax.random.fold_in(key, 29), 0)
    values = jax.random.normal(value_key, (K, NROT, L, L), jnp.float32)
    return jnp.clip(values, -6.0, 6.0).astype(jnp.bfloat16)


def set_ends(result, rng, smallest, high):
    longest = result.shape.index(max(result.shape))
    spots = []
    for shift in (0, 1):
        where = [jax.random.randint(jax.random.fold_in(rng, axis), (), 0, length) for axis, length in enumerate(result.shape)]
        where[longest] = (where[longest] + shift) % result.shape[longest]
        spots.append(tuple(where))
    return result.at[spots[0]].set(smallest).at[spots[1]].set(high)


def shard_levels(own_key, extent, cuts, smallest, top_value):
    loudness, own = 1.0, jax.random.fold_in(own_key, 6)
    for position, blocks in cuts:
        draws = jnp.exp(jax.random.uniform(jax.random.fold_in(own, position), (blocks,), jnp.float32, smallest / len(cuts), top_value / len(cuts)))
        loudness = loudness * jnp.repeat(draws, extent[position] // blocks).reshape([-1 if axis == position else 1 for axis in range(len(extent))])
    return loudness


def normal_values(rng, extent, scale, most, shards=(), kind=jnp.bfloat16):
    values = jax.random.normal(rng, extent, jnp.float32) * scale
    if len(shards) > 0:
        values = shard_levels(rng, extent, shards, -0.22, 0.18) * values
    return jnp.clip(values, min=-most, max=most).astype(kind)


def setup_inputs(seed: int = 0) -> dict:
    key_of = jax.random.split(jax.random.key(seed), 9)
    return {
        "images": normal_values(key_of[0], (PARTICLES, L, L), 1.0, 6.0, ((0, 16), (1, 2))),
        "defocus_bin": set_ends(jax.random.randint(key_of[1], (PARTICLES,), 0, NB), jax.random.fold_in(key_of[1], 1), 0, NB - 1).astype(jnp.int32),
        "ctf_kernels": normal_values(key_of[2], (NB, L), (4 * L) ** -0.5, 0.25, (), jnp.float32),
        "band_kernel": normal_values(key_of[3], (L,), (4 * L) ** -0.5, 0.25, (), jnp.float32),
        "references": draw_references(jax.random.fold_in(key_of[8], 71), 0),
        "rot_index": set_ends(jax.random.randint(key_of[5], (K, NROT), 0, 4), jax.random.fold_in(key_of[5], 1), 0, 3).astype(jnp.int32),
        "class_mask": draw_class_mask(jax.random.fold_in(key_of[8], 71), 0),
        "noise_var": jnp.clip(jnp.exp(math.log(200.0) - 2.3025851 * jax.random.uniform(key_of[7], (PARTICLES,), jnp.float32) ** shard_levels(key_of[7], (PARTICLES,), ((0, 8),), -0.2, 0.2)), 20.0, 200.0),
    }


def circulant(kernel):
    width = kernel.shape[-1]
    offsets = (jnp.arange(width)[:, None] - jnp.arange(width)[None, :]) % width
    return kernel[..., offsets]


def build_filters(ctf_kernels, band_kernel):
    width = band_kernel.shape[0]
    identity = jnp.eye(width, dtype=jnp.float32)
    band_filter = identity + circulant(band_kernel)
    phase_flip = identity[None] + circulant(ctf_kernels)
    return jnp.einsum('ri,bic->brc', band_filter, phase_flip, precision=lax.Precision.HIGHEST).astype(jnp.bfloat16)


def reference(images, defocus_bin, ctf_kernels, band_kernel, references, rot_index, class_mask, noise_var):
    filters = build_filters(ctf_kernels, band_kernel)
    stacked_images = images.reshape(PARTICLES // PL, PL, L, L)
    stacked_bins = defocus_bin.reshape(PARTICLES // PL, PL)

    def prefilter(pair):
        particle_block, bin_ids = pair
        picked = filters[bin_ids].astype(jnp.float32)
        column_pass = jnp.einsum('pij,pcj->pic', particle_block.astype(jnp.float32), picked).astype(jnp.bfloat16)
        return jnp.einsum('pri,pic->prc', picked, column_pass.astype(jnp.float32)).astype(jnp.bfloat16)

    filtered = lax.map(prefilter, (stacked_images, stacked_bins)).reshape(PARTICLES, L * L)
    refs_flat = references.reshape(K * NROT, L * L)
    half_norm = 0.5 * jnp.sum(jnp.square(refs_flat.astype(jnp.float32)), axis=1)
    inner_raw = jnp.dot(filtered, refs_flat.T, preferred_element_type=jnp.float32)
    scores = (inner_raw - half_norm[None, :]) / noise_var[:, None]
    allowed = jnp.repeat(class_mask > 0, NROT, axis=1)
    peak_score = jnp.max(jnp.where(allowed, scores, -1e30), axis=1)
    shifted = jnp.where(allowed, scores - peak_score[:, None], -1e30)
    expd = jnp.exp(shifted)
    denominator = jnp.sum(expd, axis=1)
    weights = (expd / denominator[:, None]).astype(jnp.bfloat16)
    partial_value = jnp.dot(weights.T, filtered, preferred_element_type=jnp.float32)
    stacked = partial_value.reshape(K, NROT, L, L)
    class_total = jnp.zeros((K, L, L), jnp.float32)
    for quarter in range(4):
        picked_sum = jnp.sum(jnp.where((rot_index == quarter)[:, :, None, None], stacked, 0.0), axis=1)
        class_total = class_total + jnp.rot90(picked_sum, (4 - quarter) % 4, axes=(1, 2))
    return class_total
```

```python
import functools

import jax
import jax.numpy as jnp
from jax import lax
from jax.experimental import pallas as pl
from jax.experimental.pallas import tpu as pltpu
from jax.sharding import PartitionSpec as P

F32 = jnp.float32
BF16 = jnp.bfloat16
LOW = -1e30
GROUP = 16
MIB = 1 << 20


def nt(a, b, precision=None):
    return lax.dot_general(
        a, b, (((1,), (1,)), ((), ())), preferred_element_type=F32, precision=precision
    )


def nn(a, b):
    return lax.dot_general(a, b, (((1,), (0,)), ((), ())), preferred_element_type=F32)


def anti_identity(width):
    rows = lax.broadcasted_iota(jnp.int32, (width, width), 0)
    cols = lax.broadcasted_iota(jnp.int32, (width, width), 1)
    return jnp.where(rows + cols == width - 1, 1.0, 0.0).astype(BF16)


def filters_kernel(ctf, ctf_rev, band, band_rev, left, right):
    bins, width = ctf.shape
    delta = jnp.where(lax.broadcasted_iota(jnp.int32, (1, width), 1) == 0, 1.0, 0.0)

    def rolled(row):
        return pltpu.roll(jnp.broadcast_to(row, (width, width)), 0, 1, stride=1, stride_axis=0)

    highest = lax.Precision.HIGHEST
    forward = nt(ctf[...] + delta, rolled(band_rev[...] + delta), highest)
    backward = nt(ctf_rev[...] + delta, rolled(band[...] + delta), highest)
    flip = anti_identity(width)
    for b in range(bins):
        a = rolled(backward[b : b + 1]).astype(BF16)
        a_t = rolled(forward[b : b + 1]).astype(BF16)
        left[b, :width] = a
        left[b, width:] = nn(flip, a).astype(BF16)
        right[b, :, :width] = a_t
        right[b, :, width:] = nn(a_t, flip).astype(BF16)


def build_filters(ctf, band):
    bins, width = ctf.shape

    def negate(v):
        return jnp.concatenate([v[:, :1], jnp.flip(v[:, 1:], 1)], axis=1)

    band = band.reshape(1, width)
    return pl.pallas_call(
        filters_kernel,
        out_shape=(
            jax.ShapeDtypeStruct((bins, 2 * width, width), BF16),
            jax.ShapeDtypeStruct((bins, width, 2 * width), BF16),
        ),
        name="filters",
    )(ctf, negate(ctf), band, negate(band))


def refs_kernel(refs, out, norm, scratch, *, padded):
    classes, rots, rows, width = refs.shape

    def block(start, count, j):
        for k in range(GROUP):
            if k < count:
                scratch[pl.ds(k * rows, rows)] = refs[start + k, j].astype(F32)
            else:
                scratch[pl.ds(k * rows, rows)] = jnp.zeros((rows, width), F32)
        at = pl.multiple_of(j * padded + start, GROUP)

        def step(r, acc):
            v = scratch[pl.ds(r, GROUP, stride=rows)]
            out[r, pl.ds(at, GROUP)] = v.astype(BF16)
            return acc + v * v

        acc = lax.fori_loop(0, rows, step, jnp.zeros((GROUP, width), F32), unroll=8)
        total = 0.5 * jnp.sum(acc, axis=1, keepdims=True)
        norm[pl.ds(at, GROUP)] = jnp.broadcast_to(total, (GROUP, width))

    full = classes // GROUP

    @pl.loop(0, full * rots)
    def _(i):
        block((i // rots) * GROUP, GROUP, i % rots)

    if classes % GROUP:

        @pl.loop(0, rots)
        def _(j):
            block(full * GROUP, classes % GROUP, j)


def lay_refs(refs, padded):
    classes, rots, rows, width = refs.shape
    return pl.pallas_call(
        functools.partial(refs_kernel, padded=padded),
        out_shape=(
            jax.ShapeDtypeStruct((rows, rots * padded, width), BF16),
            jax.ShapeDtypeStruct((rots * padded, width), F32),
        ),
        scratch_shapes=[pltpu.VMEM((GROUP * rows, width), F32)],
        compiler_params=pltpu.CompilerParams(vmem_limit_bytes=28 * MIB),
        name="refs",
    )(refs)


def filter_kernel(where, bins, mine, sib, left, right, plain, turned, scr, scr1, scr2, scr3):
    count, half, width = mine.shape
    top = where[0] == 0
    rows = lax.broadcasted_iota(jnp.int32, (width, width), 0)
    cols = lax.broadcasted_iota(jnp.int32, (width, width), 1)
    shift = where[0] * half
    target = jnp.where(rows < half, rows + shift, width - 1 - (rows - half + shift))
    pick = jnp.where(cols == target, 1.0, 0.0).astype(BF16)

    @pl.loop(0, count // GROUP)
    def _(g):
        base = pl.multiple_of(g * GROUP, GROUP)
        for i in range(GROUP):
            p = base + i
            b = bins[p]
            a = mine[p]
            o = sib[p]
            x = jnp.concatenate([jnp.where(top, a, o), jnp.where(top, o, a)], axis=0)
            cols_out = nn(x, right[b]).astype(BF16)
            both = nn(left[b], cols_out)
            scr[pl.ds(i * width, width)] = both[:width, :width]
            scr2[pl.ds(i * half, half)] = jnp.where(
                top, both[width : width + half, width:], both[width + half :, width:]
            )
            t = nt(pick, both[:, :width].astype(BF16))
            scr1[pl.ds(i * half, half)] = t[:half, width:]
            scr3[pl.ds(i * half, half)] = t[half:, :width]

        @pl.loop(0, width, unroll=8)
        def _(r):
            plain[r, pl.ds(base, GROUP)] = scr[pl.ds(r, GROUP, stride=width)].astype(BF16)

        @pl.loop(0, half, unroll=8)
        def _(r):
            turned[r, pl.ds(base, GROUP)] = scr[pl.ds(r + shift, GROUP, stride=width)].astype(BF16)
            for q, s in ((1, scr1), (2, scr2), (3, scr3)):
                turned[r, pl.ds(q * count + base, GROUP)] = s[
                    pl.ds(r, GROUP, stride=half)
                ].astype(BF16)


def filter_chunk(where, bins, mine, sib, left, right):
    count, half, width = mine.shape
    smem = pl.BlockSpec(memory_space=pltpu.SMEM)
    vmem = pl.BlockSpec(memory_space=pltpu.VMEM)
    return pl.pallas_call(
        filter_kernel,
        in_specs=[smem, smem, vmem, vmem, vmem, vmem],
        out_shape=(
            jax.ShapeDtypeStruct((2 * half, count, width), BF16),
            jax.ShapeDtypeStruct((half, 4 * count, width), BF16),
        ),
        scratch_shapes=[pltpu.VMEM((GROUP * 2 * half, width), F32)]
        + [pltpu.VMEM((GROUP * half, width), F32)] * 3,
        compiler_params=pltpu.CompilerParams(vmem_limit_bytes=24 * MIB),
        name="filter",
    )(where, bins, mine, sib, left, right)


def score_kernel(*args, parts):
    plains = args[:parts]
    refs, norm, mask, noise, scaled, stats = args[parts:]
    rows, height, width = refs.shape
    count = mask.shape[1]

    def step(i, acc):
        r = 2 * i
        lhs = jnp.concatenate([refs[r], refs[r + 1]], axis=1)
        rhs = jnp.concatenate(
            [jnp.concatenate([p[r], p[r + 1]], axis=1) for p in plains], axis=0
        )
        return acc + nt(lhs, rhs)

    inner = lax.fori_loop(0, rows // 2, step, jnp.zeros((height, count), F32), unroll=2)
    rots = height // mask.shape[0]
    allowed = jnp.concatenate([mask[...]] * rots, axis=0) > 0
    s = jnp.where(allowed, (inner - norm[:, :1]) / noise[...], LOW)
    scaled[...] = s
    peak = jnp.max(s, axis=0, keepdims=True)
    total = jnp.sum(jnp.exp(s - peak), axis=0, keepdims=True)
    stats[0:1] = peak
    stats[1:2] = total
    stats[2:] = jnp.zeros((stats.shape[0] - 2, count), F32)


def score(plains, refs, norm, mask, noise):
    count = mask.shape[1]
    height = refs.shape[1]
    return pl.pallas_call(
        functools.partial(score_kernel, parts=len(plains)),
        out_shape=(
            jax.ShapeDtypeStruct((height, count), F32),
            jax.ShapeDtypeStruct((8, count), F32),
        ),
        compiler_params=pltpu.CompilerParams(vmem_limit_bytes=28 * MIB),
        name="score",
    )(*plains, refs, norm, mask, noise)


def weights_kernel(scaled, mine, other, rot, out, *, sizes):
    rots, padded, count = rot.shape
    theirs = jnp.concatenate([other[:, count // 2 :], other[:, : count // 2]], axis=1)
    peak = jnp.maximum(mine[0:1], theirs[0:1])
    total = mine[1:2] * jnp.exp(mine[0:1] - peak) + theirs[1:2] * jnp.exp(theirs[0:1] - peak)
    w = (jnp.exp(scaled[...] - peak) / total).astype(BF16).astype(F32)
    quarters = []
    for q in range(4):
        acc = jnp.zeros((padded, count), F32)
        for j in range(rots):
            acc = acc + jnp.where(rot[j] == q, w[j * padded : (j + 1) * padded], 0.0)
        quarters.append(acc)
    pieces = []
    start = 0
    for size in sizes:
        pieces += [acc[:, start : start + size] for acc in quarters]
        start += size
    out[...] = jnp.concatenate(pieces, axis=1).astype(BF16)


def make_weights(scaled, mine, other, rot, sizes):
    rots, padded, count = rot.shape
    return pl.pallas_call(
        functools.partial(weights_kernel, sizes=sizes),
        out_shape=jax.ShapeDtypeStruct((padded, 4 * count), BF16),
        name="weights",
    )(scaled, mine, other, rot)


def sums_kernel(where, weights, *args, classes):
    turned = args[:-2]
    send, keep = args[-2:]
    rows = send.shape[1]
    parity = where[1]
    w = weights[...]
    for r in range(rows):
        rhs = jnp.concatenate(
            [jnp.concatenate([t[1 - parity, r], t[parity, r]], axis=1) for t in turned], axis=0
        )
        out = nn(w, rhs)
        width = out.shape[1] // 2
        send[0, r] = out[:classes, :width].astype(BF16)
        keep[0, r] = out[:classes, width:]


def sums(where, weights, turned, chunk, rows, classes):
    dom = turned[0].shape[0]
    width = turned[0].shape[3]
    padded = weights.shape[0]
    return pl.pallas_call(
        functools.partial(sums_kernel, classes=classes),
        grid=(dom // 2,),
        in_specs=[
            pl.BlockSpec(memory_space=pltpu.SMEM),
            pl.BlockSpec(weights.shape, lambda g: (0, 0)),
        ]
        + [
            pl.BlockSpec((2, rows, t.shape[2], width), lambda g: (g, chunk, 0, 0)) for t in turned
        ],
        out_specs=(
            pl.BlockSpec((1, rows, classes, width), lambda g: (g, 0, 0, 0)),
            pl.BlockSpec((1, rows, classes, width), lambda g: (g, 0, 0, 0)),
        ),
        out_shape=(
            jax.ShapeDtypeStruct((dom // 2, rows, classes, width), BF16),
            jax.ShapeDtypeStruct((dom // 2, rows, classes, width), F32),
        ),
        compiler_params=pltpu.CompilerParams(vmem_limit_bytes=16 * MIB),
        name="sums",
    )(where, weights, *turned)


def local(
    images, defocus_bin, ctf_kernels, band_kernel, references, rot_index, class_mask, noise_var
):
    section_at = lax.axis_index("section")
    class_at = lax.axis_index("cls")
    dom_at = lax.axis_index("dom")
    dom = lax.axis_size("dom")
    particles, half, width = images.shape
    classes, rots = rot_index.shape
    padded = -(-classes // GROUP) * GROUP
    swap = [(0, 1), (1, 0)]
    over_cls = functools.partial(lax.ppermute, axis_name="cls", perm=swap)
    over_section = functools.partial(lax.ppermute, axis_name="section", perm=swap)

    cut = particles // 2
    sizes = (particles, cut, particles - cut)
    other_bins = over_cls(defocus_bin)
    remote = [over_cls(images[:cut]), over_cls(images[cut:])]
    own_sib = over_section(images)

    where = jnp.stack([section_at, dom_at % 2]).astype(jnp.int32)
    left, right = build_filters(ctf_kernels, band_kernel)
    refs, norm = lay_refs(references, padded)

    def arranged(a):
        parts = a.reshape((2, particles) + a.shape[1:])
        return jnp.concatenate(
            [
                lax.dynamic_index_in_dim(parts, class_at, 0, False),
                lax.dynamic_index_in_dim(parts, 1 - class_at, 0, False),
            ]
        )

    mask = jnp.pad(arranged(class_mask).T, ((0, padded - classes), (0, 0)))
    noise = arranged(noise_var).reshape(1, 2 * particles)
    rot = jnp.broadcast_to(
        jnp.pad(rot_index.T, ((0, 0), (0, padded - classes)))[:, :, None],
        (rots, padded, 2 * particles),
    )

    plains, turned = [], []
    plain, turn = filter_chunk(where, defocus_bin, images, own_sib, left, right)
    plains.append(plain)
    turned.append(turn)
    start = 0
    for piece in remote:
        n = piece.shape[0]
        plain, turn = filter_chunk(
            where, other_bins[start : start + n], piece, over_section(piece), left, right
        )
        start += n
        plains.append(plain)
        turned.append(turn)

    scaled, stats = score(plains, refs, norm, mask, noise)
    weights = make_weights(scaled, stats, over_cls(stats), rot, sizes)

    block_rows = half // dom
    turned = [t.reshape(dom, block_rows, t.shape[1], width) for t in turned]
    chunks = min(2, block_rows)
    rows = block_rows // chunks
    done = []
    for c in range(chunks):
        send, keep = sums(where, weights, turned, c, rows, classes)
        got = lax.ppermute(send, "dom", [(i, i ^ 1) for i in range(dom)])
        bit = 1
        while keep.shape[0] > 1:
            kept = keep.reshape((keep.shape[0] // 2, 2) + keep.shape[1:])
            came = got.reshape(kept.shape)
            mine = (dom_at >> bit) & 1

            def pick(index):
                return lax.dynamic_index_in_dim(
                    kept, index, 1, False
                ) + lax.dynamic_index_in_dim(came, index, 1, False).astype(F32)

            send = pick(1 - mine).astype(BF16)
            keep = pick(mine)
            got = lax.ppermute(send, "dom", [(i, i ^ (1 << bit)) for i in range(dom)])
            bit += 1
        done.append(keep[0] + got[0].astype(F32))
    return jnp.transpose(jnp.concatenate(done, axis=0), (1, 0, 2))


def solution(mesh):
    return jax.shard_map(
        local,
        mesh=mesh,
        in_specs=(
            P(("dom", "cls"), "section", None),
            P(("dom", "cls")),
            P(),
            P(),
            P("cls", None, None, None),
            P("cls", None),
            P("dom", "cls"),
            P("dom"),
        ),
        out_specs=P("cls", ("section", "dom"), None),
        check_vma=False,
    )
```

```python
import functools

import jax
import jax.numpy as jnp
from jax import lax
from jax.experimental import pallas as pl
from jax.experimental.pallas import tpu as pltpu
from jax.sharding import PartitionSpec as P

F32 = jnp.float32
BF16 = jnp.bfloat16
LOW = -1e30
GROUP = 16
PAD = 8
DEEP = 16
MIB = 1 << 20


def nt(a, b, precision=None):
    return lax.dot_general(
        a, b, (((1,), (1,)), ((), ())), preferred_element_type=F32, precision=precision
    )


def nn(a, b):
    return lax.dot_general(a, b, (((1,), (0,)), ((), ())), preferred_element_type=F32)


def cost(microseconds):
    return pl.CostEstimate(
        flops=int(microseconds * 1e9), transcendentals=0, bytes_accessed=int(microseconds * 3e6)
    )


def filters_kernel(ctf, ctf_rev, band, band_rev, left, right):
    bins, width = ctf.shape
    delta = jnp.where(lax.broadcasted_iota(jnp.int32, (1, width), 1) == 0, 1.0, 0.0)

    def rolled(row):
        return pltpu.roll(jnp.broadcast_to(row, (width, width)), 0, 1, stride=1, stride_axis=0)

    highest = lax.Precision.HIGHEST
    forward = nt(ctf[...] + delta, rolled(band_rev[...] + delta), highest)
    backward = nt(ctf_rev[...] + delta, rolled(band[...] + delta), highest)
    for b in range(bins):
        left[b] = rolled(backward[b : b + 1]).astype(BF16)
        right[b] = rolled(forward[b : b + 1]).astype(BF16)


def build_filters(ctf, band):
    bins, width = ctf.shape

    def negate(v):
        return jnp.concatenate([v[:, :1], jnp.flip(v[:, 1:], 1)], axis=1)

    band = band.reshape(1, width)
    return pl.pallas_call(
        filters_kernel,
        out_shape=(
            jax.ShapeDtypeStruct((bins, width, width), BF16),
            jax.ShapeDtypeStruct((bins, width, width), BF16),
        ),
        cost_estimate=cost(3),
        name="filters",
    )(ctf, negate(ctf), band, negate(band))


def refs_kernel(refs, out, norm, scratch, *, padded):
    classes, rots, rows, width = refs.shape
    pitch = rows + PAD

    def block(start, count, j):
        for k in range(GROUP):
            if k < count:
                scratch[pl.ds(k * pitch, rows)] = refs[start + k, j].astype(F32)
            else:
                scratch[pl.ds(k * pitch, rows)] = jnp.zeros((rows, width), F32)
        at = pl.multiple_of(j * padded + start, GROUP)

        def step(r, acc):
            v = scratch[pl.ds(r, GROUP, stride=pitch)]
            out[r, pl.ds(at, GROUP)] = v.astype(BF16)
            return acc + v * v

        acc = lax.fori_loop(0, rows, step, jnp.zeros((GROUP, width), F32), unroll=32)
        total = 0.5 * jnp.sum(acc, axis=1, keepdims=True)
        norm[pl.ds(at, GROUP)] = jnp.broadcast_to(total, (GROUP, width))

    full = classes // GROUP

    @pl.loop(0, full * rots)
    def _(i):
        block((i // rots) * GROUP, GROUP, i % rots)

    if classes % GROUP:

        @pl.loop(0, rots)
        def _(j):
            block(full * GROUP, classes % GROUP, j)


def lay_refs(refs, padded):
    classes, rots, rows, width = refs.shape
    return pl.pallas_call(
        functools.partial(refs_kernel, padded=padded),
        out_shape=(
            jax.ShapeDtypeStruct((rows, rots * padded, width), BF16),
            jax.ShapeDtypeStruct((rots * padded, width), F32),
        ),
        scratch_shapes=[pltpu.VMEM((GROUP * (rows + PAD), width), F32)],
        compiler_params=pltpu.CompilerParams(vmem_limit_bytes=28 * MIB),
        cost_estimate=cost(11),
        name="refs",
    )(refs)


def filter_kernel(where, bins, mine, sib, left, right, plain, turned, scr, scr_t):
    count, half, width = mine.shape
    top = where[0] == 0
    pitch = width + PAD

    @pl.loop(0, count // GROUP)
    def _(g):
        base = pl.multiple_of(g * GROUP, GROUP)
        for i in range(GROUP):
            b = bins[base + i]
            a = mine[base + i]
            o = sib[base + i]
            x = jnp.concatenate([jnp.where(top, a, o), jnp.where(top, o, a)], axis=0)
            f = nn(left[b], nn(x, right[b]).astype(BF16))
            scr[pl.ds(i * pitch, width)] = f
            scr_t[pl.ds(i * pitch, width)] = f.T
        for r in range(width):
            plain[r, pl.ds(base, GROUP)] = scr[pl.ds(r, GROUP, stride=pitch)].astype(BF16)
            turned[r, pl.ds(base, GROUP)] = scr_t[pl.ds(r, GROUP, stride=pitch)].astype(BF16)


def filter_chunk(where, bins, mine, sib, left, right):
    count, half, width = mine.shape
    smem = pl.BlockSpec(memory_space=pltpu.SMEM)
    vmem = pl.BlockSpec(memory_space=pltpu.VMEM)
    return pl.pallas_call(
        filter_kernel,
        in_specs=[smem, smem, vmem, vmem, vmem, vmem],
        out_shape=(jax.ShapeDtypeStruct((2 * half, count, width), BF16),) * 2,
        scratch_shapes=[pltpu.VMEM((GROUP * (2 * half + PAD), width), F32)] * 2,
        compiler_params=pltpu.CompilerParams(vmem_limit_bytes=16 * MIB),
        cost_estimate=cost(count * 0.1),
        name="filter",
    )(where, bins, mine, sib, left, right)


def score_kernel(*args, parts):
    plains = args[:parts]
    refs, norm, mask, noise, scaled, stats = args[parts:]
    rows, height, width = refs.shape
    count = mask.shape[1]

    def step(i, acc):
        at = [DEEP * i + a for a in range(DEEP)]
        lhs = jnp.concatenate([refs[r] for r in at], axis=1)
        rhs = jnp.concatenate(
            [jnp.concatenate([p[r] for r in at], axis=1) for p in plains], axis=0
        )
        return acc + nt(lhs, rhs)

    inner = lax.fori_loop(0, rows // DEEP, step, jnp.zeros((height, count), F32))
    rots = height // mask.shape[0]
    allowed = jnp.concatenate([mask[...]] * rots, axis=0) > 0
    s = jnp.where(allowed, (inner - norm[:, :1]) / noise[...], LOW)
    scaled[...] = s
    peak = jnp.max(s, axis=0, keepdims=True)
    total = jnp.sum(jnp.exp(s - peak), axis=0, keepdims=True)
    stats[0:1] = peak
    stats[1:2] = total
    stats[2:] = jnp.zeros((stats.shape[0] - 2, count), F32)


def score(plains, refs, norm, mask, noise):
    count = mask.shape[1]
    height = refs.shape[1]
    return pl.pallas_call(
        functools.partial(score_kernel, parts=len(plains)),
        out_shape=(
            jax.ShapeDtypeStruct((height, count), F32),
            jax.ShapeDtypeStruct((8, count), F32),
        ),
        compiler_params=pltpu.CompilerParams(vmem_limit_bytes=28 * MIB),
        cost_estimate=cost(5),
        name="score",
    )(*plains, refs, norm, mask, noise)


def weights_kernel(scaled, mine, other, rot, out, *, sizes):
    rots, padded, count = rot.shape
    theirs = jnp.concatenate([other[:, count // 2 :], other[:, : count // 2]], axis=1)
    peak = jnp.maximum(mine[0:1], theirs[0:1])
    total = mine[1:2] * jnp.exp(mine[0:1] - peak) + theirs[1:2] * jnp.exp(theirs[0:1] - peak)
    w = (jnp.exp(scaled[...] - peak) / total).astype(BF16).astype(F32)
    quarters = []
    for q in range(4):
        acc = jnp.zeros((padded, count), F32)
        for j in range(rots):
            acc = acc + jnp.where(rot[j] == q, w[j * padded : (j + 1) * padded], 0.0)
        quarters.append(acc)
    for row, pair in enumerate(((0, 3), (2, 1))):
        pieces = []
        start = 0
        for size in sizes:
            pieces += [quarters[q][:, start : start + size] for q in pair]
            start += size
        out[row] = jnp.concatenate(pieces, axis=1).astype(BF16)


def make_weights(scaled, mine, other, rot, sizes):
    rots, padded, count = rot.shape
    return pl.pallas_call(
        functools.partial(weights_kernel, sizes=sizes),
        out_shape=jax.ShapeDtypeStruct((2, padded, 2 * count), BF16),
        cost_estimate=cost(2),
        name="weights",
    )(scaled, mine, other, rot)


def sums_kernel(where, weights, *args, parts, dom, chunk, classes):
    plains = args[:parts]
    turned = args[parts : 2 * parts]
    send, keep = args[2 * parts :]
    width = send.shape[3]
    rows = send.shape[1]
    height = plains[0].shape[0]
    block = height // 2 // dom
    first = where[0] * (height // 2) + chunk * rows
    parity = where[1]
    straight = weights[0]
    mirrored = weights[1]
    flip = width - 1 - lax.broadcasted_iota(jnp.int32, (straight.shape[0], width), 1)

    def stacked(up, down):
        return jnp.concatenate(
            [ref[at] for p, t in zip(plains, turned) for ref, at in ((p, up), (t, down))], axis=0
        )

    def one(g, r, rhs_at):
        return first + (2 * g + rhs_at) * block + r

    @pl.loop(0, dom // 2)
    def _(g):
        for r in range(rows):
            away = one(g, r, 1 - parity)
            here = one(g, r, parity)
            direct = nn(
                straight,
                jnp.concatenate(
                    [stacked(i, height - 1 - i) for i in (away, here)], axis=1
                ),
            )
            mirror = nn(
                mirrored,
                jnp.concatenate(
                    [stacked(height - 1 - i, i) for i in (away, here)], axis=1
                ),
            )
            out = [
                direct[:, at : at + width]
                + jnp.take_along_axis(mirror[:, at : at + width], flip, axis=1)
                for at in (0, width)
            ]
            send[g, r] = out[0][:classes].astype(BF16)
            keep[g, r] = out[1][:classes]


def sums(where, weights, plains, turned, dom, chunk, rows, classes):
    width = plains[0].shape[2]
    smem = pl.BlockSpec(memory_space=pltpu.SMEM)
    vmem = pl.BlockSpec(memory_space=pltpu.VMEM)
    return pl.pallas_call(
        functools.partial(
            sums_kernel, parts=len(plains), dom=dom, chunk=chunk, classes=classes
        ),
        in_specs=[smem] + [vmem] * (1 + 2 * len(plains)),
        out_shape=(
            jax.ShapeDtypeStruct((dom // 2, rows, classes, width), BF16),
            jax.ShapeDtypeStruct((dom // 2, rows, classes, width), F32),
        ),
        compiler_params=pltpu.CompilerParams(vmem_limit_bytes=24 * MIB),
        cost_estimate=cost(3),
        name="sums",
    )(where, weights, *plains, *turned)


def local(
    images, defocus_bin, ctf_kernels, band_kernel, references, rot_index, class_mask, noise_var
):
    section_at = lax.axis_index("section")
    class_at = lax.axis_index("cls")
    dom_at = lax.axis_index("dom")
    dom = lax.axis_size("dom")
    particles, half, width = images.shape
    classes, rots = rot_index.shape
    padded = -(-classes // GROUP) * GROUP
    swap = [(0, 1), (1, 0)]
    over_cls = functools.partial(lax.ppermute, axis_name="cls", perm=swap)
    over_section = functools.partial(lax.ppermute, axis_name="section", perm=swap)

    cut = (particles * 2 // 3) // GROUP * GROUP
    sizes = (particles, cut, particles - cut)
    other_bins = over_cls(defocus_bin)
    remote = [over_cls(images[:cut]), over_cls(images[cut:])]
    own_sib = over_section(images)

    where = jnp.stack([section_at, dom_at % 2]).astype(jnp.int32)
    left, right = build_filters(ctf_kernels, band_kernel)
    refs, norm = lay_refs(references, padded)

    def arranged(a):
        parts = a.reshape((2, particles) + a.shape[1:])
        return jnp.concatenate(
            [
                lax.dynamic_index_in_dim(parts, class_at, 0, False),
                lax.dynamic_index_in_dim(parts, 1 - class_at, 0, False),
            ]
        )

    mask = jnp.pad(arranged(class_mask).T, ((0, padded - classes), (0, 0)))
    noise = arranged(noise_var).reshape(1, 2 * particles)
    rot = jnp.broadcast_to(
        jnp.pad(rot_index.T, ((0, 0), (0, padded - classes)))[:, :, None],
        (rots, padded, 2 * particles),
    )

    plains, turned = [], []
    plain, turn = filter_chunk(where, defocus_bin, images, own_sib, left, right)
    plains.append(plain)
    turned.append(turn)
    start = 0
    for piece in remote:
        n = piece.shape[0]
        plain, turn = filter_chunk(
            where, other_bins[start : start + n], piece, over_section(piece), left, right
        )
        start += n
        plains.append(plain)
        turned.append(turn)

    scaled, stats = score(plains, refs, norm, mask, noise)
    weights = make_weights(scaled, stats, over_cls(stats), rot, sizes)

    block_rows = half // dom
    chunks = min(2, block_rows)
    rows = block_rows // chunks
    done = []
    for c in range(chunks):
        send, keep = sums(where, weights, plains, turned, dom, c, rows, classes)
        got = lax.ppermute(send, "dom", [(i, i ^ 1) for i in range(dom)])
        bit = 1
        while keep.shape[0] > 1:
            kept = keep.reshape((keep.shape[0] // 2, 2) + keep.shape[1:])
            came = got.reshape(kept.shape)
            mine = (dom_at >> bit) & 1

            def pick(index):
                return lax.dynamic_index_in_dim(
                    kept, index, 1, False
                ) + lax.dynamic_index_in_dim(came, index, 1, False).astype(F32)

            send = pick(1 - mine).astype(BF16)
            keep = pick(mine)
            got = lax.ppermute(send, "dom", [(i, i ^ (1 << bit)) for i in range(dom)])
            bit += 1
        done.append(keep[0] + got[0].astype(F32))
    return jnp.transpose(jnp.concatenate(done, axis=0), (1, 0, 2))


def solution(mesh):
    return jax.shard_map(
        local,
        mesh=mesh,
        in_specs=(
            P(("dom", "cls"), "section", None),
            P(("dom", "cls")),
            P(),
            P(),
            P("cls", None, None, None),
            P("cls", None),
            P("dom", "cls"),
            P("dom"),
        ),
        out_specs=P("cls", ("section", "dom"), None),
        check_vma=False,
    )
```

```python
import functools

import jax
import jax.numpy as jnp
from jax import lax
from jax.experimental import pallas as pl
from jax.experimental.pallas import tpu as pltpu
from jax.sharding import PartitionSpec as P

F32 = jnp.float32
BF16 = jnp.bfloat16
LOW = -1e30
GROUP = 16
PAD = 8
DEEP = 16
MIB = 1 << 20


def nt(a, b, precision=None):
    return lax.dot_general(
        a, b, (((1,), (1,)), ((), ())), preferred_element_type=F32, precision=precision
    )


def nn(a, b):
    return lax.dot_general(a, b, (((1,), (0,)), ((), ())), preferred_element_type=F32)


def cost(microseconds):
    return pl.CostEstimate(
        flops=int(microseconds * 1e9), transcendentals=0, bytes_accessed=int(microseconds * 3e6)
    )


def pinned(shape, dtype):
    return pltpu.VMEM(shape, dtype)


def held(x):
    return pltpu.with_memory_space_constraint(x, pltpu.VMEM)


def filters_kernel(ctf, band, left, right):
    bins, width = ctf.shape

    def negated(v):
        at = (width - lax.broadcasted_iota(jnp.int32, v.shape, 1)) % width
        return jnp.take_along_axis(v, at, axis=1)

    def rolled(row):
        return pltpu.roll(jnp.broadcast_to(row, (width, width)), 0, 1, stride=1, stride_axis=0)

    def with_delta(v):
        return v + jnp.where(lax.broadcasted_iota(jnp.int32, v.shape, 1) == 0, 1.0, 0.0)

    highest = lax.Precision.HIGHEST
    kernels = with_delta(ctf[...])
    bands = with_delta(jnp.broadcast_to(band[...], (8, width)))
    forward = nt(kernels, rolled(negated(bands)[:1]), highest)
    backward = nt(negated(kernels), rolled(bands[:1]), highest)
    for b in range(bins):
        left[b] = rolled(backward[b : b + 1]).astype(BF16)
        right[b] = rolled(forward[b : b + 1]).astype(BF16)


def build_filters(ctf, band):
    bins, width = ctf.shape
    return pl.pallas_call(
        filters_kernel,
        out_shape=(pinned((bins, width, width), BF16),) * 2,
        cost_estimate=cost(3),
        name="filters",
    )(ctf, band.reshape(1, width))


def refs_kernel(refs, out, norm, scratch, *, padded):
    classes, _, rows, width = refs.shape
    pitch = rows + PAD
    j = pl.program_id(0)

    def block(start, count):
        for k in range(GROUP):
            if k < count:
                scratch[pl.ds(k * pitch, rows)] = refs[start + k, 0].astype(F32)
            else:
                scratch[pl.ds(k * pitch, rows)] = jnp.zeros((rows, width), F32)
        at = pl.multiple_of(j * padded + start, GROUP)

        def step(r, acc):
            v = scratch[pl.ds(r, GROUP, stride=pitch)]
            out[r, pl.ds(at, GROUP)] = v.astype(BF16)
            return acc + v * v

        acc = lax.fori_loop(0, rows, step, jnp.zeros((GROUP, width), F32), unroll=32)
        total = 0.5 * jnp.sum(acc, axis=1, keepdims=True)
        norm[pl.ds(at, GROUP)] = jnp.broadcast_to(total, (GROUP, width))

    full = classes // GROUP

    @pl.loop(0, full)
    def _(i):
        block(i * GROUP, GROUP)

    if classes % GROUP:
        block(full * GROUP, classes % GROUP)


def lay_refs(refs, padded):
    classes, rots, rows, width = refs.shape
    vmem = pl.BlockSpec(memory_space=pltpu.VMEM)
    return pl.pallas_call(
        functools.partial(refs_kernel, padded=padded),
        grid=(rots,),
        in_specs=[pl.BlockSpec((classes, 1, rows, width), lambda j: (0, j, 0, 0))],
        out_specs=(vmem, vmem),
        out_shape=(
            pinned((rows, rots * padded, width), BF16),
            pinned((rots * padded, width), F32),
        ),
        scratch_shapes=[pltpu.VMEM((GROUP * (rows + PAD), width), F32)],
        compiler_params=pltpu.CompilerParams(vmem_limit_bytes=28 * MIB),
        cost_estimate=cost(9),
        name="refs",
    )(pltpu.with_memory_space_constraint(refs, pltpu.HBM))


def filter_kernel(where, bins, mine, sib, left, right, *rest, skip, at):
    plain, turned, scr, scr_t = rest[-4:]
    count, half, width = mine.shape
    top = where[0] == 0
    pitch = width + PAD

    @pl.loop(0, count // GROUP)
    def _(g):
        base = pl.multiple_of(g * GROUP, GROUP)
        for i in range(GROUP):
            b = bins[skip + base + i]
            a = mine[base + i]
            o = sib[base + i]
            x = jnp.concatenate([jnp.where(top, a, o), jnp.where(top, o, a)], axis=0)
            f = nn(left[b], nn(x, right[b]).astype(BF16))
            scr[pl.ds(i * pitch, width)] = f
            scr_t[pl.ds(i * pitch, width)] = f.T
        to = pl.multiple_of(at + base, GROUP)
        for r in range(width):
            plain[r, pl.ds(to, GROUP)] = scr[pl.ds(r, GROUP, stride=pitch)].astype(BF16)
            turned[r, pl.ds(to, GROUP)] = scr_t[pl.ds(r, GROUP, stride=pitch)].astype(BF16)


def filter_chunk(where, bins, mine, sib, left, right, buffers, total, skip, at):
    count, half, width = mine.shape
    smem = pl.BlockSpec(memory_space=pltpu.SMEM)
    vmem = pl.BlockSpec(memory_space=pltpu.VMEM)
    buffers = [held(b) for b in buffers]
    return pl.pallas_call(
        functools.partial(filter_kernel, skip=skip, at=at),
        in_specs=[smem, smem] + [vmem] * (4 + len(buffers)),
        out_specs=(vmem, vmem),
        out_shape=(pinned((2 * half, total, width), BF16),) * 2,
        scratch_shapes=[pltpu.VMEM((GROUP * (2 * half + PAD), width), F32)] * 2,
        input_output_aliases={6 + i: i for i in range(len(buffers))},
        compiler_params=pltpu.CompilerParams(vmem_limit_bytes=24 * MIB),
        cost_estimate=cost(count * 0.1),
        name="filter",
    )(where, bins, mine, sib, held(left), held(right), *buffers)


def score_kernel(plain, refs, norm, mask, noise, scaled, stats):
    rows, height, width = refs.shape
    count = mask.shape[1]

    def step(i, acc):
        at = [DEEP * i + a for a in range(DEEP)]
        lhs = jnp.concatenate([refs[r] for r in at], axis=1)
        rhs = jnp.concatenate([plain[r] for r in at], axis=1)
        return acc + nt(lhs, rhs)

    inner = lax.fori_loop(0, rows // DEEP, step, jnp.zeros((height, count), F32))
    rots = height // mask.shape[0]
    allowed = jnp.concatenate([mask[...]] * rots, axis=0) > 0
    s = jnp.where(allowed, (inner - norm[:, :1]) / noise[...], LOW)
    scaled[...] = s
    peak = jnp.max(s, axis=0, keepdims=True)
    total = jnp.sum(jnp.exp(s - peak), axis=0, keepdims=True)
    stats[0:1] = peak
    stats[1:2] = total
    stats[2:] = jnp.zeros((stats.shape[0] - 2, count), F32)


def score(plain, refs, norm, mask, noise):
    count = mask.shape[1]
    height = refs.shape[1]
    return pl.pallas_call(
        score_kernel,
        out_shape=(
            pinned((height, count), F32),
            pinned((8, count), F32),
        ),
        compiler_params=pltpu.CompilerParams(vmem_limit_bytes=24 * MIB),
        cost_estimate=cost(5),
        name="score",
    )(held(plain), held(refs), held(norm), mask, noise)


def weights_kernel(scaled, mine, other, rot, out):
    rots, padded, _ = rot.shape
    count = scaled.shape[1]
    theirs = jnp.concatenate([other[:, count // 2 :], other[:, : count // 2]], axis=1)
    peak = jnp.maximum(mine[0:1], theirs[0:1])
    total = mine[1:2] * jnp.exp(mine[0:1] - peak) + theirs[1:2] * jnp.exp(theirs[0:1] - peak)
    w = (jnp.exp(scaled[...] - peak) / total).astype(BF16).astype(F32)
    quarters = []
    for q in range(4):
        acc = jnp.zeros((padded, count), F32)
        for j in range(rots):
            acc = acc + jnp.where(rot[j] == q, w[j * padded : (j + 1) * padded], 0.0)
        quarters.append(acc)
    for row, pair in enumerate(((0, 3), (2, 1))):
        out[row] = jnp.concatenate([quarters[q] for q in pair], axis=1).astype(BF16)


def make_weights(scaled, mine, other, rot):
    _, padded, _ = rot.shape
    count = scaled.shape[1]
    return pl.pallas_call(
        weights_kernel,
        out_shape=pinned((2, padded, 2 * count), BF16),
        cost_estimate=cost(2),
        name="weights",
    )(held(scaled), held(mine), other, rot)


def sums_kernel(where, weights, plain, turned, send, keep, *, dom, start, classes):
    _, rows, _, width = send.shape
    height = plain.shape[0]
    block = height // 2 // dom
    first = where[0] * (height // 2) + start
    parity = where[1]
    straight = weights[0]
    mirrored = weights[1]
    flip = width - 1 - lax.broadcasted_iota(jnp.int32, (straight.shape[0], width), 1)

    @pl.loop(0, dom // 2)
    def _(g):
        for r in range(rows):
            both = [first + (2 * g + side) * block + r for side in (1 - parity, parity)]
            direct = jnp.concatenate(
                [jnp.concatenate([plain[i], turned[height - 1 - i]], axis=0) for i in both], axis=1
            )
            mirror = jnp.concatenate(
                [jnp.concatenate([plain[height - 1 - i], turned[i]], axis=0) for i in both], axis=1
            )
            direct = nn(straight, direct)
            mirror = nn(mirrored, mirror)
            away, here = [
                direct[:, at : at + width]
                + jnp.take_along_axis(mirror[:, at : at + width], flip, axis=1)
                for at in (0, width)
            ]
            send[g, r] = away[:classes].astype(BF16)
            keep[g, r] = here[:classes]


def sums(where, weights, plain, turned, dom, start, rows, classes):
    width = plain.shape[2]
    smem = pl.BlockSpec(memory_space=pltpu.SMEM)
    vmem = pl.BlockSpec(memory_space=pltpu.VMEM)
    return pl.pallas_call(
        functools.partial(sums_kernel, dom=dom, start=start, classes=classes),
        in_specs=[smem] + [vmem] * 3,
        out_shape=(
            jax.ShapeDtypeStruct((dom // 2, rows, classes, width), BF16),
            pinned((dom // 2, rows, classes, width), F32),
        ),
        compiler_params=pltpu.CompilerParams(vmem_limit_bytes=24 * MIB),
        cost_estimate=cost(rows * 0.8),
        name="sums",
    )(where, held(weights), held(plain), held(turned))


def fold_kernel(at, keep, got, *outs, fan):
    rest = keep.shape[0] // fan
    for m, out in enumerate(outs):
        for i in range(rest):
            b = i * fan + (at[0] ^ m)
            value = keep[b] + got[b].astype(F32)
            out[i] = value.astype(out.dtype)


def fold(at, keep, got, fan):
    rest = (keep.shape[0] // fan,) + keep.shape[1:]
    return pl.pallas_call(
        functools.partial(fold_kernel, fan=fan),
        in_specs=[pl.BlockSpec(memory_space=pltpu.SMEM)]
        + [pl.BlockSpec(memory_space=pltpu.VMEM)] * 2,
        out_shape=(pinned(rest, F32),) + (jax.ShapeDtypeStruct(rest, BF16),) * (fan - 1),
        compiler_params=pltpu.CompilerParams(vmem_limit_bytes=24 * MIB),
        cost_estimate=cost(1),
        name="fold",
    )(at.reshape(1), held(keep), got)


def finish_kernel(*args, counts):
    out = args[-1]
    block_rows = sum(rows for rows, _ in counts)
    classes = args[0].shape[2]
    at = 0
    row = 0
    for rows, pieces in counts:
        for r in range(rows):
            value = args[at][0, r]
            for other in args[at + 1 : at + pieces]:
                value = value + other[0, r].astype(F32)
            out[pl.ds(row, classes, stride=block_rows)] = value
            row += 1
        at += pieces


def finish(done):
    counts = tuple((pieces[0].shape[1], len(pieces)) for pieces in done)
    _, _, classes, width = done[0][0].shape
    block_rows = sum(rows for rows, _ in counts)
    flat = [held(p) if i == 0 else p for pieces in done for i, p in enumerate(pieces)]
    out = pl.pallas_call(
        functools.partial(finish_kernel, counts=counts),
        out_shape=jax.ShapeDtypeStruct((classes * block_rows, width), F32),
        compiler_params=pltpu.CompilerParams(vmem_limit_bytes=24 * MIB),
        cost_estimate=cost(1),
        name="finish",
    )(*flat)
    return out.reshape(classes, block_rows, width)


def y_pieces(particles):
    last = GROUP
    first = particles // 3 // GROUP * GROUP
    return (first, particles - first - last, last)


def row_pieces(rows):
    if rows < 4:
        return (rows,)
    part = -(-rows // 3)
    return (part, part, rows - 2 * part)


def local(
    images, defocus_bin, ctf_kernels, band_kernel, references, rot_index, class_mask, noise_var
):
    section_at = lax.axis_index("section")
    class_at = lax.axis_index("cls")
    dom_at = lax.axis_index("dom")
    dom = lax.axis_size("dom")
    particles, half, width = images.shape
    classes, rots = rot_index.shape
    padded = -(-classes // GROUP) * GROUP
    swap = [(0, 1), (1, 0)]
    over_cls = functools.partial(lax.ppermute, axis_name="cls", perm=swap)
    over_section = functools.partial(lax.ppermute, axis_name="section", perm=swap)

    sizes = y_pieces(particles)
    starts = [sum(sizes[:i]) for i in range(len(sizes))]
    remote = [over_cls(images[a : a + n]) for a, n in zip(starts, sizes)]
    other_bins = over_cls(defocus_bin)
    own_sib = over_section(images)

    where = jnp.stack([section_at, dom_at % 2]).astype(jnp.int32)
    left, right = build_filters(ctf_kernels, band_kernel)
    refs, norm = lay_refs(references, padded)

    def arranged(a):
        parts = a.reshape((2, particles) + a.shape[1:])
        return jnp.concatenate(
            [
                lax.dynamic_index_in_dim(parts, class_at, 0, False),
                lax.dynamic_index_in_dim(parts, 1 - class_at, 0, False),
            ]
        )

    mask = jnp.pad(arranged(class_mask).T, ((0, padded - classes), (0, 0)))
    noise = arranged(noise_var).reshape(1, 2 * particles)
    rot = jnp.pad(rot_index.T, ((0, 0), (0, padded - classes)))[:, :, None]

    total = 2 * particles
    buffers = filter_chunk(
        where, defocus_bin, images, own_sib, left, right, (), total, 0, 0
    )
    for a, piece in zip(starts, remote):
        buffers = filter_chunk(
            where, other_bins, piece, over_section(piece), left, right, buffers, total, a,
            particles + a,
        )
    plain, turned = buffers

    scaled, stats = score(plain, refs, norm, mask, noise)
    weights = make_weights(scaled, stats, over_cls(stats), rot)

    start = 0
    done = []
    for rows in row_pieces(half // dom):
        send, keep = sums(where, weights, plain, turned, dom, start, rows, classes)
        start += rows
        got = lax.ppermute(send, "dom", [(i, i ^ 1) for i in range(dom)])
        bit = 1
        while keep.shape[0] > 4:
            at = ((dom_at >> bit) & 1).astype(jnp.int32)
            keep, send = fold(at, keep, got, 2)
            got = lax.ppermute(send, "dom", [(i, i ^ (1 << bit)) for i in range(dom)])
            bit += 1
        fan = keep.shape[0]
        at = ((dom_at >> bit) & (fan - 1)).astype(jnp.int32)
        keep, *sends = fold(at, keep, got, fan)
        done.append(
            [keep]
            + [
                lax.ppermute(s, "dom", [(i, i ^ ((m + 1) << bit)) for i in range(dom)])
                for m, s in enumerate(sends)
            ]
        )
    return finish(done)


def solution(mesh):
    return jax.shard_map(
        local,
        mesh=mesh,
        in_specs=(
            P(("dom", "cls"), "section", None),
            P(("dom", "cls")),
            P(),
            P(),
            P("cls", None, None, None),
            P("cls", None),
            P("dom", "cls"),
            P("dom"),
        ),
        out_specs=P("cls", ("section", "dom"), None),
        check_vma=False,
    )
```

```python
import functools

import jax
import jax.numpy as jnp
from jax import lax
from jax.experimental import pallas as pl
from jax.experimental.pallas import tpu as pltpu
from jax.sharding import PartitionSpec as P

F32 = jnp.float32
BF16 = jnp.bfloat16
LOW = -1e30
GROUP = 16
PAD = 8
DEEP = 16
SUMS = 0.8
SCALE = 0.1
FOLD = 1
MIB = 1 << 20


def nt(a, b, precision=None):
    return lax.dot_general(
        a, b, (((1,), (1,)), ((), ())), preferred_element_type=F32, precision=precision
    )


def nn(a, b):
    return lax.dot_general(a, b, (((1,), (0,)), ((), ())), preferred_element_type=F32)


def cost(microseconds):
    return pl.CostEstimate(
        flops=int(microseconds * SCALE * 1e9), transcendentals=0, bytes_accessed=int(microseconds * SCALE * 3e6)
    )


def pinned(shape, dtype):
    return pltpu.VMEM(shape, dtype)


def held(x):
    return pltpu.with_memory_space_constraint(x, pltpu.VMEM)


def prepare_kernel(ctf, band, mask, noise, rot, left, right, mask_out, noise_out, rot_out, scr):
    bins, width = ctf.shape
    rots, classes = rot.shape
    padded = rot_out.shape[1]
    total = mask.shape[0]
    count = total // 2

    def negated(v):
        at = (width - lax.broadcasted_iota(jnp.int32, v.shape, 1)) % width
        return jnp.take_along_axis(v, at, axis=1)

    def rolled(row):
        return pltpu.roll(jnp.broadcast_to(row, (width, width)), 0, 1, stride=1, stride_axis=0)

    def with_delta(v):
        return v + jnp.where(lax.broadcasted_iota(jnp.int32, v.shape, 1) == 0, 1.0, 0.0)

    highest = lax.Precision.HIGHEST
    kernels = with_delta(ctf[...])
    bands = with_delta(jnp.broadcast_to(band[...], (8, width)))
    forward = nt(kernels, rolled(negated(bands)[:1]), highest)
    backward = nt(negated(kernels), rolled(bands[:1]), highest)
    for b in range(bins):
        left[b] = rolled(backward[b : b + 1]).astype(BF16)
        right[b] = rolled(forward[b : b + 1]).astype(BF16)

    scr[...] = jnp.zeros_like(scr)
    group = lax.axis_index("cls")
    for half in range(2):
        come = group if half == 0 else 1 - group
        start = pl.multiple_of(come * count, 8)
        scr[half * count : (half + 1) * count, :classes] = mask[pl.ds(start, count)].astype(F32)
    mask_out[...] = scr[...].T[:padded, :total]
    n = noise[...]
    other = jnp.concatenate([n[:, count:], n[:, :count]], axis=1)
    noise_out[...] = jnp.where(group == 0, n, other)
    square = scr.shape[1]
    scr[:square] = jnp.zeros((square, square), F32)
    scr[:rots, :classes] = rot[...].astype(F32)
    turned = scr[:square].T
    for j in range(rots):
        rot_out[j] = jnp.broadcast_to(turned[:padded, j : j + 1], (padded, square))


def prepare(ctf, band, mask, noise, rot, padded):
    bins, width = ctf.shape
    total = noise.shape[0]
    lanes = max(128, -(-padded // 128) * 128)
    tall = -(-max(total, lanes) // 128) * 128
    return pl.pallas_call(
        prepare_kernel,
        out_shape=(
            pinned((bins, width, width), BF16),
            pinned((bins, width, width), BF16),
            pinned((padded, total), F32),
            pinned((1, total), F32),
            pinned((rot.shape[0], padded, lanes), F32),
        ),
        scratch_shapes=[pltpu.VMEM((tall, lanes), F32)],
        compiler_params=pltpu.CompilerParams(vmem_limit_bytes=4 * MIB),
        cost_estimate=cost(3),
        name="prepare",
    )(ctf, band.reshape(1, width), mask, noise.reshape(1, total), rot)


def gate_kernel(piece, token, out):
    del piece, token, out


def gate(piece, token):
    anywhere = pl.BlockSpec(memory_space=pl.ANY)
    return pl.pallas_call(
        gate_kernel,
        in_specs=[anywhere, anywhere],
        out_specs=anywhere,
        out_shape=jax.ShapeDtypeStruct(piece.shape, piece.dtype),
        input_output_aliases={0: 0},
        compiler_params=pltpu.CompilerParams(vmem_limit_bytes=MIB),
        cost_estimate=cost(0.1),
        name="gate",
    )(piece, token)


def refs_kernel(refs, out, norm, scratch, *, padded):
    classes, _, rows, width = refs.shape
    pitch = rows + PAD
    j = pl.program_id(0)

    def block(start, count):
        for k in range(GROUP):
            if k < count:
                scratch[pl.ds(k * pitch, rows)] = refs[start + k, 0].astype(F32)
            else:
                scratch[pl.ds(k * pitch, rows)] = jnp.zeros((rows, width), F32)
        at = pl.multiple_of(j * padded + start, GROUP)

        def step(r, acc):
            v = scratch[pl.ds(r, GROUP, stride=pitch)]
            out[r, pl.ds(at, GROUP)] = v.astype(BF16)
            return acc + v * v

        acc = lax.fori_loop(0, rows, step, jnp.zeros((GROUP, width), F32), unroll=32)
        total = 0.5 * jnp.sum(acc, axis=1, keepdims=True)
        norm[pl.ds(at, GROUP)] = jnp.broadcast_to(total, (GROUP, width))

    full = classes // GROUP

    @pl.loop(0, full)
    def _(i):
        block(i * GROUP, GROUP)

    if classes % GROUP:
        block(full * GROUP, classes % GROUP)


def lay_refs(refs, padded):
    classes, rots, rows, width = refs.shape
    vmem = pl.BlockSpec(memory_space=pltpu.VMEM)
    return pl.pallas_call(
        functools.partial(refs_kernel, padded=padded),
        grid=(rots,),
        in_specs=[pl.BlockSpec((classes, 1, rows, width), lambda j: (0, j, 0, 0))],
        out_specs=(vmem, vmem),
        out_shape=(
            pinned((rows, rots * padded, width), BF16),
            pinned((rots * padded, width), F32),
        ),
        scratch_shapes=[pltpu.VMEM((GROUP * (rows + PAD), width), F32)],
        compiler_params=pltpu.CompilerParams(vmem_limit_bytes=12 * MIB),
        cost_estimate=cost(9),
        name="refs",
    )(pltpu.with_memory_space_constraint(refs, pltpu.HBM))


def filter_kernel(bins, mine, sib, left, right, *rest, skip, at):
    plain, turned, token, scr, scr_t = rest[-5:]
    token[...] = jnp.zeros_like(token)
    count, half, width = mine.shape
    top = lax.axis_index("section") == 0
    pitch = width + PAD

    @pl.loop(0, count // GROUP)
    def _(g):
        base = pl.multiple_of(g * GROUP, GROUP)
        for i in range(GROUP):
            b = bins[skip + base + i]
            a = mine[base + i]
            o = sib[base + i]
            x = jnp.concatenate([jnp.where(top, a, o), jnp.where(top, o, a)], axis=0)
            f = nn(left[b], nn(x, right[b]).astype(BF16))
            scr[pl.ds(i * pitch, width)] = f
            scr_t[pl.ds(i * pitch, width)] = f.T
        to = pl.multiple_of(at + base, GROUP)
        for r in range(width):
            plain[r, pl.ds(to, GROUP)] = scr[pl.ds(r, GROUP, stride=pitch)].astype(BF16)
            turned[r, pl.ds(to, GROUP)] = scr_t[pl.ds(r, GROUP, stride=pitch)].astype(BF16)


def filter_chunk(bins, mine, sib, left, right, buffers, total, skip, at):
    count, half, width = mine.shape
    smem = pl.BlockSpec(memory_space=pltpu.SMEM)
    vmem = pl.BlockSpec(memory_space=pltpu.VMEM)
    buffers = [held(b) for b in buffers]
    return pl.pallas_call(
        functools.partial(filter_kernel, skip=skip, at=at),
        in_specs=[smem] + [vmem] * (4 + len(buffers)),
        out_specs=(vmem, vmem, vmem),
        out_shape=(pinned((2 * half, total, width), BF16),) * 2
        + (jax.ShapeDtypeStruct((8, width), F32),),
        scratch_shapes=[pltpu.VMEM((GROUP * (2 * half + PAD), width), F32)] * 2,
        input_output_aliases={5 + i: i for i in range(len(buffers))},
        compiler_params=pltpu.CompilerParams(vmem_limit_bytes=8 * MIB),
        cost_estimate=cost(count * 0.1),
        name="filter",
    )(bins, mine, sib, held(left), held(right), *buffers)


def score_kernel(plain, refs, norm, mask, noise, scaled, stats):
    rows, height, width = refs.shape
    count = mask.shape[1]

    def step(i, acc):
        at = [DEEP * i + a for a in range(DEEP)]
        lhs = jnp.concatenate([refs[r] for r in at], axis=1)
        rhs = jnp.concatenate([plain[r] for r in at], axis=1)
        return acc + nt(lhs, rhs)

    inner = lax.fori_loop(0, rows // DEEP, step, jnp.zeros((height, count), F32))
    rots = height // mask.shape[0]
    allowed = jnp.concatenate([mask[...]] * rots, axis=0) > 0
    s = jnp.where(allowed, (inner - norm[:, :1]) / noise[...], LOW)
    scaled[...] = s
    peak = jnp.max(s, axis=0, keepdims=True)
    total = jnp.sum(jnp.exp(s - peak), axis=0, keepdims=True)
    stats[0:1] = peak
    stats[1:2] = total
    stats[2:] = jnp.zeros((stats.shape[0] - 2, count), F32)


def score(plain, refs, norm, mask, noise):
    count = mask.shape[1]
    height = refs.shape[1]
    return pl.pallas_call(
        score_kernel,
        out_shape=(
            pinned((height, count), F32),
            pinned((8, count), F32),
        ),
        compiler_params=pltpu.CompilerParams(vmem_limit_bytes=8 * MIB),
        cost_estimate=cost(5),
        name="score",
    )(held(plain), held(refs), held(norm), held(mask), held(noise))


def weights_kernel(scaled, mine, other, rot, out):
    rots, padded, _ = rot.shape
    count = scaled.shape[1]
    theirs = jnp.concatenate([other[:, count // 2 :], other[:, : count // 2]], axis=1)
    peak = jnp.maximum(mine[0:1], theirs[0:1])
    total = mine[1:2] * jnp.exp(mine[0:1] - peak) + theirs[1:2] * jnp.exp(theirs[0:1] - peak)
    w = (jnp.exp(scaled[...] - peak) / total).astype(BF16).astype(F32)
    quarters = []
    for q in range(4):
        acc = jnp.zeros((padded, count), F32)
        for j in range(rots):
            acc = acc + jnp.where(rot[j][:, :1] == q, w[j * padded : (j + 1) * padded], 0.0)
        quarters.append(acc)
    for row, pair in enumerate(((0, 3), (2, 1))):
        out[row] = jnp.concatenate([quarters[q] for q in pair], axis=1).astype(BF16)


def make_weights(scaled, mine, other, rot):
    _, padded, _ = rot.shape
    count = scaled.shape[1]
    return pl.pallas_call(
        weights_kernel,
        out_shape=pinned((2, padded, 2 * count), BF16),
        compiler_params=pltpu.CompilerParams(vmem_limit_bytes=8 * MIB),
        cost_estimate=cost(2),
        name="weights",
    )(held(scaled), held(mine), other, held(rot))


def sums_kernel(weights, plain, turned, send, keep, *, dom, start, classes):
    _, rows, _, width = send.shape
    height = plain.shape[0]
    block = height // 2 // dom
    first = lax.axis_index("section") * (height // 2) + start
    parity = lax.axis_index("dom") % 2
    straight = weights[0]
    mirrored = weights[1]
    flip = width - 1 - lax.broadcasted_iota(jnp.int32, (straight.shape[0], width), 1)

    @pl.loop(0, dom // 2)
    def _(g):
        for r in range(rows):
            both = [first + (2 * g + side) * block + r for side in (1 - parity, parity)]
            direct = jnp.concatenate(
                [jnp.concatenate([plain[i], turned[height - 1 - i]], axis=0) for i in both], axis=1
            )
            mirror = jnp.concatenate(
                [jnp.concatenate([plain[height - 1 - i], turned[i]], axis=0) for i in both], axis=1
            )
            direct = nn(straight, direct)
            mirror = nn(mirrored, mirror)
            away, here = [
                direct[:, at : at + width]
                + jnp.take_along_axis(mirror[:, at : at + width], flip, axis=1)
                for at in (0, width)
            ]
            send[g, r] = away[:classes].astype(BF16)
            keep[g, r] = here[:classes]


def sums(weights, plain, turned, dom, start, rows, classes):
    width = plain.shape[2]
    vmem = pl.BlockSpec(memory_space=pltpu.VMEM)
    return pl.pallas_call(
        functools.partial(sums_kernel, dom=dom, start=start, classes=classes),
        in_specs=[vmem] * 3,
        out_shape=(
            jax.ShapeDtypeStruct((dom // 2, rows, classes, width), BF16),
            pinned((dom // 2, rows, classes, width), F32),
        ),
        compiler_params=pltpu.CompilerParams(vmem_limit_bytes=8 * MIB),
        cost_estimate=cost(SUMS * rows),
        name="sums",
    )(held(weights), held(plain), held(turned))


def fold_kernel(keep, got, *outs, fan, bit):
    rest = keep.shape[0] // fan
    at = (lax.axis_index("dom") // (1 << bit)) % fan
    for m, out in enumerate(outs):
        for i in range(rest):
            b = i * fan + jnp.bitwise_xor(at, m)
            value = keep[b] + got[b].astype(F32)
            out[i] = value.astype(out.dtype)


def fold(keep, got, fan, bit):
    rest = (keep.shape[0] // fan,) + keep.shape[1:]
    return pl.pallas_call(
        functools.partial(fold_kernel, fan=fan, bit=bit),
        in_specs=[pl.BlockSpec(memory_space=pltpu.VMEM)] * 2,
        out_shape=(pinned(rest, F32),) + (jax.ShapeDtypeStruct(rest, BF16),) * (fan - 1),
        compiler_params=pltpu.CompilerParams(vmem_limit_bytes=8 * MIB),
        cost_estimate=cost(FOLD),
        name="fold",
    )(held(keep), got)


def finish_kernel(*args, counts):
    out = args[-1]
    block_rows = sum(rows for rows, _ in counts)
    classes = args[0].shape[2]
    at = 0
    row = 0
    for rows, pieces in counts:
        for r in range(rows):
            value = args[at][0, r]
            for other in args[at + 1 : at + pieces]:
                value = value + other[0, r].astype(F32)
            out[pl.ds(row, classes, stride=block_rows)] = value
            row += 1
        at += pieces


def finish(done):
    counts = tuple((pieces[0].shape[1], len(pieces)) for pieces in done)
    _, _, classes, width = done[0][0].shape
    block_rows = sum(rows for rows, _ in counts)
    flat = [held(p) if i == 0 else p for pieces in done for i, p in enumerate(pieces)]
    out = pl.pallas_call(
        functools.partial(finish_kernel, counts=counts),
        out_shape=jax.ShapeDtypeStruct((classes * block_rows, width), F32),
        compiler_params=pltpu.CompilerParams(vmem_limit_bytes=8 * MIB),
        cost_estimate=cost(1),
        name="finish",
    )(*flat)
    return out.reshape(classes, block_rows, width)


def y_pieces(particles):
    last = particles // 3 // GROUP * GROUP
    return (particles - last, last)


def row_pieces(rows):
    if rows < 4:
        return (rows,)
    part = -(-rows // 3)
    return (part, part, rows - 2 * part)


def local(
    images, defocus_bin, ctf_kernels, band_kernel, references, rot_index, class_mask, noise_var
):
    dom = lax.axis_size("dom")
    particles, half, width = images.shape
    classes = rot_index.shape[0]
    padded = -(-classes // GROUP) * GROUP
    swap = [(0, 1), (1, 0)]
    over_cls = functools.partial(lax.ppermute, axis_name="cls", perm=swap)
    over_section = functools.partial(lax.ppermute, axis_name="section", perm=swap)

    sizes = y_pieces(particles)
    starts = [sum(sizes[:i]) for i in range(len(sizes))]
    remote = [over_cls(images[a : a + n]) for a, n in zip(starts, sizes)]
    other_bins = over_cls(defocus_bin)
    own_sib = over_section(images)

    refs, norm = lay_refs(references, padded)
    left, right, mask, noise, rot = prepare(
        ctf_kernels, band_kernel, class_mask, noise_var, rot_index.T, padded
    )
    total = 2 * particles
    remote[0] = gate(remote[0], norm)
    sib = over_section(remote[0])
    *buffers, token = filter_chunk(
        defocus_bin, images, own_sib, left, right, (), total, 0, 0
    )
    for i, a in enumerate(starts):
        *buffers, token = filter_chunk(
            other_bins, remote[i], sib, left, right, buffers, total, a, particles + a
        )
        if i + 1 < len(starts):
            remote[i + 1] = gate(remote[i + 1], token)
            sib = over_section(remote[i + 1])
    plain, turned = buffers

    scaled, stats = score(plain, refs, norm, mask, noise)
    weights = make_weights(scaled, stats, over_cls(stats), rot)

    start = 0
    done = []
    for rows in row_pieces(half // dom):
        send, keep = sums(weights, plain, turned, dom, start, rows, classes)
        start += rows
        got = lax.ppermute(send, "dom", [(i, i ^ 1) for i in range(dom)])
        bit = 1
        while keep.shape[0] > 4:
            keep, send = fold(keep, got, 2, bit)
            got = lax.ppermute(send, "dom", [(i, i ^ (1 << bit)) for i in range(dom)])
            bit += 1
        keep, *sends = fold(keep, got, keep.shape[0], bit)
        done.append(
            [keep]
            + [
                lax.ppermute(s, "dom", [(i, i ^ ((m + 1) << bit)) for i in range(dom)])
                for m, s in enumerate(sends)
            ]
        )
    return finish(done)


def solution(mesh):
    return jax.shard_map(
        local,
        mesh=mesh,
        in_specs=(
            P(("dom", "cls"), "section", None),
            P(("dom", "cls")),
            P(),
            P(),
            P("cls", None, None, None),
            P("cls", None),
            P("dom", "cls"),
            P("dom"),
        ),
        out_specs=P("cls", ("section", "dom"), None),
        check_vma=False,
    )
```

```python
import functools

import jax
import jax.numpy as jnp
from jax import lax
from jax.experimental import pallas as pl
from jax.experimental.pallas import tpu as pltpu
from jax.sharding import PartitionSpec as P

F32 = jnp.float32
BF16 = jnp.bfloat16
LOW = -1e30
GROUP = 16
PAD = 8
DEEP = 16
SUMS = 0.8
SCALE = 0.1
FOLD = 1
MIB = 1 << 20


def nt(a, b, precision=None):
    return lax.dot_general(
        a, b, (((1,), (1,)), ((), ())), preferred_element_type=F32, precision=precision
    )


def nn(a, b):
    return lax.dot_general(a, b, (((1,), (0,)), ((), ())), preferred_element_type=F32)


def cost(microseconds):
    return pl.CostEstimate(
        flops=int(microseconds * SCALE * 1e9), transcendentals=0, bytes_accessed=int(microseconds * SCALE * 3e6)
    )


def pinned(shape, dtype):
    return pltpu.VMEM(shape, dtype)


def held(x):
    return pltpu.with_memory_space_constraint(x, pltpu.VMEM)


def prepare_kernel(ctf, band, mask, noise, rot, after, left, right, mask_out, noise_out, rot_out, scr):
    del after
    bins, width = ctf.shape
    rots, classes = rot.shape
    padded = rot_out.shape[1]
    total = mask.shape[0]
    count = total // 2

    def negated(v):
        at = (width - lax.broadcasted_iota(jnp.int32, v.shape, 1)) % width
        return jnp.take_along_axis(v, at, axis=1)

    def rolled(row):
        return pltpu.roll(jnp.broadcast_to(row, (width, width)), 0, 1, stride=1, stride_axis=0)

    def with_delta(v):
        return v + jnp.where(lax.broadcasted_iota(jnp.int32, v.shape, 1) == 0, 1.0, 0.0)

    highest = lax.Precision.HIGHEST
    kernels = with_delta(ctf[...])
    bands = with_delta(jnp.broadcast_to(band[...], (8, width)))
    forward = nt(kernels, rolled(negated(bands)[:1]), highest)
    backward = nt(negated(kernels), rolled(bands[:1]), highest)
    for b in range(bins):
        left[b] = rolled(backward[b : b + 1]).astype(BF16)
        right[b] = rolled(forward[b : b + 1]).astype(BF16)

    scr[...] = jnp.zeros_like(scr)
    group = lax.axis_index("cls")
    for half in range(2):
        come = group if half == 0 else 1 - group
        start = pl.multiple_of(come * count, 8)
        scr[half * count : (half + 1) * count, :classes] = mask[pl.ds(start, count)].astype(F32)
    mask_out[...] = scr[...].T[:padded, :total]
    n = noise[...]
    other = jnp.concatenate([n[:, count:], n[:, :count]], axis=1)
    noise_out[...] = jnp.where(group == 0, n, other)
    square = scr.shape[1]
    scr[:square] = jnp.zeros((square, square), F32)
    scr[:rots, :classes] = rot[...].astype(F32)
    turned = scr[:square].T
    for j in range(rots):
        rot_out[j] = jnp.broadcast_to(turned[:padded, j : j + 1], (padded, square))


def prepare(ctf, band, mask, noise, rot, after, padded):
    bins, width = ctf.shape
    total = noise.shape[0]
    lanes = max(128, -(-padded // 128) * 128)
    tall = -(-max(total, lanes) // 128) * 128
    return pl.pallas_call(
        prepare_kernel,
        out_shape=(
            pinned((bins, width, width), BF16),
            pinned((bins, width, width), BF16),
            pinned((padded, total), F32),
            pinned((1, total), F32),
            pinned((rot.shape[0], padded, lanes), F32),
        ),
        scratch_shapes=[pltpu.VMEM((tall, lanes), F32)],
        compiler_params=pltpu.CompilerParams(vmem_limit_bytes=4 * MIB),
        cost_estimate=cost(3),
        name="prepare",
    )(ctf, band.reshape(1, width), mask, noise.reshape(1, total), rot, held(after))


def gate_kernel(*refs):
    del refs


def gate(piece, *tokens):
    anywhere = pl.BlockSpec(memory_space=pl.ANY)
    return pl.pallas_call(
        gate_kernel,
        in_specs=[anywhere] * (1 + len(tokens)),
        out_specs=anywhere,
        out_shape=jax.ShapeDtypeStruct(piece.shape, piece.dtype),
        input_output_aliases={0: 0},
        compiler_params=pltpu.CompilerParams(vmem_limit_bytes=MIB),
        cost_estimate=cost(0.1),
        name="gate",
    )(piece, *tokens)


def refs_kernel(refs, out, norm, scratch, *, padded):
    classes, _, rows, width = refs.shape
    pitch = rows + PAD
    j = pl.program_id(0)

    def block(start, count):
        for k in range(GROUP):
            if k < count:
                scratch[pl.ds(k * pitch, rows)] = refs[start + k, 0].astype(F32)
            else:
                scratch[pl.ds(k * pitch, rows)] = jnp.zeros((rows, width), F32)
        at = pl.multiple_of(j * padded + start, GROUP)

        def step(r, acc):
            v = scratch[pl.ds(r, GROUP, stride=pitch)]
            out[r, pl.ds(at, GROUP)] = v.astype(BF16)
            return acc + v * v

        acc = lax.fori_loop(0, rows, step, jnp.zeros((GROUP, width), F32), unroll=32)
        total = 0.5 * jnp.sum(acc, axis=1, keepdims=True)
        norm[pl.ds(at, GROUP)] = jnp.broadcast_to(total, (GROUP, width))

    full = classes // GROUP

    @pl.loop(0, full)
    def _(i):
        block(i * GROUP, GROUP)

    if classes % GROUP:
        block(full * GROUP, classes % GROUP)


def lay_refs(refs, padded):
    classes, rots, rows, width = refs.shape
    vmem = pl.BlockSpec(memory_space=pltpu.VMEM)
    return pl.pallas_call(
        functools.partial(refs_kernel, padded=padded),
        grid=(rots,),
        in_specs=[pl.BlockSpec((classes, 1, rows, width), lambda j: (0, j, 0, 0))],
        out_specs=(vmem, vmem),
        out_shape=(
            pinned((rows, rots * padded, width), BF16),
            pinned((rots * padded, width), F32),
        ),
        scratch_shapes=[pltpu.VMEM((GROUP * (rows + PAD), width), F32)],
        compiler_params=pltpu.CompilerParams(vmem_limit_bytes=12 * MIB),
        cost_estimate=cost(9),
        name="refs",
    )(pltpu.with_memory_space_constraint(refs, pltpu.HBM))


def filter_kernel(bins, mine, left, right, *rest, parts, skip, at):
    sibs = rest[:parts]
    plain, turned, token, scr, scr_t = rest[-5:]
    token[...] = jnp.zeros_like(token)
    width = mine.shape[2]
    top = lax.axis_index("section") == 0
    pitch = width + PAD

    def part(sib, first):
        @pl.loop(0, sib.shape[0] // GROUP)
        def _(g):
            base = pl.multiple_of(g * GROUP, GROUP)
            for i in range(GROUP):
                b = bins[skip + first + base + i]
                a = mine[first + base + i]
                o = sib[base + i]
                x = jnp.concatenate([jnp.where(top, a, o), jnp.where(top, o, a)], axis=0)
                f = nn(left[b], nn(x, right[b]).astype(BF16))
                scr[pl.ds(i * pitch, width)] = f
                scr_t[pl.ds(i * pitch, width)] = f.T
            to = pl.multiple_of(at + first + base, GROUP)
            for r in range(width):
                plain[r, pl.ds(to, GROUP)] = scr[pl.ds(r, GROUP, stride=pitch)].astype(BF16)
                turned[r, pl.ds(to, GROUP)] = scr_t[pl.ds(r, GROUP, stride=pitch)].astype(BF16)

    first = 0
    for sib in sibs:
        part(sib, first)
        first += sib.shape[0]


def filter_chunk(bins, mine, sibs, left, right, buffers, total, skip, at):
    count, half, width = mine.shape
    smem = pl.BlockSpec(memory_space=pltpu.SMEM)
    vmem = pl.BlockSpec(memory_space=pltpu.VMEM)
    parts = len(sibs)
    return pl.pallas_call(
        functools.partial(filter_kernel, parts=parts, skip=skip, at=at),
        in_specs=[smem] + [vmem] * (3 + parts + len(buffers)),
        out_specs=(vmem, vmem, vmem),
        out_shape=(pinned((2 * half, total, width), BF16),) * 2
        + (jax.ShapeDtypeStruct((8, width), F32),),
        scratch_shapes=[pltpu.VMEM((GROUP * (2 * half + PAD), width), F32)] * 2,
        input_output_aliases={4 + parts + i: i for i in range(len(buffers))},
        compiler_params=pltpu.CompilerParams(vmem_limit_bytes=8 * MIB),
        cost_estimate=cost(count * 0.1),
        name="filter",
    )(bins, mine, held(left), held(right), *sibs, *[held(b) for b in buffers])


def score_kernel(plain, refs, norm, mask, noise, scaled, stats):
    rows, height, width = refs.shape
    count = mask.shape[1]

    def step(i, acc):
        at = [DEEP * i + a for a in range(DEEP)]
        lhs = jnp.concatenate([refs[r] for r in at], axis=1)
        rhs = jnp.concatenate([plain[r] for r in at], axis=1)
        return acc + nt(lhs, rhs)

    inner = lax.fori_loop(0, rows // DEEP, step, jnp.zeros((height, count), F32))
    rots = height // mask.shape[0]
    allowed = jnp.concatenate([mask[...]] * rots, axis=0) > 0
    s = jnp.where(allowed, (inner - norm[:, :1]) / noise[...], LOW)
    scaled[...] = s
    peak = jnp.max(s, axis=0, keepdims=True)
    total = jnp.sum(jnp.exp(s - peak), axis=0, keepdims=True)
    stats[0:1] = peak
    stats[1:2] = total
    stats[2:] = jnp.zeros((stats.shape[0] - 2, count), F32)


def score(plain, refs, norm, mask, noise):
    count = mask.shape[1]
    height = refs.shape[1]
    return pl.pallas_call(
        score_kernel,
        out_shape=(
            pinned((height, count), F32),
            pinned((8, count), F32),
        ),
        compiler_params=pltpu.CompilerParams(vmem_limit_bytes=8 * MIB),
        cost_estimate=cost(5),
        name="score",
    )(held(plain), held(refs), held(norm), held(mask), held(noise))


def weights_kernel(scaled, mine, other, rot, out):
    rots, padded, _ = rot.shape
    count = scaled.shape[1]
    theirs = jnp.concatenate([other[:, count // 2 :], other[:, : count // 2]], axis=1)
    peak = jnp.maximum(mine[0:1], theirs[0:1])
    total = mine[1:2] * jnp.exp(mine[0:1] - peak) + theirs[1:2] * jnp.exp(theirs[0:1] - peak)
    w = (jnp.exp(scaled[...] - peak) / total).astype(BF16).astype(F32)
    quarters = []
    for q in range(4):
        acc = jnp.zeros((padded, count), F32)
        for j in range(rots):
            acc = acc + jnp.where(rot[j][:, :1] == q, w[j * padded : (j + 1) * padded], 0.0)
        quarters.append(acc)
    for row, pair in enumerate(((0, 3), (2, 1))):
        out[row] = jnp.concatenate([quarters[q] for q in pair], axis=1).astype(BF16)


def make_weights(scaled, mine, other, rot):
    _, padded, _ = rot.shape
    count = scaled.shape[1]
    return pl.pallas_call(
        weights_kernel,
        out_shape=pinned((2, padded, 2 * count), BF16),
        compiler_params=pltpu.CompilerParams(vmem_limit_bytes=8 * MIB),
        cost_estimate=cost(2),
        name="weights",
    )(held(scaled), held(mine), other, held(rot))


def sums_kernel(weights, plain, turned, *rest, dom, start, classes):
    send, keep = rest[-2:]
    _, rows, _, width = send.shape
    height = plain.shape[0]
    block = height // 2 // dom
    first = lax.axis_index("section") * (height // 2) + start
    parity = lax.axis_index("dom") % 2
    straight = weights[0]
    mirrored = weights[1]
    flip = width - 1 - lax.broadcasted_iota(jnp.int32, (straight.shape[0], width), 1)

    @pl.loop(0, dom // 2)
    def _(g):
        for r in range(rows):
            both = [first + (2 * g + side) * block + r for side in (1 - parity, parity)]
            direct = jnp.concatenate(
                [jnp.concatenate([plain[i], turned[height - 1 - i]], axis=0) for i in both], axis=1
            )
            mirror = jnp.concatenate(
                [jnp.concatenate([plain[height - 1 - i], turned[i]], axis=0) for i in both], axis=1
            )
            direct = nn(straight, direct)
            mirror = nn(mirrored, mirror)
            away, here = [
                direct[:, at : at + width]
                + jnp.take_along_axis(mirror[:, at : at + width], flip, axis=1)
                for at in (0, width)
            ]
            send[g, r] = away[:classes].astype(BF16)
            keep[g, r] = here[:classes]


def sums(weights, plain, turned, after, dom, start, rows, classes):
    width = plain.shape[2]
    vmem = pl.BlockSpec(memory_space=pltpu.VMEM)
    return pl.pallas_call(
        functools.partial(sums_kernel, dom=dom, start=start, classes=classes),
        in_specs=[vmem] * 3 + [pl.BlockSpec(memory_space=pl.ANY)] * len(after),
        out_shape=(
            jax.ShapeDtypeStruct((dom // 2, rows, classes, width), BF16),
            pinned((dom // 2, rows, classes, width), F32),
        ),
        compiler_params=pltpu.CompilerParams(vmem_limit_bytes=8 * MIB),
        cost_estimate=cost(SUMS * rows),
        name="sums",
    )(held(weights), held(plain), held(turned), *after)


def fold_kernel(keep, got, *outs, fan, bit):
    outs = outs[-fan:]
    rest = keep.shape[0] // fan
    at = (lax.axis_index("dom") // (1 << bit)) % fan
    for m, out in enumerate(outs):
        for i in range(rest):
            b = i * fan + jnp.bitwise_xor(at, m)
            value = keep[b] + got[b].astype(F32)
            out[i] = value.astype(out.dtype)


def fold(keep, got, after, fan, bit):
    rest = (keep.shape[0] // fan,) + keep.shape[1:]
    return pl.pallas_call(
        functools.partial(fold_kernel, fan=fan, bit=bit),
        in_specs=[pl.BlockSpec(memory_space=pltpu.VMEM)] * 2
        + [pl.BlockSpec(memory_space=pl.ANY)] * len(after),
        out_shape=(pinned(rest, F32),) + (jax.ShapeDtypeStruct(rest, BF16),) * (fan - 1),
        compiler_params=pltpu.CompilerParams(vmem_limit_bytes=8 * MIB),
        cost_estimate=cost(FOLD),
        name="fold",
    )(held(keep), got, *after)


def finish_kernel(*args, counts):
    out = args[-1]
    block_rows = sum(rows for rows, _ in counts)
    classes = args[0].shape[2]
    at = 0
    row = 0
    for rows, pieces in counts:
        for r in range(rows):
            value = args[at][0, r]
            for other in args[at + 1 : at + pieces]:
                value = value + other[0, r].astype(F32)
            out[pl.ds(row, classes, stride=block_rows)] = value
            row += 1
        at += pieces


def finish(done):
    counts = tuple((pieces[0].shape[1], len(pieces)) for pieces in done)
    _, _, classes, width = done[0][0].shape
    block_rows = sum(rows for rows, _ in counts)
    flat = [held(p) if i == 0 else p for pieces in done for i, p in enumerate(pieces)]
    out = pl.pallas_call(
        functools.partial(finish_kernel, counts=counts),
        out_shape=jax.ShapeDtypeStruct((classes * block_rows, width), F32),
        compiler_params=pltpu.CompilerParams(vmem_limit_bytes=8 * MIB),
        cost_estimate=cost(1),
        name="finish",
    )(*flat)
    return out.reshape(classes, block_rows, width)


def y_pieces(particles):
    last = particles // 3 // GROUP * GROUP
    return (particles - last, last)


def row_pieces(rows):
    if rows < 4:
        return (rows,)
    part = -(-rows // 3)
    return (part, part, rows - 2 * part)


def local(
    images, defocus_bin, ctf_kernels, band_kernel, references, rot_index, class_mask, noise_var
):
    dom = lax.axis_size("dom")
    particles, half, width = images.shape
    classes = rot_index.shape[0]
    padded = -(-classes // GROUP) * GROUP
    swap = [(0, 1), (1, 0)]
    over_cls = functools.partial(lax.ppermute, axis_name="cls", perm=swap)
    over_section = functools.partial(lax.ppermute, axis_name="section", perm=swap)

    sizes = y_pieces(particles)
    starts = [sum(sizes[:i]) for i in range(len(sizes))]
    remote = [over_cls(images[a : a + n]) for a, n in zip(starts, sizes)]
    other_bins = over_cls(defocus_bin)
    own_sib = over_section(images)

    refs, norm = lay_refs(references, padded)
    left, right, mask, noise, rot = prepare(
        ctf_kernels, band_kernel, class_mask, noise_var, rot_index.T, norm, padded
    )
    total = 2 * particles
    *buffers, token = filter_chunk(
        defocus_bin, images, [own_sib], left, right, (), total, 0, 0
    )
    tokens = (token, other_bins)
    for i, a in enumerate(starts):
        piece = gate(remote[i], *tokens)
        step = GROUP if i + 1 < len(starts) else sizes[i]
        sibs = [over_section(piece[b : b + step]) for b in range(0, sizes[i], step)]
        *buffers, token = filter_chunk(
            other_bins, piece, sibs, left, right, buffers, total, a, particles + a
        )
        tokens = (token,)
    plain, turned = buffers

    scaled, stats = score(plain, refs, norm, mask, noise)
    weights = make_weights(scaled, stats, over_cls(stats), rot)

    start = 0
    done = []
    summed, folded = (), ()
    for rows in row_pieces(half // dom):
        send, keep = sums(weights, plain, turned, summed, dom, start, rows, classes)
        summed = (send,)
        start += rows
        got = lax.ppermute(send, "dom", [(i, i ^ 1) for i in range(dom)])
        bit = 1
        while keep.shape[0] > 4:
            keep, send = fold(keep, got, folded, 2, bit)
            got = lax.ppermute(send, "dom", [(i, i ^ (1 << bit)) for i in range(dom)])
            bit += 1
        keep, *sends = fold(keep, got, folded, keep.shape[0], bit)
        folded = tuple(
            lax.ppermute(s, "dom", [(i, i ^ ((m + 1) << bit)) for i in range(dom)])
            for m, s in enumerate(sends)
        )
        done.append((keep,) + folded)
    return finish(done)


def solution(mesh):
    return jax.shard_map(
        local,
        mesh=mesh,
        in_specs=(
            P(("dom", "cls"), "section", None),
            P(("dom", "cls")),
            P(),
            P(),
            P("cls", None, None, None),
            P("cls", None),
            P("dom", "cls"),
            P("dom"),
        ),
        out_specs=P("cls", ("section", "dom"), None),
        check_vma=False,
    )
```

```python
import functools

import jax
import jax.numpy as jnp
from jax import lax
from jax.experimental import pallas as pl
from jax.experimental.pallas import tpu as pltpu
from jax.sharding import PartitionSpec as P

F32 = jnp.float32
BF16 = jnp.bfloat16
LOW = -1e30
GROUP = 16
PAD = 8
DEEP = 16
SUMS = 0.8
SCALE = 0.1
FOLD = 1
MIB = 1 << 20


def nt(a, b, precision=None):
    return lax.dot_general(
        a, b, (((1,), (1,)), ((), ())), preferred_element_type=F32, precision=precision
    )


def nn(a, b):
    return lax.dot_general(a, b, (((1,), (0,)), ((), ())), preferred_element_type=F32)


def cost(microseconds):
    return pl.CostEstimate(
        flops=int(microseconds * SCALE * 1e9), transcendentals=0, bytes_accessed=int(microseconds * SCALE * 3e6)
    )


def pinned(shape, dtype):
    return pltpu.VMEM(shape, dtype)


def held(x):
    return pltpu.with_memory_space_constraint(x, pltpu.VMEM)


def prepare_kernel(ctf, band, mask, noise, rot, after, left, right, mask_out, noise_out, rot_out, scr):
    del after
    bins, width = ctf.shape
    rots, classes = rot.shape
    padded = rot_out.shape[1]
    total = mask.shape[0]
    count = total // 2

    def negated(v):
        at = (width - lax.broadcasted_iota(jnp.int32, v.shape, 1)) % width
        return jnp.take_along_axis(v, at, axis=1)

    def rolled(row):
        return pltpu.roll(jnp.broadcast_to(row, (width, width)), 0, 1, stride=1, stride_axis=0)

    def with_delta(v):
        return v + jnp.where(lax.broadcasted_iota(jnp.int32, v.shape, 1) == 0, 1.0, 0.0)

    highest = lax.Precision.HIGHEST
    kernels = with_delta(ctf[...])
    bands = with_delta(jnp.broadcast_to(band[...], (8, width)))
    forward = nt(kernels, rolled(negated(bands)[:1]), highest)
    backward = nt(negated(kernels), rolled(bands[:1]), highest)
    for b in range(bins):
        left[b] = rolled(backward[b : b + 1]).astype(BF16)
        right[b] = rolled(forward[b : b + 1]).astype(BF16)

    scr[...] = jnp.zeros_like(scr)
    group = lax.axis_index("cls")
    for half in range(2):
        come = group if half == 0 else 1 - group
        start = pl.multiple_of(come * count, 8)
        scr[half * count : (half + 1) * count, :classes] = mask[pl.ds(start, count)].astype(F32)
    mask_out[...] = scr[...].T[:padded, :total]
    n = noise[...]
    other = jnp.concatenate([n[:, count:], n[:, :count]], axis=1)
    noise_out[...] = jnp.where(group == 0, n, other)
    square = scr.shape[1]
    scr[:square] = jnp.zeros((square, square), F32)
    scr[:rots, :classes] = rot[...].astype(F32)
    turned = scr[:square].T
    for j in range(rots):
        rot_out[j] = jnp.broadcast_to(turned[:padded, j : j + 1], (padded, square))


def prepare(ctf, band, mask, noise, rot, after, padded):
    bins, width = ctf.shape
    total = noise.shape[0]
    lanes = max(128, -(-padded // 128) * 128)
    tall = -(-max(total, lanes) // 128) * 128
    return pl.pallas_call(
        prepare_kernel,
        out_shape=(
            pinned((bins, width, width), BF16),
            pinned((bins, width, width), BF16),
            pinned((padded, total), F32),
            pinned((1, total), F32),
            pinned((rot.shape[0], padded, lanes), F32),
        ),
        scratch_shapes=[pltpu.VMEM((tall, lanes), F32)],
        compiler_params=pltpu.CompilerParams(vmem_limit_bytes=4 * MIB),
        cost_estimate=cost(3),
        name="prepare",
    )(ctf, band.reshape(1, width), mask, noise.reshape(1, total), rot, held(after))


def gate_kernel(*refs):
    del refs


def gate(piece, *tokens):
    anywhere = pl.BlockSpec(memory_space=pl.ANY)
    return pl.pallas_call(
        gate_kernel,
        in_specs=[anywhere] * (1 + len(tokens)),
        out_specs=anywhere,
        out_shape=jax.ShapeDtypeStruct(piece.shape, piece.dtype),
        input_output_aliases={0: 0},
        compiler_params=pltpu.CompilerParams(vmem_limit_bytes=MIB),
        cost_estimate=cost(0.1),
        name="gate",
    )(piece, *tokens)


def refs_kernel(refs, out, norm, scratch, *, padded):
    classes, _, rows, width = refs.shape
    pitch = rows + PAD
    j = pl.program_id(0)

    def block(start, count):
        for k in range(GROUP):
            if k < count:
                scratch[pl.ds(k * pitch, rows)] = refs[start + k, 0].astype(F32)
            else:
                scratch[pl.ds(k * pitch, rows)] = jnp.zeros((rows, width), F32)
        at = pl.multiple_of(j * padded + start, GROUP)

        def step(r, acc):
            v = scratch[pl.ds(r, GROUP, stride=pitch)]
            out[r, pl.ds(at, GROUP)] = v.astype(BF16)
            return acc + v * v

        acc = lax.fori_loop(0, rows, step, jnp.zeros((GROUP, width), F32), unroll=32)
        total = 0.5 * jnp.sum(acc, axis=1, keepdims=True)
        norm[pl.ds(at, GROUP)] = jnp.broadcast_to(total, (GROUP, width))

    full = classes // GROUP

    @pl.loop(0, full)
    def _(i):
        block(i * GROUP, GROUP)

    if classes % GROUP:
        block(full * GROUP, classes % GROUP)


def lay_refs(refs, padded):
    classes, rots, rows, width = refs.shape
    vmem = pl.BlockSpec(memory_space=pltpu.VMEM)
    return pl.pallas_call(
        functools.partial(refs_kernel, padded=padded),
        grid=(rots,),
        in_specs=[pl.BlockSpec((classes, 1, rows, width), lambda j: (0, j, 0, 0))],
        out_specs=(vmem, vmem),
        out_shape=(
            pinned((rows, rots * padded, width), BF16),
            pinned((rots * padded, width), F32),
        ),
        scratch_shapes=[pltpu.VMEM((GROUP * (rows + PAD), width), F32)],
        compiler_params=pltpu.CompilerParams(vmem_limit_bytes=12 * MIB),
        cost_estimate=cost(9),
        name="refs",
    )(pltpu.with_memory_space_constraint(refs, pltpu.HBM))


def filter_kernel(bins, mine, left, right, *rest, parts, skip, at):
    sibs = rest[:parts]
    plain, turned, token, scr, scr_t = rest[-5:]
    token[...] = jnp.zeros_like(token)
    width = mine.shape[2]
    top = lax.axis_index("section") == 0
    pitch = width + PAD

    def part(sib, first):
        @pl.loop(0, sib.shape[0] // GROUP)
        def _(g):
            base = pl.multiple_of(g * GROUP, GROUP)
            for i in range(GROUP):
                b = bins[skip + first + base + i]
                a = mine[first + base + i]
                o = sib[base + i]
                x = jnp.concatenate([jnp.where(top, a, o), jnp.where(top, o, a)], axis=0)
                f = nn(left[b], nn(x, right[b]).astype(BF16))
                scr[pl.ds(i * pitch, width)] = f
                scr_t[pl.ds(i * pitch, width)] = f.T
            to = pl.multiple_of(at + first + base, GROUP)
            for r in range(width):
                plain[r, pl.ds(to, GROUP)] = scr[pl.ds(r, GROUP, stride=pitch)].astype(BF16)
                turned[r, pl.ds(to, GROUP)] = scr_t[pl.ds(r, GROUP, stride=pitch)].astype(BF16)

    first = 0
    for sib in sibs:
        part(sib, first)
        first += sib.shape[0]


def filter_chunk(bins, mine, sibs, left, right, buffers, total, skip, at):
    count, half, width = mine.shape
    smem = pl.BlockSpec(memory_space=pltpu.SMEM)
    vmem = pl.BlockSpec(memory_space=pltpu.VMEM)
    parts = len(sibs)
    return pl.pallas_call(
        functools.partial(filter_kernel, parts=parts, skip=skip, at=at),
        in_specs=[smem] + [vmem] * (3 + parts + len(buffers)),
        out_specs=(vmem, vmem, vmem),
        out_shape=(pinned((2 * half, total, width), BF16),) * 2
        + (jax.ShapeDtypeStruct((8, width), F32),),
        scratch_shapes=[pltpu.VMEM((GROUP * (2 * half + PAD), width), F32)] * 2,
        input_output_aliases={4 + parts + i: i for i in range(len(buffers))},
        compiler_params=pltpu.CompilerParams(vmem_limit_bytes=8 * MIB),
        cost_estimate=cost(count * 0.1),
        name="filter",
    )(bins, mine, held(left), held(right), *sibs, *[held(b) for b in buffers])


def score_kernel(plain, refs, norm, mask, noise, scaled, stats):
    rows, height, width = refs.shape
    count = mask.shape[1]

    def step(i, acc):
        at = [DEEP * i + a for a in range(DEEP)]
        lhs = jnp.concatenate([refs[r] for r in at], axis=1)
        rhs = jnp.concatenate([plain[r] for r in at], axis=1)
        return acc + nt(lhs, rhs)

    inner = lax.fori_loop(0, rows // DEEP, step, jnp.zeros((height, count), F32))
    rots = height // mask.shape[0]
    allowed = jnp.concatenate([mask[...]] * rots, axis=0) > 0
    s = jnp.where(allowed, (inner - norm[:, :1]) / noise[...], LOW)
    scaled[...] = s
    peak = jnp.max(s, axis=0, keepdims=True)
    total = jnp.sum(jnp.exp(s - peak), axis=0, keepdims=True)
    stats[0:1] = peak
    stats[1:2] = total
    stats[2:] = jnp.zeros((stats.shape[0] - 2, count), F32)


def score(plain, refs, norm, mask, noise):
    count = mask.shape[1]
    height = refs.shape[1]
    return pl.pallas_call(
        score_kernel,
        out_shape=(
            pinned((height, count), F32),
            pinned((8, count), F32),
        ),
        compiler_params=pltpu.CompilerParams(vmem_limit_bytes=8 * MIB),
        cost_estimate=cost(5),
        name="score",
    )(held(plain), held(refs), held(norm), held(mask), held(noise))


def weights_kernel(scaled, mine, other, rot, out):
    rots, padded, _ = rot.shape
    count = scaled.shape[1]
    theirs = jnp.concatenate([other[:, count // 2 :], other[:, : count // 2]], axis=1)
    peak = jnp.maximum(mine[0:1], theirs[0:1])
    total = mine[1:2] * jnp.exp(mine[0:1] - peak) + theirs[1:2] * jnp.exp(theirs[0:1] - peak)
    w = (jnp.exp(scaled[...] - peak) / total).astype(BF16).astype(F32)
    quarters = []
    for q in range(4):
        acc = jnp.zeros((padded, count), F32)
        for j in range(rots):
            acc = acc + jnp.where(rot[j][:, :1] == q, w[j * padded : (j + 1) * padded], 0.0)
        quarters.append(acc)
    for row, pair in enumerate(((0, 3), (2, 1))):
        out[row] = jnp.concatenate([quarters[q] for q in pair], axis=1).astype(BF16)


def make_weights(scaled, mine, other, rot):
    _, padded, _ = rot.shape
    count = scaled.shape[1]
    return pl.pallas_call(
        weights_kernel,
        out_shape=pinned((2, padded, 2 * count), BF16),
        compiler_params=pltpu.CompilerParams(vmem_limit_bytes=8 * MIB),
        cost_estimate=cost(2),
        name="weights",
    )(held(scaled), held(mine), other, held(rot))


def sums_kernel(weights, plain, turned, *rest, outer, dom, start, rows, classes):
    outs = rest[-(dom // 2 if outer else 2) :]
    width = outs[0].shape[2]
    height = plain.shape[0]
    block = height // 2 // dom
    first = lax.axis_index("section") * (height // 2) + start
    own = lax.axis_index("dom")
    parity = own % 2
    straight = weights[0]
    mirrored = weights[1]
    flip = width - 1 - lax.broadcasted_iota(jnp.int32, (straight.shape[0], width), 1)

    def pair(g, sides, r):
        both = [first + (2 * g + side) * block + r for side in sides]
        direct = jnp.concatenate(
            [jnp.concatenate([plain[i], turned[height - 1 - i]], axis=0) for i in both], axis=1
        )
        mirror = jnp.concatenate(
            [jnp.concatenate([plain[height - 1 - i], turned[i]], axis=0) for i in both], axis=1
        )
        direct = nn(straight, direct)
        mirror = nn(mirrored, mirror)
        return [
            (
                direct[:, at : at + width]
                + jnp.take_along_axis(mirror[:, at : at + width], flip, axis=1)
            )[:classes]
            for at in (0, width)
        ]

    if outer:
        for m, out in enumerate(outs):
            for r in range(rows):
                for side, value in enumerate(pair(jnp.bitwise_xor(own // 2, m), (0, 1), r)):
                    out[side, r * classes : (r + 1) * classes] = value.astype(out.dtype)
    else:
        keep, send = outs

        @pl.loop(0, dom // 2)
        def _(g):
            for r in range(rows):
                away, here = pair(g, (1 - parity, parity), r)
                at = slice(r * classes, (r + 1) * classes)
                send[g, at] = away.astype(BF16)
                keep[g, at] = here


def sums(weights, plain, turned, after, outer, dom, start, rows, classes):
    width = plain.shape[2]
    vmem = pl.BlockSpec(memory_space=pltpu.VMEM)
    count = 2 if outer else dom // 2
    shape = (count, rows * classes, width)
    return pl.pallas_call(
        functools.partial(
            sums_kernel, outer=outer, dom=dom, start=start, rows=rows, classes=classes
        ),
        in_specs=[vmem] * 3 + [pl.BlockSpec(memory_space=pl.ANY)] * len(after),
        out_shape=(pinned(shape, F32),)
        + (pltpu.HBM(shape, BF16),) * (dom // 2 - 1 if outer else 1),
        compiler_params=pltpu.CompilerParams(vmem_limit_bytes=8 * MIB),
        cost_estimate=cost(SUMS * rows),
        name="sums",
    )(held(weights), held(plain), held(turned), *after)


def gather_kernel(keep, *rest, came):
    got = rest[:came]
    here, away = rest[-2:]
    parity = lax.axis_index("dom") % 2
    for out, side in ((here, parity), (away, 1 - parity)):
        value = keep[side]
        for other in got:
            value = value + other[side].astype(F32)
        out[0] = value.astype(out.dtype)


def gather(keep, got):
    shape = (1,) + keep.shape[1:]
    return pl.pallas_call(
        functools.partial(gather_kernel, came=len(got)),
        out_shape=(pinned(shape, F32), jax.ShapeDtypeStruct(shape, BF16)),
        compiler_params=pltpu.CompilerParams(vmem_limit_bytes=8 * MIB),
        cost_estimate=cost(FOLD),
        name="gather",
    )(held(keep), *got)


def fold_kernel(keep, got, *outs, fan, bit):
    outs = outs[-fan:]
    rest = keep.shape[0] // fan
    at = (lax.axis_index("dom") // (1 << bit)) % fan
    for m, out in enumerate(outs):
        for i in range(rest):
            b = i * fan + jnp.bitwise_xor(at, m)
            value = keep[b] + got[b].astype(F32)
            out[i] = value.astype(out.dtype)


def fold(keep, got, after, fan, bit):
    rest = (keep.shape[0] // fan,) + keep.shape[1:]
    return pl.pallas_call(
        functools.partial(fold_kernel, fan=fan, bit=bit),
        in_specs=[pl.BlockSpec(memory_space=pltpu.VMEM)] * 2
        + [pl.BlockSpec(memory_space=pl.ANY)] * len(after),
        out_shape=(pinned(rest, F32),) + (jax.ShapeDtypeStruct(rest, BF16),) * (fan - 1),
        compiler_params=pltpu.CompilerParams(vmem_limit_bytes=8 * MIB),
        cost_estimate=cost(FOLD),
        name="fold",
    )(held(keep), got, *after)


def finish_kernel(*args, counts, classes):
    out = args[-1]
    block_rows = sum(rows for rows, _ in counts)
    at = 0
    row = 0
    for rows, pieces in counts:
        for r in range(rows):
            cut = slice(r * classes, (r + 1) * classes)
            value = args[at][0, cut]
            for other in args[at + 1 : at + pieces]:
                value = value + other[0, cut].astype(F32)
            out[pl.ds(row, classes, stride=block_rows)] = value
            row += 1
        at += pieces


def finish(done, classes):
    counts = tuple((pieces[0].shape[1] // classes, len(pieces)) for pieces in done)
    width = done[0][0].shape[2]
    block_rows = sum(rows for rows, _ in counts)
    flat = [held(p) if i == 0 else p for pieces in done for i, p in enumerate(pieces)]
    out = pl.pallas_call(
        functools.partial(finish_kernel, counts=counts, classes=classes),
        out_shape=jax.ShapeDtypeStruct((classes * block_rows, width), F32),
        compiler_params=pltpu.CompilerParams(vmem_limit_bytes=8 * MIB),
        cost_estimate=cost(1),
        name="finish",
    )(*flat)
    return out.reshape(classes, block_rows, width)


def y_pieces(particles):
    last = particles // 3 // GROUP * GROUP
    return (particles - last, last)


def row_pieces(rows, dom):
    if rows < 4 or dom > 8:
        return (rows, 0)
    outer = rows * 3 // 8
    return (rows - outer, outer)


def local(
    images, defocus_bin, ctf_kernels, band_kernel, references, rot_index, class_mask, noise_var
):
    dom = lax.axis_size("dom")
    particles, half, width = images.shape
    classes = rot_index.shape[0]
    padded = -(-classes // GROUP) * GROUP
    swap = [(0, 1), (1, 0)]
    over_cls = functools.partial(lax.ppermute, axis_name="cls", perm=swap)
    over_section = functools.partial(lax.ppermute, axis_name="section", perm=swap)

    sizes = y_pieces(particles)
    starts = [sum(sizes[:i]) for i in range(len(sizes))]
    remote = [over_cls(images[a : a + n]) for a, n in zip(starts, sizes)]
    other_bins = over_cls(defocus_bin)
    own_sib = over_section(images)

    refs, norm = lay_refs(references, padded)
    left, right, mask, noise, rot = prepare(
        ctf_kernels, band_kernel, class_mask, noise_var, rot_index.T, norm, padded
    )
    total = 2 * particles
    *buffers, token = filter_chunk(
        defocus_bin, images, [own_sib], left, right, (), total, 0, 0
    )
    tokens = (token, other_bins)
    for i, a in enumerate(starts):
        piece = gate(remote[i], *tokens)
        step = GROUP if i + 1 < len(starts) else sizes[i]
        sibs = [over_section(piece[b : b + step]) for b in range(0, sizes[i], step)]
        *buffers, token = filter_chunk(
            other_bins, piece, sibs, left, right, buffers, total, a, particles + a
        )
        tokens = (token,)
    plain, turned = buffers

    scaled, stats = score(plain, refs, norm, mask, noise)
    weights = make_weights(scaled, stats, over_cls(stats), rot)

    def along(x, mask):
        return lax.ppermute(x, "dom", [(i, i ^ mask) for i in range(dom)])

    inner, outer = row_pieces(half // dom, dom)
    keep, send = sums(weights, plain, turned, (), False, dom, 0, inner, classes)
    got = along(send, 1)
    if outer:
        keep_b, *sends_b = sums(
            weights, plain, turned, (send,), True, dom, inner, outer, classes
        )
        got_b = [along(s, (m + 1) << 1) for m, s in enumerate(sends_b)]
    bit = 1
    while keep.shape[0] > 4:
        keep, send = fold(keep, got, (), 2, bit)
        got = along(send, 1 << bit)
        bit += 1
    keep, *sends = fold(keep, got, (), keep.shape[0], bit)
    done = [[keep] + [along(s, (m + 1) << bit) for m, s in enumerate(sends)]]
    if outer:
        keep_b, send_b = gather(keep_b, got_b)
        done.append([keep_b, along(send_b, 1)])
    return finish(done, classes)


def solution(mesh):
    return jax.shard_map(
        local,
        mesh=mesh,
        in_specs=(
            P(("dom", "cls"), "section", None),
            P(("dom", "cls")),
            P(),
            P(),
            P("cls", None, None, None),
            P("cls", None),
            P("dom", "cls"),
            P("dom"),
        ),
        out_specs=P("cls", ("section", "dom"), None),
        check_vma=False,
    )
```

```python
import functools

import jax
import jax.numpy as jnp
from jax import lax
from jax.experimental import pallas as pl
from jax.experimental.pallas import tpu as pltpu
from jax.sharding import PartitionSpec as P

F32 = jnp.float32
BF16 = jnp.bfloat16
LOW = -1e30
GROUP = 16
PAD = 8
DEEP = 64
SUMS = 0.8
SCALE = 0.1
FOLD = 1
MIB = 1 << 20


def nt(a, b, precision=None):
    return lax.dot_general(
        a, b, (((1,), (1,)), ((), ())), preferred_element_type=F32, precision=precision
    )


def nn(a, b):
    return lax.dot_general(a, b, (((1,), (0,)), ((), ())), preferred_element_type=F32)


def cost(microseconds):
    return pl.CostEstimate(
        flops=int(microseconds * SCALE * 1e9), transcendentals=0, bytes_accessed=int(microseconds * SCALE * 3e6)
    )


def pinned(shape, dtype):
    return pltpu.VMEM(shape, dtype)


def held(x):
    return pltpu.with_memory_space_constraint(x, pltpu.VMEM)


def prepare_kernel(ctf, band, mask, noise, rot, after, left, right, mask_out, noise_out, rot_out, scr):
    del after
    bins, width = ctf.shape
    rots, classes = rot.shape
    padded = rot_out.shape[1]
    total = mask.shape[0]
    count = total // 2

    def negated(v):
        at = (width - lax.broadcasted_iota(jnp.int32, v.shape, 1)) % width
        return jnp.take_along_axis(v, at, axis=1)

    def rolled(row):
        return pltpu.roll(jnp.broadcast_to(row, (width, width)), 0, 1, stride=1, stride_axis=0)

    def with_delta(v):
        return v + jnp.where(lax.broadcasted_iota(jnp.int32, v.shape, 1) == 0, 1.0, 0.0)

    highest = lax.Precision.HIGHEST
    kernels = with_delta(ctf[...])
    bands = with_delta(jnp.broadcast_to(band[...], (8, width)))
    forward = nt(kernels, rolled(negated(bands)[:1]), highest)
    backward = nt(negated(kernels), rolled(bands[:1]), highest)
    for b in range(bins):
        left[b] = rolled(backward[b : b + 1]).astype(BF16)
        right[b] = rolled(forward[b : b + 1]).astype(BF16)

    scr[...] = jnp.zeros_like(scr)
    group = lax.axis_index("cls")
    for half in range(2):
        come = group if half == 0 else 1 - group
        start = pl.multiple_of(come * count, 8)
        scr[half * count : (half + 1) * count, :classes] = mask[pl.ds(start, count)].astype(F32)
    mask_out[...] = scr[...].T[:padded, :total]
    n = noise[...]
    other = jnp.concatenate([n[:, count:], n[:, :count]], axis=1)
    noise_out[...] = jnp.where(group == 0, n, other)
    square = scr.shape[1]
    scr[:square] = jnp.zeros((square, square), F32)
    scr[:rots, :classes] = rot[...].astype(F32)
    turned = scr[:square].T
    for j in range(rots):
        rot_out[j] = jnp.broadcast_to(turned[:padded, j : j + 1], (padded, square))


def prepare(ctf, band, mask, noise, rot, after, padded):
    bins, width = ctf.shape
    total = noise.shape[0]
    lanes = max(128, -(-padded // 128) * 128)
    tall = -(-max(total, lanes) // 128) * 128
    return pl.pallas_call(
        prepare_kernel,
        out_shape=(
            pinned((bins, width, width), BF16),
            pinned((bins, width, width), BF16),
            pinned((padded, total), F32),
            pinned((1, total), F32),
            pinned((rot.shape[0], padded, lanes), F32),
        ),
        scratch_shapes=[pltpu.VMEM((tall, lanes), F32)],
        compiler_params=pltpu.CompilerParams(vmem_limit_bytes=4 * MIB),
        cost_estimate=cost(3),
        name="prepare",
    )(ctf, band.reshape(1, width), mask, noise.reshape(1, total), rot, held(after))


def gate_kernel(*refs):
    del refs


def gate(piece, *tokens):
    anywhere = pl.BlockSpec(memory_space=pl.ANY)
    return pl.pallas_call(
        gate_kernel,
        in_specs=[anywhere] * (1 + len(tokens)),
        out_specs=anywhere,
        out_shape=jax.ShapeDtypeStruct(piece.shape, piece.dtype),
        input_output_aliases={0: 0},
        compiler_params=pltpu.CompilerParams(vmem_limit_bytes=MIB),
        cost_estimate=cost(0.1),
        name="gate",
    )(piece, *tokens)


def refs_kernel(refs, out, norm, scratch, *, padded):
    classes, _, rows, width = refs.shape
    pitch = rows + PAD
    j = pl.program_id(0)

    def block(start, count):
        for k in range(GROUP):
            if k < count:
                scratch[pl.ds(k * pitch, rows)] = refs[start + k, 0].astype(F32)
            else:
                scratch[pl.ds(k * pitch, rows)] = jnp.zeros((rows, width), F32)
        at = pl.multiple_of(j * padded + start, GROUP)

        def step(r, acc):
            v = scratch[pl.ds(r, GROUP, stride=pitch)]
            out[r, pl.ds(at, GROUP)] = v.astype(BF16)
            return acc + v * v

        acc = lax.fori_loop(0, rows, step, jnp.zeros((GROUP, width), F32), unroll=32)
        total = 0.5 * jnp.sum(acc, axis=1, keepdims=True)
        norm[pl.ds(at, GROUP)] = jnp.broadcast_to(total, (GROUP, width))

    full = classes // GROUP

    @pl.loop(0, full)
    def _(i):
        block(i * GROUP, GROUP)

    if classes % GROUP:
        block(full * GROUP, classes % GROUP)


def lay_refs(refs, padded):
    classes, rots, rows, width = refs.shape
    vmem = pl.BlockSpec(memory_space=pltpu.VMEM)
    return pl.pallas_call(
        functools.partial(refs_kernel, padded=padded),
        grid=(rots,),
        in_specs=[pl.BlockSpec((classes, 1, rows, width), lambda j: (0, j, 0, 0))],
        out_specs=(vmem, vmem),
        out_shape=(
            pinned((rows, rots * padded, width), BF16),
            pinned((rots * padded, width), F32),
        ),
        scratch_shapes=[pltpu.VMEM((GROUP * (rows + PAD), width), F32)],
        compiler_params=pltpu.CompilerParams(vmem_limit_bytes=12 * MIB),
        cost_estimate=cost(9),
        name="refs",
    )(pltpu.with_memory_space_constraint(refs, pltpu.HBM))


def filter_kernel(bins, mine, left, right, *rest, parts, skip, at):
    sibs = rest[:parts]
    plain, turned, token = rest[-7:-4]
    scratch = rest[-4:]
    token[...] = jnp.zeros_like(token)
    width = mine.shape[2]
    top = lax.axis_index("section") == 0
    pitch = width + PAD

    def group(sib, base, first, turn):
        scr, scr_t = scratch[2 * turn : 2 * turn + 2]
        for i in range(GROUP):
            b = bins[skip + first + base + i]
            a = mine[first + base + i]
            o = sib[base + i]
            x = jnp.concatenate([jnp.where(top, a, o), jnp.where(top, o, a)], axis=0)
            f = nn(left[b], nn(x, right[b]).astype(BF16))
            scr[pl.ds(i * pitch, width)] = f
            scr_t[pl.ds(i * pitch, width)] = f.T
        to = pl.multiple_of(at + first + base, GROUP)
        for r in range(width):
            plain[r, pl.ds(to, GROUP)] = scr[pl.ds(r, GROUP, stride=pitch)].astype(BF16)
            turned[r, pl.ds(to, GROUP)] = scr_t[pl.ds(r, GROUP, stride=pitch)].astype(BF16)

    first = 0
    for n, sib in enumerate(sibs):
        count = sib.shape[0]
        if count <= 2 * GROUP:
            for g in range(count // GROUP):
                group(sib, g * GROUP, first, (n + g) % 2)
        else:

            @pl.loop(0, count // GROUP)
            def _(g):
                group(sib, pl.multiple_of(g * GROUP, GROUP), first, 0)

        first += count


def filter_chunk(bins, mine, sibs, left, right, buffers, total, skip, at):
    count, half, width = mine.shape
    smem = pl.BlockSpec(memory_space=pltpu.SMEM)
    vmem = pl.BlockSpec(memory_space=pltpu.VMEM)
    parts = len(sibs)
    return pl.pallas_call(
        functools.partial(filter_kernel, parts=parts, skip=skip, at=at),
        in_specs=[smem] + [vmem] * (3 + parts + len(buffers)),
        out_specs=(vmem, vmem, vmem),
        out_shape=(pinned((2 * half, total, width), BF16),) * 2
        + (jax.ShapeDtypeStruct((8, width), F32),),
        scratch_shapes=[pltpu.VMEM((GROUP * (2 * half + PAD), width), F32)] * 4,
        input_output_aliases={4 + parts + i: i for i in range(len(buffers))},
        compiler_params=pltpu.CompilerParams(vmem_limit_bytes=8 * MIB),
        cost_estimate=cost(count * 0.1),
        name="filter",
    )(bins, mine, held(left), held(right), *sibs, *[held(b) for b in buffers])


def score_kernel(plain, refs, norm, mask, noise, scaled, stats):
    rows, height, width = refs.shape
    count = mask.shape[1]

    def step(i, acc):
        at = [DEEP * i + a for a in range(DEEP)]
        lhs = jnp.concatenate([refs[r] for r in at], axis=1)
        rhs = jnp.concatenate([plain[r] for r in at], axis=1)
        return acc + nt(lhs, rhs)

    inner = lax.fori_loop(0, rows // DEEP, step, jnp.zeros((height, count), F32))
    rots = height // mask.shape[0]
    allowed = jnp.concatenate([mask[...]] * rots, axis=0) > 0
    s = jnp.where(allowed, (inner - norm[:, :1]) / noise[...], LOW)
    scaled[...] = s
    peak = jnp.max(s, axis=0, keepdims=True)
    total = jnp.sum(jnp.exp(s - peak), axis=0, keepdims=True)
    stats[0:1] = peak
    stats[1:2] = total
    stats[2:] = jnp.zeros((stats.shape[0] - 2, count), F32)


def score(plain, refs, norm, mask, noise):
    count = mask.shape[1]
    height = refs.shape[1]
    return pl.pallas_call(
        score_kernel,
        out_shape=(
            pinned((height, count), F32),
            pinned((8, count), F32),
        ),
        compiler_params=pltpu.CompilerParams(vmem_limit_bytes=8 * MIB),
        cost_estimate=cost(5),
        name="score",
    )(held(plain), held(refs), held(norm), held(mask), held(noise))


def weights_kernel(scaled, mine, other, rot, out):
    rots, padded, _ = rot.shape
    count = scaled.shape[1]
    theirs = jnp.concatenate([other[:, count // 2 :], other[:, : count // 2]], axis=1)
    peak = jnp.maximum(mine[0:1], theirs[0:1])
    total = mine[1:2] * jnp.exp(mine[0:1] - peak) + theirs[1:2] * jnp.exp(theirs[0:1] - peak)
    w = (jnp.exp(scaled[...] - peak) / total).astype(BF16).astype(F32)
    quarters = []
    for q in range(4):
        acc = jnp.zeros((padded, count), F32)
        for j in range(rots):
            acc = acc + jnp.where(rot[j][:, :1] == q, w[j * padded : (j + 1) * padded], 0.0)
        quarters.append(acc)
    for row, pair in enumerate(((0, 3), (2, 1))):
        out[row] = jnp.concatenate([quarters[q] for q in pair], axis=1).astype(BF16)


def make_weights(scaled, mine, other, rot):
    _, padded, _ = rot.shape
    count = scaled.shape[1]
    return pl.pallas_call(
        weights_kernel,
        out_shape=pinned((2, padded, 2 * count), BF16),
        compiler_params=pltpu.CompilerParams(vmem_limit_bytes=8 * MIB),
        cost_estimate=cost(2),
        name="weights",
    )(held(scaled), held(mine), other, held(rot))


def sums_kernel(weights, plain, turned, *rest, outer, dom, start, rows, classes):
    outs = rest[-(dom // 2 if outer else 2) :]
    width = outs[0].shape[2]
    height = plain.shape[0]
    block = height // 2 // dom
    first = lax.axis_index("section") * (height // 2) + start
    own = lax.axis_index("dom")
    parity = own % 2
    straight = weights[0]
    mirrored = weights[1]
    flip = width - 1 - lax.broadcasted_iota(jnp.int32, (straight.shape[0], width), 1)

    def pair(g, sides, r):
        both = [first + (2 * g + side) * block + r for side in sides]
        direct = jnp.concatenate(
            [jnp.concatenate([plain[i], turned[height - 1 - i]], axis=0) for i in both], axis=1
        )
        mirror = jnp.concatenate(
            [jnp.concatenate([plain[height - 1 - i], turned[i]], axis=0) for i in both], axis=1
        )
        direct = nn(straight, direct)
        mirror = nn(mirrored, mirror)
        return [
            (
                direct[:, at : at + width]
                + jnp.take_along_axis(mirror[:, at : at + width], flip, axis=1)
            )[:classes]
            for at in (0, width)
        ]

    if outer:
        for m, out in enumerate(outs):
            for r in range(rows):
                for side, value in enumerate(pair(jnp.bitwise_xor(own // 2, m), (0, 1), r)):
                    out[side, r * classes : (r + 1) * classes] = value.astype(out.dtype)
    else:
        keep, send = outs

        @pl.loop(0, dom // 2)
        def _(g):
            for r in range(rows):
                away, here = pair(g, (1 - parity, parity), r)
                at = slice(r * classes, (r + 1) * classes)
                send[g, at] = away.astype(BF16)
                keep[g, at] = here


def sums(weights, plain, turned, after, outer, dom, start, rows, classes):
    width = plain.shape[2]
    vmem = pl.BlockSpec(memory_space=pltpu.VMEM)
    count = 2 if outer else dom // 2
    shape = (count, rows * classes, width)
    return pl.pallas_call(
        functools.partial(
            sums_kernel, outer=outer, dom=dom, start=start, rows=rows, classes=classes
        ),
        in_specs=[vmem] * 3 + [pl.BlockSpec(memory_space=pl.ANY)] * len(after),
        out_shape=(pinned(shape, F32),)
        + (jax.ShapeDtypeStruct(shape, BF16),) * (dom // 2 - 1 if outer else 1),
        compiler_params=pltpu.CompilerParams(vmem_limit_bytes=8 * MIB),
        cost_estimate=cost(SUMS * rows),
        name="sums",
    )(held(weights), held(plain), held(turned), *after)


def gather_kernel(keep, *rest, came):
    got = rest[:came]
    here, away = rest[-2:]
    parity = lax.axis_index("dom") % 2
    for out, side in ((here, parity), (away, 1 - parity)):
        value = keep[side]
        for other in got:
            value = value + other[side].astype(F32)
        out[0] = value.astype(out.dtype)


def gather(keep, got):
    shape = (1,) + keep.shape[1:]
    return pl.pallas_call(
        functools.partial(gather_kernel, came=len(got)),
        out_shape=(pinned(shape, F32), jax.ShapeDtypeStruct(shape, BF16)),
        compiler_params=pltpu.CompilerParams(vmem_limit_bytes=8 * MIB),
        cost_estimate=cost(FOLD),
        name="gather",
    )(held(keep), *got)


def fold_kernel(keep, got, *outs, fan, bit):
    outs = outs[-fan:]
    rest = keep.shape[0] // fan
    at = (lax.axis_index("dom") // (1 << bit)) % fan
    for m, out in enumerate(outs):
        for i in range(rest):
            b = i * fan + jnp.bitwise_xor(at, m)
            value = keep[b] + got[b].astype(F32)
            out[i] = value.astype(out.dtype)


def fold(keep, got, after, fan, bit):
    rest = (keep.shape[0] // fan,) + keep.shape[1:]
    return pl.pallas_call(
        functools.partial(fold_kernel, fan=fan, bit=bit),
        in_specs=[pl.BlockSpec(memory_space=pltpu.VMEM)] * 2
        + [pl.BlockSpec(memory_space=pl.ANY)] * len(after),
        out_shape=(pinned(rest, F32),) + (jax.ShapeDtypeStruct(rest, BF16),) * (fan - 1),
        compiler_params=pltpu.CompilerParams(vmem_limit_bytes=8 * MIB),
        cost_estimate=cost(FOLD),
        name="fold",
    )(held(keep), got, *after)


def finish_kernel(*args, counts, classes):
    out = args[-1]
    block_rows = sum(rows for rows, _ in counts)
    at = 0
    row = 0
    for rows, pieces in counts:
        for r in range(rows):
            cut = slice(r * classes, (r + 1) * classes)
            value = args[at][0, cut]
            for other in args[at + 1 : at + pieces]:
                value = value + other[0, cut].astype(F32)
            out[pl.ds(row, classes, stride=block_rows)] = value
            row += 1
        at += pieces


def finish(done, classes):
    counts = tuple((pieces[0].shape[1] // classes, len(pieces)) for pieces in done)
    width = done[0][0].shape[2]
    block_rows = sum(rows for rows, _ in counts)
    flat = [held(p) if i == 0 else p for pieces in done for i, p in enumerate(pieces)]
    out = pl.pallas_call(
        functools.partial(finish_kernel, counts=counts, classes=classes),
        out_shape=jax.ShapeDtypeStruct((classes * block_rows, width), F32),
        compiler_params=pltpu.CompilerParams(vmem_limit_bytes=8 * MIB),
        cost_estimate=cost(1),
        name="finish",
    )(*flat)
    return out.reshape(classes, block_rows, width)


def y_pieces(particles):
    last = particles // 3 // GROUP * GROUP
    return (particles - last, last)


def row_pieces(rows, dom):
    if rows < 4 or dom > 8:
        return (rows, 0)
    outer = rows * 3 // 8
    return (rows - outer, outer)


def local(
    images, defocus_bin, ctf_kernels, band_kernel, references, rot_index, class_mask, noise_var
):
    dom = lax.axis_size("dom")
    particles, half, width = images.shape
    classes = rot_index.shape[0]
    padded = -(-classes // GROUP) * GROUP
    swap = [(0, 1), (1, 0)]
    over_cls = functools.partial(lax.ppermute, axis_name="cls", perm=swap)
    over_section = functools.partial(lax.ppermute, axis_name="section", perm=swap)

    sizes = y_pieces(particles)
    starts = [sum(sizes[:i]) for i in range(len(sizes))]
    remote = [over_cls(images[a : a + n]) for a, n in zip(starts, sizes)]
    other_bins = over_cls(defocus_bin)
    own_sib = over_section(images)

    refs, norm = lay_refs(references, padded)
    left, right, mask, noise, rot = prepare(
        ctf_kernels, band_kernel, class_mask, noise_var, rot_index.T, norm, padded
    )
    total = 2 * particles
    *buffers, token = filter_chunk(
        defocus_bin, images, [own_sib], left, right, (), total, 0, 0
    )
    tokens = (token, other_bins)
    for i, a in enumerate(starts):
        piece = gate(remote[i], *tokens)
        step = GROUP if i + 1 < len(starts) else sizes[i]
        sibs = [over_section(piece[b : b + step]) for b in range(0, sizes[i], step)]
        *buffers, token = filter_chunk(
            other_bins, piece, sibs, left, right, buffers, total, a, particles + a
        )
        tokens = (token,)
    plain, turned = buffers

    scaled, stats = score(plain, refs, norm, mask, noise)
    weights = make_weights(scaled, stats, over_cls(stats), rot)

    def along(x, mask):
        return lax.ppermute(x, "dom", [(i, i ^ mask) for i in range(dom)])

    def spread(sends, bit):
        far_first = sorted(range(len(sends)), key=lambda m: m == 0)
        return [along(sends[m], (m + 1) << bit) for m in far_first]

    inner, outer = row_pieces(half // dom, dom)
    keep, send = sums(weights, plain, turned, (), False, dom, 0, inner, classes)
    got = along(send, 1)
    if outer:
        keep_b, *sends_b = sums(
            weights, plain, turned, (send,), True, dom, inner, outer, classes
        )
        got_b = spread(sends_b, 1)
    bit = 1
    while keep.shape[0] > 4:
        keep, send = fold(keep, got, (), 2, bit)
        got = along(send, 1 << bit)
        bit += 1
    keep, *sends = fold(keep, got, (), keep.shape[0], bit)
    done = [[keep] + spread(sends, bit)]
    if outer:
        keep_b, send_b = gather(keep_b, got_b)
        done.append([keep_b, along(send_b, 1)])
    return finish(done, classes)


def solution(mesh):
    return jax.shard_map(
        local,
        mesh=mesh,
        in_specs=(
            P(("dom", "cls"), "section", None),
            P(("dom", "cls")),
            P(),
            P(),
            P("cls", None, None, None),
            P("cls", None),
            P("dom", "cls"),
            P("dom"),
        ),
        out_specs=P("cls", ("section", "dom"), None),
        check_vma=False,
    )
```

```python
import functools

import jax
import jax.numpy as jnp
from jax import lax
from jax.experimental import pallas as pl
from jax.experimental.pallas import tpu as pltpu
from jax.sharding import PartitionSpec as P

F32 = jnp.float32
BF16 = jnp.bfloat16
LOW = -1e30
GROUP = 16
PAD = 8
DEEP = 128
SUMS = 0.8
SCALE = 0.1
FOLD = 1
MIB = 1 << 20


def nt(a, b, precision=None):
    return lax.dot_general(
        a, b, (((1,), (1,)), ((), ())), preferred_element_type=F32, precision=precision
    )


def nn(a, b):
    return lax.dot_general(a, b, (((1,), (0,)), ((), ())), preferred_element_type=F32)


def cost(microseconds):
    return pl.CostEstimate(
        flops=int(microseconds * SCALE * 1e9), transcendentals=0, bytes_accessed=int(microseconds * SCALE * 3e6)
    )


def pinned(shape, dtype):
    return pltpu.VMEM(shape, dtype)


def held(x):
    return pltpu.with_memory_space_constraint(x, pltpu.VMEM)


def prepare_kernel(ctf, band, mask, noise, rot, after, left, right, mask_out, noise_out, rot_out, scr):
    del after
    bins, width = ctf.shape
    rots, classes = rot.shape
    padded = rot_out.shape[1]
    total = mask.shape[0]
    count = total // 2

    def negated(v):
        at = (width - lax.broadcasted_iota(jnp.int32, v.shape, 1)) % width
        return jnp.take_along_axis(v, at, axis=1)

    def rolled(row):
        return pltpu.roll(jnp.broadcast_to(row, (width, width)), 0, 1, stride=1, stride_axis=0)

    def with_delta(v):
        return v + jnp.where(lax.broadcasted_iota(jnp.int32, v.shape, 1) == 0, 1.0, 0.0)

    highest = lax.Precision.HIGHEST
    kernels = with_delta(ctf[...])
    bands = with_delta(jnp.broadcast_to(band[...], (8, width)))
    forward = nt(kernels, rolled(negated(bands)[:1]), highest)
    backward = nt(negated(kernels), rolled(bands[:1]), highest)
    for b in range(bins):
        left[b] = rolled(backward[b : b + 1]).astype(BF16)
        right[b] = rolled(forward[b : b + 1]).astype(BF16)

    scr[...] = jnp.zeros_like(scr)
    group = lax.axis_index("cls")
    for half in range(2):
        come = group if half == 0 else 1 - group
        start = pl.multiple_of(come * count, 8)
        scr[half * count : (half + 1) * count, :classes] = mask[pl.ds(start, count)].astype(F32)
    mask_out[...] = scr[...].T[:padded, :total]
    n = noise[...]
    other = jnp.concatenate([n[:, count:], n[:, :count]], axis=1)
    noise_out[...] = jnp.where(group == 0, n, other)
    square = scr.shape[1]
    scr[:square] = jnp.zeros((square, square), F32)
    scr[:rots, :classes] = rot[...].astype(F32)
    turned = scr[:square].T
    for j in range(rots):
        rot_out[j] = jnp.broadcast_to(turned[:padded, j : j + 1], (padded, square))


def prepare(ctf, band, mask, noise, rot, after, padded):
    bins, width = ctf.shape
    total = noise.shape[0]
    lanes = max(128, -(-padded // 128) * 128)
    tall = -(-max(total, lanes) // 128) * 128
    return pl.pallas_call(
        prepare_kernel,
        out_shape=(
            pinned((bins, width, width), BF16),
            pinned((bins, width, width), BF16),
            pinned((padded, total), F32),
            pinned((1, total), F32),
            pinned((rot.shape[0], padded, lanes), F32),
        ),
        scratch_shapes=[pltpu.VMEM((tall, lanes), F32)],
        compiler_params=pltpu.CompilerParams(vmem_limit_bytes=4 * MIB),
        cost_estimate=cost(3),
        name="prepare",
    )(ctf, band.reshape(1, width), mask, noise.reshape(1, total), rot, held(after))


def gate_kernel(*refs):
    del refs


def gate(piece, *tokens):
    anywhere = pl.BlockSpec(memory_space=pl.ANY)
    return pl.pallas_call(
        gate_kernel,
        in_specs=[anywhere] * (1 + len(tokens)),
        out_specs=anywhere,
        out_shape=jax.ShapeDtypeStruct(piece.shape, piece.dtype),
        input_output_aliases={0: 0},
        compiler_params=pltpu.CompilerParams(vmem_limit_bytes=MIB),
        cost_estimate=cost(0.1),
        name="gate",
    )(piece, *tokens)


def refs_kernel(refs, out, norm, scratch, *, padded):
    classes, _, rows, width = refs.shape
    pitch = rows + PAD
    j = pl.program_id(0)

    def block(start, count):
        for k in range(GROUP):
            if k < count:
                scratch[pl.ds(k * pitch, rows)] = refs[start + k, 0].astype(F32)
            else:
                scratch[pl.ds(k * pitch, rows)] = jnp.zeros((rows, width), F32)
        at = pl.multiple_of(j * padded + start, GROUP)

        def step(r, acc):
            v = scratch[pl.ds(r, GROUP, stride=pitch)]
            out[r, pl.ds(at, GROUP)] = v.astype(BF16)
            return acc + v * v

        acc = lax.fori_loop(0, rows, step, jnp.zeros((GROUP, width), F32), unroll=32)
        total = 0.5 * jnp.sum(acc, axis=1, keepdims=True)
        norm[pl.ds(at, GROUP)] = jnp.broadcast_to(total, (GROUP, width))

    full = classes // GROUP

    @pl.loop(0, full)
    def _(i):
        block(i * GROUP, GROUP)

    if classes % GROUP:
        block(full * GROUP, classes % GROUP)


def lay_refs(refs, padded):
    classes, rots, rows, width = refs.shape
    vmem = pl.BlockSpec(memory_space=pltpu.VMEM)
    return pl.pallas_call(
        functools.partial(refs_kernel, padded=padded),
        grid=(rots,),
        in_specs=[pl.BlockSpec((classes, 1, rows, width), lambda j: (0, j, 0, 0))],
        out_specs=(vmem, vmem),
        out_shape=(
            pinned((rows, rots * padded, width), BF16),
            pinned((rots * padded, width), F32),
        ),
        scratch_shapes=[pltpu.VMEM((GROUP * (rows + PAD), width), F32)],
        compiler_params=pltpu.CompilerParams(vmem_limit_bytes=12 * MIB),
        cost_estimate=cost(9),
        name="refs",
    )(pltpu.with_memory_space_constraint(refs, pltpu.HBM))


def filter_kernel(bins, mine, left, right, *rest, parts, skip, at):
    sibs = rest[:parts]
    plain, turned, token = rest[-7:-4]
    scratch = rest[-4:]
    token[...] = jnp.zeros_like(token)
    width = mine.shape[2]
    top = lax.axis_index("section") == 0
    pitch = width + PAD

    def group(base, source, turn):
        scr, scr_t = scratch[2 * turn : 2 * turn + 2]
        for i in range(GROUP):
            b = bins[skip + base + i]
            a = mine[base + i]
            o = source(i)
            x = jnp.concatenate([jnp.where(top, a, o), jnp.where(top, o, a)], axis=0)
            f = nn(left[b], nn(x, right[b]).astype(BF16))
            scr[pl.ds(i * pitch, width)] = f
            scr_t[pl.ds(i * pitch, width)] = f.T
        to = pl.multiple_of(at + base, GROUP)
        for r in range(width):
            plain[r, pl.ds(to, GROUP)] = scr[pl.ds(r, GROUP, stride=pitch)].astype(BF16)
            turned[r, pl.ds(to, GROUP)] = scr_t[pl.ds(r, GROUP, stride=pitch)].astype(BF16)

    groups = mine.shape[0] // GROUP
    if parts > 1 or groups <= 2:
        places = [(sib, i) for sib in sibs for i in range(sib.shape[0])]
        for g in range(groups):

            def source(i, g=g):
                sib, place = places[g * GROUP + i]
                return sib[place]

            group(g * GROUP, source, g % 2)
    else:

        @pl.loop(0, groups)
        def _(g):
            base = pl.multiple_of(g * GROUP, GROUP)
            group(base, lambda i: sibs[0][base + i], 0)


def filter_chunk(bins, mine, sibs, left, right, buffers, total, skip, at):
    count, half, width = mine.shape
    smem = pl.BlockSpec(memory_space=pltpu.SMEM)
    vmem = pl.BlockSpec(memory_space=pltpu.VMEM)
    parts = len(sibs)
    return pl.pallas_call(
        functools.partial(filter_kernel, parts=parts, skip=skip, at=at),
        in_specs=[smem] + [vmem] * (3 + parts + len(buffers)),
        out_specs=(vmem, vmem, vmem),
        out_shape=(pinned((2 * half, total, width), BF16),) * 2
        + (jax.ShapeDtypeStruct((8, width), F32),),
        scratch_shapes=[pltpu.VMEM((GROUP * (2 * half + PAD), width), F32)] * 4,
        input_output_aliases={4 + parts + i: i for i in range(len(buffers))},
        compiler_params=pltpu.CompilerParams(vmem_limit_bytes=8 * MIB),
        cost_estimate=cost(count * 0.1),
        name="filter",
    )(bins, mine, held(left), held(right), *sibs, *[held(b) for b in buffers])


def score_kernel(plain, refs, norm, mask, noise, scaled, stats):
    rows, height, width = refs.shape
    count = mask.shape[1]

    def step(i, acc):
        at = [DEEP * i + a for a in range(DEEP)]
        lhs = jnp.concatenate([refs[r] for r in at], axis=1)
        rhs = jnp.concatenate([plain[r] for r in at], axis=1)
        return acc + nt(lhs, rhs)

    inner = lax.fori_loop(0, rows // DEEP, step, jnp.zeros((height, count), F32))
    rots = height // mask.shape[0]
    allowed = jnp.concatenate([mask[...]] * rots, axis=0) > 0
    s = jnp.where(allowed, (inner - norm[:, :1]) / noise[...], LOW)
    scaled[...] = s
    peak = jnp.max(s, axis=0, keepdims=True)
    total = jnp.sum(jnp.exp(s - peak), axis=0, keepdims=True)
    stats[0:1] = peak
    stats[1:2] = total
    stats[2:] = jnp.zeros((stats.shape[0] - 2, count), F32)


def score(plain, refs, norm, mask, noise):
    count = mask.shape[1]
    height = refs.shape[1]
    return pl.pallas_call(
        score_kernel,
        out_shape=(
            pinned((height, count), F32),
            pinned((8, count), F32),
        ),
        compiler_params=pltpu.CompilerParams(vmem_limit_bytes=8 * MIB),
        cost_estimate=cost(5),
        name="score",
    )(held(plain), held(refs), held(norm), held(mask), held(noise))


def weigh(scaled, mine, other, rot, out):
    rots, padded, _ = rot.shape
    count = scaled.shape[1]
    theirs = jnp.concatenate([other[:, count // 2 :], other[:, : count // 2]], axis=1)
    peak = jnp.maximum(mine[0:1], theirs[0:1])
    total = mine[1:2] * jnp.exp(mine[0:1] - peak) + theirs[1:2] * jnp.exp(theirs[0:1] - peak)
    w = (jnp.exp(scaled[...] - peak) / total).astype(BF16).astype(F32)
    quarters = []
    for q in range(4):
        acc = jnp.zeros((padded, count), F32)
        for j in range(rots):
            acc = acc + jnp.where(rot[j][:, :1] == q, w[j * padded : (j + 1) * padded], 0.0)
        quarters.append(acc)
    for row, pair in enumerate(((0, 3), (2, 1))):
        out[row] = jnp.concatenate([quarters[q] for q in pair], axis=1).astype(BF16)


def sums_kernel(plain, turned, *rest, outer, dom, start, rows, classes):
    if outer:
        weights = rest[0]
        outs = rest[-(dom // 2) :]
    else:
        weights = rest[-1]
        outs = rest[-3:-1]
        weigh(*rest[:4], weights)
    width = outs[0].shape[2]
    height = plain.shape[0]
    block = height // 2 // dom
    first = lax.axis_index("section") * (height // 2) + start
    own = lax.axis_index("dom")
    parity = own % 2
    straight = weights[0]
    mirrored = weights[1]
    flip = width - 1 - lax.broadcasted_iota(jnp.int32, (straight.shape[0], width), 1)

    def pair(g, sides, r):
        both = [first + (2 * g + side) * block + r for side in sides]
        direct = jnp.concatenate(
            [jnp.concatenate([plain[i], turned[height - 1 - i]], axis=0) for i in both], axis=1
        )
        mirror = jnp.concatenate(
            [jnp.concatenate([plain[height - 1 - i], turned[i]], axis=0) for i in both], axis=1
        )
        direct = nn(straight, direct)
        mirror = nn(mirrored, mirror)
        return [
            (
                direct[:, at : at + width]
                + jnp.take_along_axis(mirror[:, at : at + width], flip, axis=1)
            )[:classes]
            for at in (0, width)
        ]

    if outer:
        for m, out in enumerate(outs):
            for r in range(rows):
                for side, value in enumerate(pair(jnp.bitwise_xor(own // 2, m), (0, 1), r)):
                    out[side, r * classes : (r + 1) * classes] = value.astype(out.dtype)
    else:
        keep, send = outs

        @pl.loop(0, dom // 2)
        def _(g):
            for r in range(rows):
                away, here = pair(g, (1 - parity, parity), r)
                at = slice(r * classes, (r + 1) * classes)
                send[g, at] = away.astype(BF16)
                keep[g, at] = here


def sums(inputs, plain, turned, after, outer, dom, start, rows, classes):
    width = plain.shape[2]
    vmem = pl.BlockSpec(memory_space=pltpu.VMEM)
    count = 2 if outer else dom // 2
    shape = (count, rows * classes, width)
    out_shape = [pinned(shape, F32)]
    out_shape += [jax.ShapeDtypeStruct(shape, BF16)] * (dom // 2 - 1 if outer else 1)
    if not outer:
        rot = inputs[3]
        out_shape.append(pinned((2, rot.shape[1], 2 * plain.shape[1]), BF16))
    return pl.pallas_call(
        functools.partial(
            sums_kernel, outer=outer, dom=dom, start=start, rows=rows, classes=classes
        ),
        in_specs=[vmem] * (2 + len(inputs)) + [pl.BlockSpec(memory_space=pl.ANY)] * len(after),
        out_shape=tuple(out_shape),
        compiler_params=pltpu.CompilerParams(vmem_limit_bytes=8 * MIB),
        cost_estimate=cost(SUMS * rows),
        name="sums",
    )(held(plain), held(turned), *inputs, *after)


def gather_kernel(keep, *rest, came):
    got = rest[:came]
    here, away = rest[-2:]
    parity = lax.axis_index("dom") % 2
    for out, side in ((here, parity), (away, 1 - parity)):
        value = keep[side]
        for other in got:
            value = value + other[side].astype(F32)
        out[0] = value.astype(out.dtype)


def gather(keep, got):
    shape = (1,) + keep.shape[1:]
    return pl.pallas_call(
        functools.partial(gather_kernel, came=len(got)),
        out_shape=(pinned(shape, F32), jax.ShapeDtypeStruct(shape, BF16)),
        compiler_params=pltpu.CompilerParams(vmem_limit_bytes=8 * MIB),
        cost_estimate=cost(FOLD),
        name="gather",
    )(held(keep), *got)


def fold_kernel(keep, got, *outs, fan, bit):
    outs = outs[-fan:]
    rest = keep.shape[0] // fan
    at = (lax.axis_index("dom") // (1 << bit)) % fan
    for m, out in enumerate(outs):
        for i in range(rest):
            b = i * fan + jnp.bitwise_xor(at, m)
            value = keep[b] + got[b].astype(F32)
            out[i] = value.astype(out.dtype)


def fold(keep, got, after, fan, bit):
    rest = (keep.shape[0] // fan,) + keep.shape[1:]
    return pl.pallas_call(
        functools.partial(fold_kernel, fan=fan, bit=bit),
        in_specs=[pl.BlockSpec(memory_space=pltpu.VMEM)] * 2
        + [pl.BlockSpec(memory_space=pl.ANY)] * len(after),
        out_shape=(pinned(rest, F32),) + (jax.ShapeDtypeStruct(rest, BF16),) * (fan - 1),
        compiler_params=pltpu.CompilerParams(vmem_limit_bytes=8 * MIB),
        cost_estimate=cost(FOLD),
        name="fold",
    )(held(keep), got, *after)


def finish_kernel(*args, counts, classes):
    out = args[-1]
    block_rows = sum(rows for rows, _ in counts)
    at = 0
    row = 0
    for rows, pieces in counts:
        for r in range(rows):
            cut = slice(r * classes, (r + 1) * classes)
            value = args[at][0, cut]
            for other in args[at + 1 : at + pieces]:
                value = value + other[0, cut].astype(F32)
            out[pl.ds(row, classes, stride=block_rows)] = value
            row += 1
        at += pieces


def finish(done, classes):
    counts = tuple((pieces[0].shape[1] // classes, len(pieces)) for pieces in done)
    width = done[0][0].shape[2]
    block_rows = sum(rows for rows, _ in counts)
    flat = [held(p) if i == 0 else p for pieces in done for i, p in enumerate(pieces)]
    out = pl.pallas_call(
        functools.partial(finish_kernel, counts=counts, classes=classes),
        out_shape=jax.ShapeDtypeStruct((classes * block_rows, width), F32),
        compiler_params=pltpu.CompilerParams(vmem_limit_bytes=8 * MIB),
        cost_estimate=cost(1),
        name="finish",
    )(*flat)
    return out.reshape(classes, block_rows, width)


def y_pieces(particles):
    last = GROUP
    middle = particles // 3 // GROUP * GROUP
    return ((particles - middle - last, GROUP), (middle, GROUP // 2), (last, last))


def row_pieces(rows, dom):
    if rows < 4 or dom > 8:
        return (rows, 0)
    outer = rows * 3 // 8
    return (rows - outer, outer)


def local(
    images, defocus_bin, ctf_kernels, band_kernel, references, rot_index, class_mask, noise_var
):
    dom = lax.axis_size("dom")
    particles, half, width = images.shape
    classes = rot_index.shape[0]
    padded = -(-classes // GROUP) * GROUP
    swap = [(0, 1), (1, 0)]
    over_cls = functools.partial(lax.ppermute, axis_name="cls", perm=swap)
    over_section = functools.partial(lax.ppermute, axis_name="section", perm=swap)

    sizes, steps = zip(*y_pieces(particles))
    starts = [sum(sizes[:i]) for i in range(len(sizes))]
    remote = [over_cls(images[a : a + n]) for a, n in zip(starts, sizes)]
    other_bins = over_cls(defocus_bin)
    own_sib = over_section(images)

    refs, norm = lay_refs(references, padded)
    left, right, mask, noise, rot = prepare(
        ctf_kernels, band_kernel, class_mask, noise_var, rot_index.T, norm, padded
    )
    total = 2 * particles
    *buffers, token = filter_chunk(
        defocus_bin, images, [own_sib], left, right, (), total, 0, 0
    )
    tokens = (token, other_bins)
    for i, a in enumerate(starts):
        piece = gate(remote[i], *tokens)
        step = steps[i]
        sibs = [over_section(piece[b : b + step]) for b in range(0, sizes[i], step)]
        *buffers, token = filter_chunk(
            other_bins, piece, sibs, left, right, buffers, total, a, particles + a
        )
        tokens = (token,)
    plain, turned = buffers

    scaled, stats = score(plain, refs, norm, mask, noise)
    inputs = (held(scaled), held(stats), over_cls(stats), held(rot))

    def along(x, mask):
        return lax.ppermute(x, "dom", [(i, i ^ mask) for i in range(dom)])

    def spread(sends, bit):
        far_first = sorted(range(len(sends)), key=lambda m: m == 0)
        return [along(sends[m], (m + 1) << bit) for m in far_first]

    inner, outer = row_pieces(half // dom, dom)
    keep, send, weights = sums(inputs, plain, turned, (), False, dom, 0, inner, classes)
    got = along(send, 1)
    if outer:
        keep_b, *sends_b = sums(
            (held(weights),), plain, turned, (send,), True, dom, inner, outer, classes
        )
        got_b = spread(sends_b, 1)
    bit = 1
    while keep.shape[0] > 4:
        keep, send = fold(keep, got, (), 2, bit)
        got = along(send, 1 << bit)
        bit += 1
    keep, *sends = fold(keep, got, (), keep.shape[0], bit)
    done = [[keep] + spread(sends, bit)]
    if outer:
        keep_b, send_b = gather(keep_b, got_b)
        done.append([keep_b, along(send_b, 1)])
    return finish(done, classes)


def solution(mesh):
    return jax.shard_map(
        local,
        mesh=mesh,
        in_specs=(
            P(("dom", "cls"), "section", None),
            P(("dom", "cls")),
            P(),
            P(),
            P("cls", None, None, None),
            P("cls", None),
            P("dom", "cls"),
            P("dom"),
        ),
        out_specs=P("cls", ("section", "dom"), None),
        check_vma=False,
    )
```

```python
import functools

import jax
import jax.numpy as jnp
from jax import lax
from jax.experimental import pallas as pl
from jax.experimental.pallas import tpu as pltpu
from jax.sharding import PartitionSpec as P

F32 = jnp.float32
BF16 = jnp.bfloat16
LOW = -1e30
GROUP = 16
PAD = 8
DEEP = 128
SUMS = 0.8
SCALE = 0.1
FOLD = 1
MIB = 1 << 20


def nt(a, b, precision=None):
    return lax.dot_general(
        a, b, (((1,), (1,)), ((), ())), preferred_element_type=F32, precision=precision
    )


def nn(a, b):
    return lax.dot_general(a, b, (((1,), (0,)), ((), ())), preferred_element_type=F32)


def cost(microseconds):
    return pl.CostEstimate(
        flops=int(microseconds * SCALE * 1e9), transcendentals=0, bytes_accessed=int(microseconds * SCALE * 3e6)
    )


def pinned(shape, dtype):
    return pltpu.VMEM(shape, dtype)


def held(x):
    return pltpu.with_memory_space_constraint(x, pltpu.VMEM)


def prepare_kernel(ctf, band, mask, noise, rot, after, left, right, mask_out, noise_out, rot_out, scr):
    del after
    bins, width = ctf.shape
    rots, classes = rot.shape
    padded = rot_out.shape[1]
    total = mask.shape[0]
    count = total // 2

    def negated(v):
        at = (width - lax.broadcasted_iota(jnp.int32, v.shape, 1)) % width
        return jnp.take_along_axis(v, at, axis=1)

    def rolled(row):
        return pltpu.roll(jnp.broadcast_to(row, (width, width)), 0, 1, stride=1, stride_axis=0)

    def with_delta(v):
        return v + jnp.where(lax.broadcasted_iota(jnp.int32, v.shape, 1) == 0, 1.0, 0.0)

    highest = lax.Precision.HIGHEST
    kernels = with_delta(ctf[...])
    bands = with_delta(jnp.broadcast_to(band[...], (8, width)))
    forward = nt(kernels, rolled(negated(bands)[:1]), highest)
    backward = nt(negated(kernels), rolled(bands[:1]), highest)
    for b in range(bins):
        left[b] = rolled(backward[b : b + 1]).astype(BF16)
        right[b] = rolled(forward[b : b + 1]).astype(BF16)

    scr[...] = jnp.zeros_like(scr)
    group = lax.axis_index("cls")
    for half in range(2):
        come = group if half == 0 else 1 - group
        start = pl.multiple_of(come * count, 8)
        scr[half * count : (half + 1) * count, :classes] = mask[pl.ds(start, count)].astype(F32)
    mask_out[...] = scr[...].T[:padded, :total]
    n = noise[...]
    other = jnp.concatenate([n[:, count:], n[:, :count]], axis=1)
    noise_out[...] = jnp.where(group == 0, n, other)
    square = scr.shape[1]
    scr[:square] = jnp.zeros((square, square), F32)
    scr[:rots, :classes] = rot[...].astype(F32)
    turned = scr[:square].T
    for j in range(rots):
        rot_out[j] = jnp.broadcast_to(turned[:padded, j : j + 1], (padded, square))


def prepare(ctf, band, mask, noise, rot, after, padded):
    bins, width = ctf.shape
    total = noise.shape[0]
    lanes = max(128, -(-padded // 128) * 128)
    tall = -(-max(total, lanes) // 128) * 128
    return pl.pallas_call(
        prepare_kernel,
        out_shape=(
            pinned((bins, width, width), BF16),
            pinned((bins, width, width), BF16),
            pinned((padded, total), F32),
            pinned((1, total), F32),
            pinned((rot.shape[0], padded, lanes), F32),
        ),
        scratch_shapes=[pltpu.VMEM((tall, lanes), F32)],
        compiler_params=pltpu.CompilerParams(vmem_limit_bytes=4 * MIB),
        cost_estimate=cost(3),
        name="prepare",
    )(ctf, band.reshape(1, width), mask, noise.reshape(1, total), rot, held(after))


def gate_kernel(*refs):
    del refs


def gate(piece, *tokens):
    anywhere = pl.BlockSpec(memory_space=pl.ANY)
    return pl.pallas_call(
        gate_kernel,
        in_specs=[anywhere] * (1 + len(tokens)),
        out_specs=anywhere,
        out_shape=jax.ShapeDtypeStruct(piece.shape, piece.dtype),
        input_output_aliases={0: 0},
        compiler_params=pltpu.CompilerParams(vmem_limit_bytes=MIB),
        cost_estimate=cost(0.1),
        name="gate",
    )(piece, *tokens)


def refs_kernel(refs, out, norm, scratch, *, padded):
    classes, _, rows, width = refs.shape
    pitch = rows + PAD
    j = pl.program_id(0)

    def block(start, count):
        for k in range(GROUP):
            if k < count:
                scratch[pl.ds(k * pitch, rows)] = refs[start + k, 0].astype(F32)
            else:
                scratch[pl.ds(k * pitch, rows)] = jnp.zeros((rows, width), F32)
        at = pl.multiple_of(j * padded + start, GROUP)

        def step(r, acc):
            v = scratch[pl.ds(r, GROUP, stride=pitch)]
            out[r, pl.ds(at, GROUP)] = v.astype(BF16)
            return acc + v * v

        acc = lax.fori_loop(0, rows, step, jnp.zeros((GROUP, width), F32), unroll=32)
        total = 0.5 * jnp.sum(acc, axis=1, keepdims=True)
        norm[pl.ds(at, GROUP)] = jnp.broadcast_to(total, (GROUP, width))

    full = classes // GROUP

    @pl.loop(0, full)
    def _(i):
        block(i * GROUP, GROUP)

    if classes % GROUP:
        block(full * GROUP, classes % GROUP)


def lay_refs(refs, padded):
    classes, rots, rows, width = refs.shape
    vmem = pl.BlockSpec(memory_space=pltpu.VMEM)
    return pl.pallas_call(
        functools.partial(refs_kernel, padded=padded),
        grid=(rots,),
        in_specs=[pl.BlockSpec((classes, 1, rows, width), lambda j: (0, j, 0, 0))],
        out_specs=(vmem, vmem),
        out_shape=(
            pinned((rows, rots * padded, width), BF16),
            pinned((rots * padded, width), F32),
        ),
        scratch_shapes=[pltpu.VMEM((GROUP * (rows + PAD), width), F32)],
        compiler_params=pltpu.CompilerParams(vmem_limit_bytes=12 * MIB),
        cost_estimate=cost(9),
        name="refs",
    )(pltpu.with_memory_space_constraint(refs, pltpu.HBM))


def filter_kernel(*args, picked, parts, skip, at, chained):
    bins = None if picked else args[0]
    mine, left, right, *rest = args[0 if picked else 1 :]
    sibs = rest[:parts]
    plain, turned, *token = rest[-6 - chained : -4]
    scratch = rest[-4:]
    for t in token:
        t[...] = jnp.zeros_like(t)
    width = mine.shape[2]
    top = lax.axis_index("section") == 0
    pitch = width + PAD

    def group(base, source, turn):
        scr, scr_t = scratch[2 * turn : 2 * turn + 2]
        for i in range(GROUP):
            b = base + i if picked else bins[skip + base + i]
            a = mine[base + i]
            o = source(i)
            x = jnp.concatenate([jnp.where(top, a, o), jnp.where(top, o, a)], axis=0)
            f = nn(left[b], nn(x, right[b]).astype(BF16))
            scr[pl.ds(i * pitch, width)] = f
            scr_t[pl.ds(i * pitch, width)] = f.T
        to = pl.multiple_of(at + base, GROUP)
        for r in range(width):
            plain[r, pl.ds(to, GROUP)] = scr[pl.ds(r, GROUP, stride=pitch)].astype(BF16)
            turned[r, pl.ds(to, GROUP)] = scr_t[pl.ds(r, GROUP, stride=pitch)].astype(BF16)

    groups = mine.shape[0] // GROUP
    if parts > 1 or groups <= 2:
        places = [(sib, i) for sib in sibs for i in range(sib.shape[0])]
        for g in range(groups):

            def source(i, g=g):
                sib, place = places[g * GROUP + i]
                return sib[place]

            group(g * GROUP, source, g % 2)
    else:

        @pl.loop(0, groups)
        def _(g):
            base = pl.multiple_of(g * GROUP, GROUP)
            group(base, lambda i: sibs[0][base + i], 0)


def filter_chunk(bins, mine, sibs, left, right, buffers, total, skip, at, chained):
    count, half, width = mine.shape
    smem = pl.BlockSpec(memory_space=pltpu.SMEM)
    vmem = pl.BlockSpec(memory_space=pltpu.VMEM)
    parts = len(sibs)
    picked = bins is None
    head = [] if picked else [bins]
    return pl.pallas_call(
        functools.partial(
            filter_kernel, picked=picked, parts=parts, skip=skip, at=at, chained=chained
        ),
        in_specs=[smem] * len(head) + [vmem] * (3 + parts + len(buffers)),
        out_specs=(vmem,) * (2 + chained),
        out_shape=(pinned((2 * half, total, width), BF16),) * 2
        + (pinned((8, width), F32),) * chained,
        scratch_shapes=[pltpu.VMEM((GROUP * (2 * half + PAD), width), F32)] * 4,
        input_output_aliases={len(head) + 3 + parts + i: i for i in range(len(buffers))},
        compiler_params=pltpu.CompilerParams(vmem_limit_bytes=8 * MIB),
        cost_estimate=cost(count * 0.1),
        name="filter",
    )(*head, mine, held(left), held(right), *sibs, *[held(b) for b in buffers])


def pick_kernel(bins, left, right, after, left_out, right_out, *, skip):
    del after
    for i in range(left_out.shape[0]):
        left_out[i] = left[bins[skip + i]]
        right_out[i] = right[bins[skip + i]]


def pick(bins, left, right, after, skip, count):
    vmem = pl.BlockSpec(memory_space=pltpu.VMEM)
    return pl.pallas_call(
        functools.partial(pick_kernel, skip=skip),
        in_specs=[pl.BlockSpec(memory_space=pltpu.SMEM), vmem, vmem, vmem],
        out_shape=(pinned((count,) + left.shape[1:], BF16),) * 2,
        compiler_params=pltpu.CompilerParams(vmem_limit_bytes=4 * MIB),
        cost_estimate=cost(1),
        name="pick",
    )(bins, held(left), held(right), held(after))


def score_kernel(plain, refs, norm, mask, noise, scaled, stats):
    rows, height, width = refs.shape
    count = mask.shape[1]

    def step(i, acc):
        at = [DEEP * i + a for a in range(DEEP)]
        lhs = jnp.concatenate([refs[r] for r in at], axis=1)
        rhs = jnp.concatenate([plain[r] for r in at], axis=1)
        return acc + nt(lhs, rhs)

    inner = lax.fori_loop(0, rows // DEEP, step, jnp.zeros((height, count), F32))
    rots = height // mask.shape[0]
    allowed = jnp.concatenate([mask[...]] * rots, axis=0) > 0
    s = jnp.where(allowed, (inner - norm[:, :1]) / noise[...], LOW)
    scaled[...] = s
    peak = jnp.max(s, axis=0, keepdims=True)
    total = jnp.sum(jnp.exp(s - peak), axis=0, keepdims=True)
    stats[0:1] = peak
    stats[1:2] = total
    stats[2:] = jnp.zeros((stats.shape[0] - 2, count), F32)


def score(plain, refs, norm, mask, noise):
    count = mask.shape[1]
    height = refs.shape[1]
    return pl.pallas_call(
        score_kernel,
        out_shape=(
            pinned((height, count), F32),
            pinned((8, count), F32),
        ),
        compiler_params=pltpu.CompilerParams(vmem_limit_bytes=8 * MIB),
        cost_estimate=cost(5),
        name="score",
    )(held(plain), held(refs), held(norm), held(mask), held(noise))


def weigh(scaled, mine, other, rot, out):
    rots, padded, _ = rot.shape
    count = scaled.shape[1]
    theirs = jnp.concatenate([other[:, count // 2 :], other[:, : count // 2]], axis=1)
    peak = jnp.maximum(mine[0:1], theirs[0:1])
    total = mine[1:2] * jnp.exp(mine[0:1] - peak) + theirs[1:2] * jnp.exp(theirs[0:1] - peak)
    w = (jnp.exp(scaled[...] - peak) / total).astype(BF16).astype(F32)
    quarters = []
    for q in range(4):
        acc = jnp.zeros((padded, count), F32)
        for j in range(rots):
            acc = acc + jnp.where(rot[j][:, :1] == q, w[j * padded : (j + 1) * padded], 0.0)
        quarters.append(acc)
    for row, pair in enumerate(((0, 3), (2, 1))):
        out[row] = jnp.concatenate([quarters[q] for q in pair], axis=1).astype(BF16)


def sums_kernel(plain, turned, *rest, outer, dom, start, rows, classes):
    if outer:
        weights = rest[0]
        outs = rest[-(dom // 2) :]
    else:
        weights = rest[-1]
        outs = rest[-3:-1]
        weigh(*rest[:4], weights)
    width = outs[0].shape[2]
    height = plain.shape[0]
    block = height // 2 // dom
    first = lax.axis_index("section") * (height // 2) + start
    own = lax.axis_index("dom")
    parity = own % 2
    straight = weights[0]
    mirrored = weights[1]
    flip = width - 1 - lax.broadcasted_iota(jnp.int32, (straight.shape[0], width), 1)

    def pair(g, sides, r):
        both = [first + (2 * g + side) * block + r for side in sides]
        direct = jnp.concatenate(
            [jnp.concatenate([plain[i], turned[height - 1 - i]], axis=0) for i in both], axis=1
        )
        mirror = jnp.concatenate(
            [jnp.concatenate([plain[height - 1 - i], turned[i]], axis=0) for i in both], axis=1
        )
        direct = nn(straight, direct)
        mirror = nn(mirrored, mirror)
        return [
            (
                direct[:, at : at + width]
                + jnp.take_along_axis(mirror[:, at : at + width], flip, axis=1)
            )[:classes]
            for at in (0, width)
        ]

    if outer:
        for m, out in enumerate(outs):
            for r in range(rows):
                for side, value in enumerate(pair(jnp.bitwise_xor(own // 2, m), (0, 1), r)):
                    out[side, r * classes : (r + 1) * classes] = value.astype(out.dtype)
    else:
        keep, send = outs

        @pl.loop(0, dom // 2)
        def _(g):
            for r in range(rows):
                away, here = pair(g, (1 - parity, parity), r)
                at = slice(r * classes, (r + 1) * classes)
                send[g, at] = away.astype(BF16)
                keep[g, at] = here


def sums(inputs, plain, turned, after, outer, dom, start, rows, classes):
    width = plain.shape[2]
    vmem = pl.BlockSpec(memory_space=pltpu.VMEM)
    count = 2 if outer else dom // 2
    shape = (count, rows * classes, width)
    out_shape = [pinned(shape, F32)]
    out_shape += [jax.ShapeDtypeStruct(shape, BF16)] * (dom // 2 - 1 if outer else 1)
    if not outer:
        rot = inputs[3]
        out_shape.append(pinned((2, rot.shape[1], 2 * plain.shape[1]), BF16))
    return pl.pallas_call(
        functools.partial(
            sums_kernel, outer=outer, dom=dom, start=start, rows=rows, classes=classes
        ),
        in_specs=[vmem] * (2 + len(inputs)) + [pl.BlockSpec(memory_space=pl.ANY)] * len(after),
        out_shape=tuple(out_shape),
        compiler_params=pltpu.CompilerParams(vmem_limit_bytes=8 * MIB),
        cost_estimate=cost(SUMS * rows),
        name="sums",
    )(held(plain), held(turned), *inputs, *after)


def gather_kernel(keep, *rest, came):
    got = rest[:came]
    here, away = rest[-2:]
    parity = lax.axis_index("dom") % 2
    for out, side in ((here, parity), (away, 1 - parity)):
        value = keep[side]
        for other in got:
            value = value + other[side].astype(F32)
        out[0] = value.astype(out.dtype)


def gather(keep, got):
    shape = (1,) + keep.shape[1:]
    return pl.pallas_call(
        functools.partial(gather_kernel, came=len(got)),
        out_shape=(pinned(shape, F32), jax.ShapeDtypeStruct(shape, BF16)),
        compiler_params=pltpu.CompilerParams(vmem_limit_bytes=8 * MIB),
        cost_estimate=cost(FOLD),
        name="gather",
    )(held(keep), *got)


def fold_kernel(keep, got, *outs, fan, bit):
    outs = outs[-fan:]
    rest = keep.shape[0] // fan
    at = (lax.axis_index("dom") // (1 << bit)) % fan
    for m, out in enumerate(outs):
        for i in range(rest):
            b = i * fan + jnp.bitwise_xor(at, m)
            value = keep[b] + got[b].astype(F32)
            out[i] = value.astype(out.dtype)


def fold(keep, got, after, fan, bit):
    rest = (keep.shape[0] // fan,) + keep.shape[1:]
    return pl.pallas_call(
        functools.partial(fold_kernel, fan=fan, bit=bit),
        in_specs=[pl.BlockSpec(memory_space=pltpu.VMEM)] * 2
        + [pl.BlockSpec(memory_space=pl.ANY)] * len(after),
        out_shape=(pinned(rest, F32),) + (jax.ShapeDtypeStruct(rest, BF16),) * (fan - 1),
        compiler_params=pltpu.CompilerParams(vmem_limit_bytes=8 * MIB),
        cost_estimate=cost(FOLD),
        name="fold",
    )(held(keep), got, *after)


def finish_kernel(*args, counts, classes):
    out = args[-1]
    block_rows = sum(rows for rows, _ in counts)
    at = 0
    row = 0
    for rows, pieces in counts:
        for r in range(rows):
            cut = slice(r * classes, (r + 1) * classes)
            value = args[at][0, cut]
            for other in args[at + 1 : at + pieces]:
                value = value + other[0, cut].astype(F32)
            out[pl.ds(row, classes, stride=block_rows)] = value
            row += 1
        at += pieces


def finish(done, classes):
    counts = tuple((pieces[0].shape[1] // classes, len(pieces)) for pieces in done)
    width = done[0][0].shape[2]
    block_rows = sum(rows for rows, _ in counts)
    flat = [held(p) if i == 0 else p for pieces in done for i, p in enumerate(pieces)]
    out = pl.pallas_call(
        functools.partial(finish_kernel, counts=counts, classes=classes),
        out_shape=jax.ShapeDtypeStruct((classes * block_rows, width), F32),
        compiler_params=pltpu.CompilerParams(vmem_limit_bytes=8 * MIB),
        cost_estimate=cost(1),
        name="finish",
    )(*flat)
    return out.reshape(classes, block_rows, width)


def y_pieces(particles):
    last = GROUP
    middle = particles // 3 // GROUP * GROUP
    return ((particles - middle - last, GROUP), (middle, GROUP // 2), (last, last))


def row_pieces(rows, dom):
    if rows < 4 or dom > 8:
        return (rows, 0)
    outer = rows * 3 // 8
    return (rows - outer, outer)


def local(
    images, defocus_bin, ctf_kernels, band_kernel, references, rot_index, class_mask, noise_var
):
    dom = lax.axis_size("dom")
    particles, half, width = images.shape
    classes = rot_index.shape[0]
    padded = -(-classes // GROUP) * GROUP
    swap = [(0, 1), (1, 0)]
    over_cls = functools.partial(lax.ppermute, axis_name="cls", perm=swap)
    over_section = functools.partial(lax.ppermute, axis_name="section", perm=swap)

    sizes, steps = zip(*y_pieces(particles))
    starts = [sum(sizes[:i]) for i in range(len(sizes))]
    remote = [over_cls(images[a : a + n]) for a, n in zip(starts, sizes)]
    other_bins = over_cls(defocus_bin)
    own_sib = over_section(images)

    refs, norm = lay_refs(references, padded)
    left, right, mask, noise, rot = prepare(
        ctf_kernels, band_kernel, class_mask, noise_var, rot_index.T, norm, padded
    )
    total = 2 * particles
    *buffers, token = filter_chunk(
        defocus_bin, images, [own_sib], left, right, (), total, 0, 0, 1
    )
    chosen = pick(other_bins, left, right, token, starts[-1], sizes[-1])
    tokens = [chosen[0]]
    for i, a in enumerate(starts):
        piece = gate(remote[i], *tokens)
        step = steps[i]
        sibs = [over_section(piece[b : b + step]) for b in range(0, sizes[i], step)]
        last = i + 1 == len(starts)
        filters = (None, piece, sibs, *chosen) if last else (other_bins, piece, sibs, left, right)
        made = filter_chunk(*filters, buffers, total, a, particles + a, int(not last))
        buffers = made[:2]
        tokens = made[2:]
    plain, turned = buffers

    scaled, stats = score(plain, refs, norm, mask, noise)
    inputs = (held(scaled), held(stats), over_cls(stats), held(rot))

    def along(x, mask):
        return lax.ppermute(x, "dom", [(i, i ^ mask) for i in range(dom)])

    def spread(sends, bit):
        far_first = sorted(range(len(sends)), key=lambda m: m == 0)
        return [along(sends[m], (m + 1) << bit) for m in far_first]

    inner, outer = row_pieces(half // dom, dom)
    keep, send, weights = sums(inputs, plain, turned, (), False, dom, 0, inner, classes)
    got = along(send, 1)
    if outer:
        keep_b, *sends_b = sums(
            (held(weights),), plain, turned, (send,), True, dom, inner, outer, classes
        )
        got_b = spread(sends_b, 1)
    bit = 1
    while keep.shape[0] > 4:
        keep, send = fold(keep, got, (), 2, bit)
        got = along(send, 1 << bit)
        bit += 1
    keep, *sends = fold(keep, got, (), keep.shape[0], bit)
    done = [[keep] + spread(sends, bit)]
    if outer:
        keep_b, send_b = gather(keep_b, got_b)
        done.append([keep_b, along(send_b, 1)])
    return finish(done, classes)


def solution(mesh):
    return jax.shard_map(
        local,
        mesh=mesh,
        in_specs=(
            P(("dom", "cls"), "section", None),
            P(("dom", "cls")),
            P(),
            P(),
            P("cls", None, None, None),
            P("cls", None),
            P("dom", "cls"),
            P("dom"),
        ),
        out_specs=P("cls", ("section", "dom"), None),
        check_vma=False,
    )
```

```python
import functools

import jax
import jax.numpy as jnp
from jax import lax
from jax.experimental import pallas as pl
from jax.experimental.pallas import tpu as pltpu
from jax.sharding import PartitionSpec as P

F32 = jnp.float32
BF16 = jnp.bfloat16
LOW = -1e30
GROUP = 16
PAD = 8
DEEP = 128
SUMS = 0.8
SCALE = 0.1
FOLD = 1
MIB = 1 << 20


def nt(a, b, precision=None):
    return lax.dot_general(
        a, b, (((1,), (1,)), ((), ())), preferred_element_type=F32, precision=precision
    )


def nn(a, b):
    return lax.dot_general(a, b, (((1,), (0,)), ((), ())), preferred_element_type=F32)


def cost(microseconds):
    return pl.CostEstimate(
        flops=int(microseconds * SCALE * 1e9), transcendentals=0, bytes_accessed=int(microseconds * SCALE * 3e6)
    )


def pinned(shape, dtype):
    return pltpu.VMEM(shape, dtype)


def held(x):
    return pltpu.with_memory_space_constraint(x, pltpu.VMEM)


def prepare_kernel(ctf, band, mask, noise, rot, after, left, right, mask_out, noise_out, rot_out, scr):
    del after
    bins, width = ctf.shape
    rots, classes = rot.shape
    padded = rot_out.shape[1]
    total = mask.shape[0]
    count = total // 2

    def negated(v):
        at = (width - lax.broadcasted_iota(jnp.int32, v.shape, 1)) % width
        return jnp.take_along_axis(v, at, axis=1)

    def rolled(row):
        return pltpu.roll(jnp.broadcast_to(row, (width, width)), 0, 1, stride=1, stride_axis=0)

    def with_delta(v):
        return v + jnp.where(lax.broadcasted_iota(jnp.int32, v.shape, 1) == 0, 1.0, 0.0)

    highest = lax.Precision.HIGHEST
    kernels = with_delta(ctf[...])
    bands = with_delta(jnp.broadcast_to(band[...], (8, width)))
    forward = nt(kernels, rolled(negated(bands)[:1]), highest)
    backward = nt(negated(kernels), rolled(bands[:1]), highest)
    for b in range(bins):
        left[b] = rolled(backward[b : b + 1]).astype(BF16)
        right[b] = rolled(forward[b : b + 1]).astype(BF16)

    scr[...] = jnp.zeros_like(scr)
    group = lax.axis_index("cls")
    for half in range(2):
        come = group if half == 0 else 1 - group
        start = pl.multiple_of(come * count, 8)
        scr[half * count : (half + 1) * count, :classes] = mask[pl.ds(start, count)].astype(F32)
    mask_out[...] = scr[...].T[:padded, :total]
    n = noise[...]
    other = jnp.concatenate([n[:, count:], n[:, :count]], axis=1)
    noise_out[...] = jnp.where(group == 0, n, other)
    square = scr.shape[1]
    scr[:square] = jnp.zeros((square, square), F32)
    scr[:rots, :classes] = rot[...].astype(F32)
    turned = scr[:square].T
    for j in range(rots):
        rot_out[j] = jnp.broadcast_to(turned[:padded, j : j + 1], (padded, square))


def prepare(ctf, band, mask, noise, rot, after, padded):
    bins, width = ctf.shape
    total = noise.shape[0]
    lanes = max(128, -(-padded // 128) * 128)
    tall = -(-max(total, lanes) // 128) * 128
    return pl.pallas_call(
        prepare_kernel,
        out_shape=(
            pinned((bins, width, width), BF16),
            pinned((bins, width, width), BF16),
            pinned((padded, total), F32),
            pinned((1, total), F32),
            pinned((rot.shape[0], padded, lanes), F32),
        ),
        scratch_shapes=[pltpu.VMEM((tall, lanes), F32)],
        compiler_params=pltpu.CompilerParams(vmem_limit_bytes=4 * MIB),
        cost_estimate=cost(3),
        name="prepare",
    )(ctf, band.reshape(1, width), mask, noise.reshape(1, total), rot, held(after))


def gate_kernel(*refs):
    del refs


def gate(piece, *tokens):
    anywhere = pl.BlockSpec(memory_space=pl.ANY)
    return pl.pallas_call(
        gate_kernel,
        in_specs=[anywhere] * (1 + len(tokens)),
        out_specs=anywhere,
        out_shape=jax.ShapeDtypeStruct(piece.shape, piece.dtype),
        input_output_aliases={0: 0},
        compiler_params=pltpu.CompilerParams(vmem_limit_bytes=MIB),
        cost_estimate=cost(0.1),
        name="gate",
    )(piece, *tokens)


def refs_kernel(refs, out, norm, scratch, *, padded):
    classes, _, rows, width = refs.shape
    pitch = rows + PAD
    j = pl.program_id(0)

    def block(start, count):
        for k in range(GROUP):
            if k < count:
                scratch[pl.ds(k * pitch, rows)] = refs[start + k, 0].astype(F32)
            else:
                scratch[pl.ds(k * pitch, rows)] = jnp.zeros((rows, width), F32)
        at = pl.multiple_of(j * padded + start, GROUP)

        def step(r, acc):
            v = scratch[pl.ds(r, GROUP, stride=pitch)]
            out[r, pl.ds(at, GROUP)] = v.astype(BF16)
            return acc + v * v

        acc = lax.fori_loop(0, rows, step, jnp.zeros((GROUP, width), F32), unroll=32)
        total = 0.5 * jnp.sum(acc, axis=1, keepdims=True)
        norm[pl.ds(at, GROUP)] = jnp.broadcast_to(total, (GROUP, width))

    full = classes // GROUP

    @pl.loop(0, full)
    def _(i):
        block(i * GROUP, GROUP)

    if classes % GROUP:
        block(full * GROUP, classes % GROUP)


def lay_refs(refs, padded):
    classes, rots, rows, width = refs.shape
    vmem = pl.BlockSpec(memory_space=pltpu.VMEM)
    return pl.pallas_call(
        functools.partial(refs_kernel, padded=padded),
        grid=(rots,),
        in_specs=[pl.BlockSpec((classes, 1, rows, width), lambda j: (0, j, 0, 0))],
        out_specs=(vmem, vmem),
        out_shape=(
            pinned((rows, rots * padded, width), BF16),
            pinned((rots * padded, width), F32),
        ),
        scratch_shapes=[pltpu.VMEM((GROUP * (rows + PAD), width), F32)],
        compiler_params=pltpu.CompilerParams(vmem_limit_bytes=12 * MIB),
        cost_estimate=cost(9),
        name="refs",
    )(pltpu.with_memory_space_constraint(refs, pltpu.HBM))


def filter_kernel(*args, picked, parts, skip, at, chained):
    bins = None if picked else args[0]
    mine, left, right, *rest = args[0 if picked else 1 :]
    sibs = rest[:parts]
    plain, turned, *token = rest[-6 - chained : -4]
    scratch = rest[-4:]
    for t in token:
        t[...] = jnp.zeros_like(t)
    width = mine.shape[2]
    top = lax.axis_index("section") == 0
    pitch = width + PAD

    def group(base, source, turn):
        scr, scr_t = scratch[2 * turn : 2 * turn + 2]
        for i in range(GROUP):
            b = base + i if picked else bins[skip + base + i]
            a = mine[base + i]
            o = source(i)
            x = jnp.concatenate([jnp.where(top, a, o), jnp.where(top, o, a)], axis=0)
            f = nn(left[b], nn(x, right[b]).astype(BF16))
            scr[pl.ds(i * pitch, width)] = f
            scr_t[pl.ds(i * pitch, width)] = f.T
        to = pl.multiple_of(at + base, GROUP)
        for r in range(width):
            plain[r, pl.ds(to, GROUP)] = scr[pl.ds(r, GROUP, stride=pitch)].astype(BF16)
            turned[r, pl.ds(to, GROUP)] = scr_t[pl.ds(r, GROUP, stride=pitch)].astype(BF16)

    groups = mine.shape[0] // GROUP
    if parts > 1 or groups <= 2:
        places = [(sib, i) for sib in sibs for i in range(sib.shape[0])]
        for g in range(groups):

            def source(i, g=g):
                sib, place = places[g * GROUP + i]
                return sib[place]

            group(g * GROUP, source, g % 2)
    else:

        @pl.loop(0, groups)
        def _(g):
            base = pl.multiple_of(g * GROUP, GROUP)
            group(base, lambda i: sibs[0][base + i], 0)


def filter_chunk(bins, mine, sibs, left, right, buffers, total, skip, at, chained):
    count, half, width = mine.shape
    smem = pl.BlockSpec(memory_space=pltpu.SMEM)
    vmem = pl.BlockSpec(memory_space=pltpu.VMEM)
    parts = len(sibs)
    picked = bins is None
    head = [] if picked else [bins]
    return pl.pallas_call(
        functools.partial(
            filter_kernel, picked=picked, parts=parts, skip=skip, at=at, chained=chained
        ),
        in_specs=[smem] * len(head) + [vmem] * (3 + parts + len(buffers)),
        out_specs=(vmem,) * (2 + chained),
        out_shape=(pinned((2 * half, total, width), BF16),) * 2
        + (pinned((8, width), F32),) * chained,
        scratch_shapes=[pltpu.VMEM((GROUP * (2 * half + PAD), width), F32)] * 4,
        input_output_aliases={len(head) + 3 + parts + i: i for i in range(len(buffers))},
        compiler_params=pltpu.CompilerParams(vmem_limit_bytes=8 * MIB),
        cost_estimate=cost(count * 0.1),
        name="filter",
    )(*head, mine, held(left), held(right), *sibs, *[held(b) for b in buffers])


def pick_kernel(bins, left, right, after, left_out, right_out, *, skip):
    del after
    for i in range(left_out.shape[0]):
        left_out[i] = left[bins[skip + i]]
        right_out[i] = right[bins[skip + i]]


def pick(bins, left, right, after, skip, count):
    vmem = pl.BlockSpec(memory_space=pltpu.VMEM)
    return pl.pallas_call(
        functools.partial(pick_kernel, skip=skip),
        in_specs=[pl.BlockSpec(memory_space=pltpu.SMEM), vmem, vmem, vmem],
        out_shape=(pinned((count,) + left.shape[1:], BF16),) * 2,
        compiler_params=pltpu.CompilerParams(vmem_limit_bytes=4 * MIB),
        cost_estimate=cost(1),
        name="pick",
    )(bins, held(left), held(right), held(after))


def score_kernel(plain, refs, norm, mask, noise, scaled, stats):
    rows, height, width = refs.shape
    count = mask.shape[1]

    def step(i, acc):
        at = [DEEP * i + a for a in range(DEEP)]
        lhs = jnp.concatenate([refs[r] for r in at], axis=1)
        rhs = jnp.concatenate([plain[r] for r in at], axis=1)
        return acc + nt(lhs, rhs)

    inner = lax.fori_loop(0, rows // DEEP, step, jnp.zeros((height, count), F32))
    rots = height // mask.shape[0]
    allowed = jnp.concatenate([mask[...]] * rots, axis=0) > 0
    s = jnp.where(allowed, (inner - norm[:, :1]) / noise[...], LOW)
    scaled[...] = s
    peak = jnp.max(s, axis=0, keepdims=True)
    total = jnp.sum(jnp.exp(s - peak), axis=0, keepdims=True)
    stats[0:1] = peak
    stats[1:2] = total
    stats[2:] = jnp.zeros((stats.shape[0] - 2, count), F32)


def score(plain, refs, norm, mask, noise):
    count = mask.shape[1]
    height = refs.shape[1]
    return pl.pallas_call(
        score_kernel,
        out_shape=(
            pinned((height, count), F32),
            pinned((8, count), F32),
        ),
        compiler_params=pltpu.CompilerParams(vmem_limit_bytes=8 * MIB),
        cost_estimate=cost(5),
        name="score",
    )(held(plain), held(refs), held(norm), held(mask), held(noise))


def weigh(scaled, mine, other, rot, out):
    rots, padded, _ = rot.shape
    count = scaled.shape[1]
    theirs = jnp.concatenate([other[:, count // 2 :], other[:, : count // 2]], axis=1)
    peak = jnp.maximum(mine[0:1], theirs[0:1])
    total = mine[1:2] * jnp.exp(mine[0:1] - peak) + theirs[1:2] * jnp.exp(theirs[0:1] - peak)
    w = (jnp.exp(scaled[...] - peak) / total).astype(BF16).astype(F32)
    quarters = []
    for q in range(4):
        acc = jnp.zeros((padded, count), F32)
        for j in range(rots):
            acc = acc + jnp.where(rot[j][:, :1] == q, w[j * padded : (j + 1) * padded], 0.0)
        quarters.append(acc)
    for row, pair in enumerate(((0, 3), (2, 1))):
        out[row] = jnp.concatenate([quarters[q] for q in pair], axis=1).astype(BF16)


def sums_kernel(plain, turned, *rest, first_call, outer, dom, start, rows, classes):
    if outer:
        weights = rest[0]
        outs = rest[-(dom // 2) :]
    elif first_call:
        weights = rest[-1]
        outs = rest[-3:-1]
        weigh(*rest[:4], weights)
    else:
        weights = rest[0]
        outs = rest[-2:]
    width = outs[0].shape[2]
    height = plain.shape[0]
    block = height // 2 // dom
    first = lax.axis_index("section") * (height // 2) + start
    own = lax.axis_index("dom")
    parity = own % 2
    straight = weights[0]
    mirrored = weights[1]
    flip = width - 1 - lax.broadcasted_iota(jnp.int32, (straight.shape[0], width), 1)

    def pair(g, sides, r):
        both = [first + (2 * g + side) * block + r for side in sides]
        direct = jnp.concatenate(
            [jnp.concatenate([plain[i], turned[height - 1 - i]], axis=0) for i in both], axis=1
        )
        mirror = jnp.concatenate(
            [jnp.concatenate([plain[height - 1 - i], turned[i]], axis=0) for i in both], axis=1
        )
        direct = nn(straight, direct)
        mirror = nn(mirrored, mirror)
        return [
            (
                direct[:, at : at + width]
                + jnp.take_along_axis(mirror[:, at : at + width], flip, axis=1)
            )[:classes]
            for at in (0, width)
        ]

    if outer:
        for m, out in enumerate(outs):
            for r in range(rows):
                for side, value in enumerate(pair(jnp.bitwise_xor(own // 2, m), (0, 1), r)):
                    out[side, r * classes : (r + 1) * classes] = value.astype(out.dtype)
    else:
        keep, send = outs

        @pl.loop(0, dom // 2)
        def _(g):
            for r in range(rows):
                away, here = pair(g, (1 - parity, parity), r)
                at = slice(r * classes, (r + 1) * classes)
                send[g, at] = away.astype(BF16)
                keep[g, at] = here


def sums(inputs, plain, turned, after, outer, dom, start, rows, classes):
    width = plain.shape[2]
    vmem = pl.BlockSpec(memory_space=pltpu.VMEM)
    count = 2 if outer else dom // 2
    shape = (count, rows * classes, width)
    out_shape = [pinned(shape, F32)]
    out_shape += [jax.ShapeDtypeStruct(shape, BF16)] * (dom // 2 - 1 if outer else 1)
    first_call = len(inputs) > 1
    if first_call:
        rot = inputs[3]
        out_shape.append(pinned((2, rot.shape[1], 2 * plain.shape[1]), BF16))
    return pl.pallas_call(
        functools.partial(
            sums_kernel, first_call=first_call, outer=outer, dom=dom, start=start, rows=rows, classes=classes
        ),
        in_specs=[vmem] * (2 + len(inputs)) + [pl.BlockSpec(memory_space=pl.ANY)] * len(after),
        out_shape=tuple(out_shape),
        compiler_params=pltpu.CompilerParams(vmem_limit_bytes=8 * MIB),
        cost_estimate=cost(SUMS * rows),
        name="sums",
    )(held(plain), held(turned), *inputs, *after)


def gather_kernel(keep, *rest, came):
    got = rest[:came]
    here, away = rest[-2:]
    parity = lax.axis_index("dom") % 2
    for out, side in ((here, parity), (away, 1 - parity)):
        value = keep[side]
        for other in got:
            value = value + other[side].astype(F32)
        out[0] = value.astype(out.dtype)


def gather(keep, got, after):
    shape = (1,) + keep.shape[1:]
    return pl.pallas_call(
        functools.partial(gather_kernel, came=len(got)),
        in_specs=[pl.BlockSpec(memory_space=pltpu.VMEM)] * (1 + len(got))
        + [pl.BlockSpec(memory_space=pl.ANY)] * len(after),
        out_shape=(pinned(shape, F32), jax.ShapeDtypeStruct(shape, BF16)),
        compiler_params=pltpu.CompilerParams(vmem_limit_bytes=8 * MIB),
        cost_estimate=cost(FOLD),
        name="gather",
    )(held(keep), *got, *after)


def fold_kernel(keep, got, *outs, fan, bit):
    outs = outs[-fan:]
    rest = keep.shape[0] // fan
    at = (lax.axis_index("dom") // (1 << bit)) % fan
    for m, out in enumerate(outs):
        for i in range(rest):
            b = i * fan + jnp.bitwise_xor(at, m)
            value = keep[b] + got[b].astype(F32)
            out[i] = value.astype(out.dtype)


def fold(keep, got, after, fan, bit):
    rest = (keep.shape[0] // fan,) + keep.shape[1:]
    return pl.pallas_call(
        functools.partial(fold_kernel, fan=fan, bit=bit),
        in_specs=[pl.BlockSpec(memory_space=pltpu.VMEM)] * 2
        + [pl.BlockSpec(memory_space=pl.ANY)] * len(after),
        out_shape=(pinned(rest, F32),) + (jax.ShapeDtypeStruct(rest, BF16),) * (fan - 1),
        compiler_params=pltpu.CompilerParams(vmem_limit_bytes=8 * MIB),
        cost_estimate=cost(FOLD),
        name="fold",
    )(held(keep), got, *after)


def finish_kernel(*args, counts, classes):
    out = args[-1]
    block_rows = sum(rows for rows, _ in counts)
    at = 0
    row = 0
    for rows, pieces in counts:
        for r in range(rows):
            cut = slice(r * classes, (r + 1) * classes)
            value = args[at][0, cut]
            for other in args[at + 1 : at + pieces]:
                value = value + other[0, cut].astype(F32)
            out[pl.ds(row, classes, stride=block_rows)] = value
            row += 1
        at += pieces


def finish(done, classes):
    counts = tuple((pieces[0].shape[1] // classes, len(pieces)) for pieces in done)
    width = done[0][0].shape[2]
    block_rows = sum(rows for rows, _ in counts)
    flat = [held(p) if i == 0 else p for pieces in done for i, p in enumerate(pieces)]
    out = pl.pallas_call(
        functools.partial(finish_kernel, counts=counts, classes=classes),
        out_shape=jax.ShapeDtypeStruct((classes * block_rows, width), F32),
        compiler_params=pltpu.CompilerParams(vmem_limit_bytes=8 * MIB),
        cost_estimate=cost(1),
        name="finish",
    )(*flat)
    return out.reshape(classes, block_rows, width)


def y_pieces(particles):
    last = GROUP
    middle = particles // 3 // GROUP * GROUP
    return ((particles - middle - last, GROUP), (middle, GROUP // 2), (last, last))


def row_pieces(rows, dom):
    if rows < 8 or dom > 8:
        return (rows,), 0
    part = rows * 3 // 8
    return (part, part), rows - 2 * part


def local(
    images, defocus_bin, ctf_kernels, band_kernel, references, rot_index, class_mask, noise_var
):
    dom = lax.axis_size("dom")
    particles, half, width = images.shape
    classes = rot_index.shape[0]
    padded = -(-classes // GROUP) * GROUP
    swap = [(0, 1), (1, 0)]
    over_cls = functools.partial(lax.ppermute, axis_name="cls", perm=swap)
    over_section = functools.partial(lax.ppermute, axis_name="section", perm=swap)

    sizes, steps = zip(*y_pieces(particles))
    starts = [sum(sizes[:i]) for i in range(len(sizes))]
    remote = [over_cls(images[a : a + n]) for a, n in zip(starts, sizes)]
    other_bins = over_cls(defocus_bin)
    own_sib = over_section(images)

    refs, norm = lay_refs(references, padded)
    left, right, mask, noise, rot = prepare(
        ctf_kernels, band_kernel, class_mask, noise_var, rot_index.T, norm, padded
    )
    total = 2 * particles
    *buffers, token = filter_chunk(
        defocus_bin, images, [own_sib], left, right, (), total, 0, 0, 1
    )
    chosen = pick(other_bins, left, right, token, starts[-1], sizes[-1])
    tokens = [chosen[0]]
    for i, a in enumerate(starts):
        piece = gate(remote[i], *tokens)
        step = steps[i]
        sibs = [over_section(piece[b : b + step]) for b in range(0, sizes[i], step)]
        last = i + 1 == len(starts)
        filters = (None, piece, sibs, *chosen) if last else (other_bins, piece, sibs, left, right)
        made = filter_chunk(*filters, buffers, total, a, particles + a, int(not last))
        buffers = made[:2]
        tokens = made[2:]
    plain, turned = buffers

    scaled, stats = score(plain, refs, norm, mask, noise)
    inputs = (held(scaled), held(stats), over_cls(stats), held(rot))

    def along(x, mask):
        return lax.ppermute(x, "dom", [(i, i ^ mask) for i in range(dom)])

    def spread(sends, bit):
        far_first = sorted(range(len(sends)), key=lambda m: m == 0)
        return [along(sends[m], (m + 1) << bit) for m in far_first]

    firsts, outer = row_pieces(half // dom, dom)
    start = 0
    weights = None
    after = ()
    parts = []
    for rows in firsts:
        args = inputs if weights is None else (held(weights),)
        keep, send, *made = sums(args, plain, turned, after, False, dom, start, rows, classes)
        weights = made[0] if made else weights
        start += rows
        after = (send,)
        parts.append((keep, along(send, 1)))
    got_b = []
    if outer:
        keep_b, *sends_b = sums(
            (held(weights),), plain, turned, after, True, dom, start, outer, classes
        )
        got_b = spread(sends_b, 1)
    done = []
    after = ()
    for keep, got in parts:
        bit = 1
        while keep.shape[0] > 4:
            keep, send = fold(keep, got, after, 2, bit)
            got = along(send, 1 << bit)
            bit += 1
        keep, *sends = fold(keep, got, after, keep.shape[0], bit)
        done.append([keep] + spread(sends, bit))
        after = tuple(got_b)
    if outer:
        keep_b, send_b = gather(keep_b, got_b, done[0][1:] if True else [])
        done.append([keep_b, along(send_b, 1)])
    return finish(done, classes)


def solution(mesh):
    return jax.shard_map(
        local,
        mesh=mesh,
        in_specs=(
            P(("dom", "cls"), "section", None),
            P(("dom", "cls")),
            P(),
            P(),
            P("cls", None, None, None),
            P("cls", None),
            P("dom", "cls"),
            P("dom"),
        ),
        out_specs=P("cls", ("section", "dom"), None),
        check_vma=False,
    )
```

```python
import functools

import jax
import jax.numpy as jnp
from jax import lax
from jax.experimental import pallas as pl
from jax.experimental.pallas import tpu as pltpu
from jax.sharding import PartitionSpec as P

F32 = jnp.float32
BF16 = jnp.bfloat16
LOW = -1e30
GROUP = 16
PAD = 8
DEEP = 128
SUMS = 0.8
SCALE = 0.1
FOLD = 1
MIB = 1 << 20


def nt(a, b, precision=None):
    return lax.dot_general(
        a, b, (((1,), (1,)), ((), ())), preferred_element_type=F32, precision=precision
    )


def nn(a, b):
    return lax.dot_general(a, b, (((1,), (0,)), ((), ())), preferred_element_type=F32)


def cost(microseconds):
    return pl.CostEstimate(
        flops=int(microseconds * SCALE * 1e9), transcendentals=0, bytes_accessed=int(microseconds * SCALE * 3e6)
    )


def pinned(shape, dtype):
    return pltpu.VMEM(shape, dtype)


def held(x):
    return pltpu.with_memory_space_constraint(x, pltpu.VMEM)


def prepare_kernel(ctf, band, mask, noise, rot, after, left, right, mask_out, noise_out, rot_out, scr):
    del after
    bins, width = ctf.shape
    rots, classes = rot.shape
    padded = rot_out.shape[1]
    total = mask.shape[0]
    count = total // 2

    def negated(v):
        at = (width - lax.broadcasted_iota(jnp.int32, v.shape, 1)) % width
        return jnp.take_along_axis(v, at, axis=1)

    def rolled(row):
        return pltpu.roll(jnp.broadcast_to(row, (width, width)), 0, 1, stride=1, stride_axis=0)

    def with_delta(v):
        return v + jnp.where(lax.broadcasted_iota(jnp.int32, v.shape, 1) == 0, 1.0, 0.0)

    highest = lax.Precision.HIGHEST
    kernels = with_delta(ctf[...])
    bands = with_delta(jnp.broadcast_to(band[...], (8, width)))
    forward = nt(kernels, rolled(negated(bands)[:1]), highest)
    backward = nt(negated(kernels), rolled(bands[:1]), highest)
    for b in range(bins):
        left[b] = rolled(backward[b : b + 1]).astype(BF16)
        right[b] = rolled(forward[b : b + 1]).astype(BF16)

    scr[...] = jnp.zeros_like(scr)
    group = lax.axis_index("cls")
    for half in range(2):
        come = group if half == 0 else 1 - group
        start = pl.multiple_of(come * count, 8)
        scr[half * count : (half + 1) * count, :classes] = mask[pl.ds(start, count)].astype(F32)
    mask_out[...] = scr[...].T[:padded, :total]
    n = noise[...]
    other = jnp.concatenate([n[:, count:], n[:, :count]], axis=1)
    noise_out[...] = jnp.where(group == 0, n, other)
    square = scr.shape[1]
    scr[:square] = jnp.zeros((square, square), F32)
    scr[:rots, :classes] = rot[...].astype(F32)
    turned = scr[:square].T
    for j in range(rots):
        rot_out[j] = jnp.broadcast_to(turned[:padded, j : j + 1], (padded, square))


def prepare(ctf, band, mask, noise, rot, after, padded):
    bins, width = ctf.shape
    total = noise.shape[0]
    lanes = max(128, -(-padded // 128) * 128)
    tall = -(-max(total, lanes) // 128) * 128
    return pl.pallas_call(
        prepare_kernel,
        out_shape=(
            pinned((bins, width, width), BF16),
            pinned((bins, width, width), BF16),
            pinned((padded, total), F32),
            pinned((1, total), F32),
            pinned((rot.shape[0], padded, lanes), F32),
        ),
        scratch_shapes=[pltpu.VMEM((tall, lanes), F32)],
        compiler_params=pltpu.CompilerParams(vmem_limit_bytes=4 * MIB),
        cost_estimate=cost(3),
        name="prepare",
    )(ctf, band.reshape(1, width), mask, noise.reshape(1, total), rot, held(after))


def cut_kernel(images, out, done):
    copy = pltpu.make_async_copy(images.at[pl.ds(0, out.shape[0])], out, done)
    copy.start()
    copy.wait()


def cut(images, count):
    return pl.pallas_call(
        cut_kernel,
        in_specs=[pl.BlockSpec(memory_space=pl.ANY)],
        out_specs=pl.BlockSpec(memory_space=pltpu.VMEM),
        out_shape=pinned((count,) + images.shape[1:], images.dtype),
        scratch_shapes=[pltpu.SemaphoreType.DMA(())],
        compiler_params=pltpu.CompilerParams(vmem_limit_bytes=2 * MIB),
        cost_estimate=cost(1),
        name="cut",
    )(pltpu.with_memory_space_constraint(images, pltpu.HBM))


def gate_kernel(*refs):
    del refs


def gate(piece, *tokens):
    anywhere = pl.BlockSpec(memory_space=pl.ANY)
    return pl.pallas_call(
        gate_kernel,
        in_specs=[anywhere] * (1 + len(tokens)),
        out_specs=anywhere,
        out_shape=jax.ShapeDtypeStruct(piece.shape, piece.dtype),
        input_output_aliases={0: 0},
        compiler_params=pltpu.CompilerParams(vmem_limit_bytes=MIB),
        cost_estimate=cost(0.1),
        name="gate",
    )(piece, *tokens)


def refs_kernel(refs, out, norm, scratch, *, padded):
    classes, _, rows, width = refs.shape
    pitch = rows + PAD
    j = pl.program_id(0)

    def block(start, count):
        for k in range(GROUP):
            if k < count:
                scratch[pl.ds(k * pitch, rows)] = refs[start + k, 0].astype(F32)
            else:
                scratch[pl.ds(k * pitch, rows)] = jnp.zeros((rows, width), F32)
        at = pl.multiple_of(j * padded + start, GROUP)

        def step(r, acc):
            v = scratch[pl.ds(r, GROUP, stride=pitch)]
            out[r, pl.ds(at, GROUP)] = v.astype(BF16)
            return acc + v * v

        acc = lax.fori_loop(0, rows, step, jnp.zeros((GROUP, width), F32), unroll=32)
        total = 0.5 * jnp.sum(acc, axis=1, keepdims=True)
        norm[pl.ds(at, GROUP)] = jnp.broadcast_to(total, (GROUP, width))

    full = classes // GROUP

    @pl.loop(0, full)
    def _(i):
        block(i * GROUP, GROUP)

    if classes % GROUP:
        block(full * GROUP, classes % GROUP)


def lay_refs(refs, padded):
    classes, rots, rows, width = refs.shape
    vmem = pl.BlockSpec(memory_space=pltpu.VMEM)
    return pl.pallas_call(
        functools.partial(refs_kernel, padded=padded),
        grid=(rots,),
        in_specs=[pl.BlockSpec((classes, 1, rows, width), lambda j: (0, j, 0, 0))],
        out_specs=(vmem, vmem),
        out_shape=(
            pinned((rows, rots * padded, width), BF16),
            pinned((rots * padded, width), F32),
        ),
        scratch_shapes=[pltpu.VMEM((GROUP * (rows + PAD), width), F32)],
        compiler_params=pltpu.CompilerParams(vmem_limit_bytes=12 * MIB),
        cost_estimate=cost(9),
        name="refs",
    )(pltpu.with_memory_space_constraint(refs, pltpu.HBM))


def filter_kernel(*args, picked, parts, skip, at, chained):
    bins = None if picked else args[0]
    mine, left, right, *rest = args[0 if picked else 1 :]
    sibs = rest[:parts]
    plain, turned, *token = rest[-6 - chained : -4]
    scratch = rest[-4:]
    for t in token:
        t[...] = jnp.zeros_like(t)
    width = mine.shape[2]
    top = lax.axis_index("section") == 0
    pitch = width + PAD

    def group(base, source, turn):
        scr, scr_t = scratch[2 * turn : 2 * turn + 2]
        for i in range(GROUP):
            b = base + i if picked else bins[skip + base + i]
            a = mine[base + i]
            o = source(i)
            x = jnp.concatenate([jnp.where(top, a, o), jnp.where(top, o, a)], axis=0)
            f = nn(left[b], nn(x, right[b]).astype(BF16))
            scr[pl.ds(i * pitch, width)] = f
            scr_t[pl.ds(i * pitch, width)] = f.T
        to = pl.multiple_of(at + base, GROUP)
        for r in range(width):
            plain[r, pl.ds(to, GROUP)] = scr[pl.ds(r, GROUP, stride=pitch)].astype(BF16)
            turned[r, pl.ds(to, GROUP)] = scr_t[pl.ds(r, GROUP, stride=pitch)].astype(BF16)

    groups = mine.shape[0] // GROUP
    if groups > 3:
        base = 0
        for sib in sibs:
            sib_groups = sib.shape[0] // GROUP

            @pl.loop(0, sib_groups)
            def _(g, sib=sib, base=base):
                at = pl.multiple_of(g * GROUP, GROUP)
                group(base + at, lambda i: sib[at + i], 0)

            base += sib.shape[0]
    else:
        places = [(sib, i) for sib in sibs for i in range(sib.shape[0])]
        for g in range(groups):

            def source(i, g=g):
                sib, place = places[g * GROUP + i]
                return sib[place]

            group(g * GROUP, source, g % 2)


def filter_chunk(bins, mine, sibs, left, right, buffers, total, skip, at, chained):
    count, half, width = mine.shape
    smem = pl.BlockSpec(memory_space=pltpu.SMEM)
    vmem = pl.BlockSpec(memory_space=pltpu.VMEM)
    parts = len(sibs)
    picked = bins is None
    head = [] if picked else [bins]
    return pl.pallas_call(
        functools.partial(
            filter_kernel, picked=picked, parts=parts, skip=skip, at=at, chained=chained
        ),
        in_specs=[smem] * len(head) + [vmem] * (3 + parts + len(buffers)),
        out_specs=(vmem,) * (2 + chained),
        out_shape=(pinned((2 * half, total, width), BF16),) * 2
        + (pinned((8, width), F32),) * chained,
        scratch_shapes=[pltpu.VMEM((GROUP * (2 * half + PAD), width), F32)] * 4,
        input_output_aliases={len(head) + 3 + parts + i: i for i in range(len(buffers))},
        compiler_params=pltpu.CompilerParams(vmem_limit_bytes=8 * MIB),
        cost_estimate=cost(count * 0.1),
        name="filter",
    )(*head, mine, held(left), held(right), *sibs, *[held(b) for b in buffers])


def pick_kernel(bins, left, right, after, left_out, right_out, *, skip):
    del after
    for i in range(left_out.shape[0]):
        left_out[i] = left[bins[skip + i]]
        right_out[i] = right[bins[skip + i]]


def pick(bins, left, right, after, skip, count):
    vmem = pl.BlockSpec(memory_space=pltpu.VMEM)
    return pl.pallas_call(
        functools.partial(pick_kernel, skip=skip),
        in_specs=[pl.BlockSpec(memory_space=pltpu.SMEM), vmem, vmem, vmem],
        out_shape=(pinned((count,) + left.shape[1:], BF16),) * 2,
        compiler_params=pltpu.CompilerParams(vmem_limit_bytes=4 * MIB),
        cost_estimate=cost(1),
        name="pick",
    )(bins, held(left), held(right), held(after))


def score_kernel(plain, refs, norm, mask, noise, scaled, stats):
    rows, height, width = refs.shape
    count = mask.shape[1]

    def step(i, acc):
        at = [DEEP * i + a for a in range(DEEP)]
        lhs = jnp.concatenate([refs[r] for r in at], axis=1)
        rhs = jnp.concatenate([plain[r] for r in at], axis=1)
        return acc + nt(lhs, rhs)

    inner = lax.fori_loop(0, rows // DEEP, step, jnp.zeros((height, count), F32))
    rots = height // mask.shape[0]
    allowed = jnp.concatenate([mask[...]] * rots, axis=0) > 0
    s = jnp.where(allowed, (inner - norm[:, :1]) / noise[...], LOW)
    scaled[...] = s
    peak = jnp.max(s, axis=0, keepdims=True)
    total = jnp.sum(jnp.exp(s - peak), axis=0, keepdims=True)
    stats[0:1] = peak
    stats[1:2] = total
    stats[2:] = jnp.zeros((stats.shape[0] - 2, count), F32)


def score(plain, refs, norm, mask, noise):
    count = mask.shape[1]
    height = refs.shape[1]
    return pl.pallas_call(
        score_kernel,
        out_shape=(
            pinned((height, count), F32),
            pinned((8, count), F32),
        ),
        compiler_params=pltpu.CompilerParams(vmem_limit_bytes=8 * MIB),
        cost_estimate=cost(5),
        name="score",
    )(held(plain), held(refs), held(norm), held(mask), held(noise))


def weigh(scaled, mine, other, rot, out):
    rots, padded, _ = rot.shape
    count = scaled.shape[1]
    theirs = jnp.concatenate([other[:, count // 2 :], other[:, : count // 2]], axis=1)
    peak = jnp.maximum(mine[0:1], theirs[0:1])
    total = mine[1:2] * jnp.exp(mine[0:1] - peak) + theirs[1:2] * jnp.exp(theirs[0:1] - peak)
    w = (jnp.exp(scaled[...] - peak) / total).astype(BF16).astype(F32)
    quarters = []
    for q in range(4):
        acc = jnp.zeros((padded, count), F32)
        for j in range(rots):
            acc = acc + jnp.where(rot[j][:, :1] == q, w[j * padded : (j + 1) * padded], 0.0)
        quarters.append(acc)
    for row, pair in enumerate(((0, 3), (2, 1))):
        out[row] = jnp.concatenate([quarters[q] for q in pair], axis=1).astype(BF16)


def sums_kernel(plain, turned, *rest, outer, dom, start, rows, classes):
    if outer:
        weights = rest[0]
        outs = rest[-(dom // 2) :]
    else:
        weights = rest[-1]
        outs = rest[-3:-1]
        weigh(*rest[:4], weights)
    width = outs[0].shape[2]
    height = plain.shape[0]
    block = height // 2 // dom
    first = lax.axis_index("section") * (height // 2) + start
    own = lax.axis_index("dom")
    parity = own % 2
    straight = weights[0]
    mirrored = weights[1]
    flip = width - 1 - lax.broadcasted_iota(jnp.int32, (straight.shape[0], width), 1)

    def pair(g, sides, r):
        both = [first + (2 * g + side) * block + r for side in sides]
        direct = jnp.concatenate(
            [jnp.concatenate([plain[i], turned[height - 1 - i]], axis=0) for i in both], axis=1
        )
        mirror = jnp.concatenate(
            [jnp.concatenate([plain[height - 1 - i], turned[i]], axis=0) for i in both], axis=1
        )
        direct = nn(straight, direct)
        mirror = nn(mirrored, mirror)
        return [
            (
                direct[:, at : at + width]
                + jnp.take_along_axis(mirror[:, at : at + width], flip, axis=1)
            )[:classes]
            for at in (0, width)
        ]

    if outer:
        for m, out in enumerate(outs):
            for r in range(rows):
                for side, value in enumerate(pair(jnp.bitwise_xor(own // 2, m), (0, 1), r)):
                    out[side, r * classes : (r + 1) * classes] = value.astype(out.dtype)
    else:
        keep, send = outs

        @pl.loop(0, dom // 2)
        def _(g):
            for r in range(rows):
                away, here = pair(g, (1 - parity, parity), r)
                at = slice(r * classes, (r + 1) * classes)
                send[g, at] = away.astype(BF16)
                keep[g, at] = here


def sums(inputs, plain, turned, after, outer, dom, start, rows, classes):
    width = plain.shape[2]
    vmem = pl.BlockSpec(memory_space=pltpu.VMEM)
    count = 2 if outer else dom // 2
    shape = (count, rows * classes, width)
    out_shape = [pinned(shape, F32)]
    out_shape += [jax.ShapeDtypeStruct(shape, BF16)] * (dom // 2 - 1 if outer else 1)
    if not outer:
        rot = inputs[3]
        out_shape.append(pinned((2, rot.shape[1], 2 * plain.shape[1]), BF16))
    return pl.pallas_call(
        functools.partial(
            sums_kernel, outer=outer, dom=dom, start=start, rows=rows, classes=classes
        ),
        in_specs=[vmem] * (2 + len(inputs)) + [pl.BlockSpec(memory_space=pl.ANY)] * len(after),
        out_shape=tuple(out_shape),
        compiler_params=pltpu.CompilerParams(vmem_limit_bytes=8 * MIB),
        cost_estimate=cost(SUMS * rows),
        name="sums",
    )(held(plain), held(turned), *inputs, *after)


def gather_kernel(keep, *rest, came):
    got = rest[:came]
    here, away = rest[-2:]
    parity = lax.axis_index("dom") % 2
    for out, side in ((here, parity), (away, 1 - parity)):
        value = keep[side]
        for other in got:
            value = value + other[side].astype(F32)
        out[0] = value.astype(out.dtype)


def gather(keep, got):
    shape = (1,) + keep.shape[1:]
    return pl.pallas_call(
        functools.partial(gather_kernel, came=len(got)),
        out_shape=(pinned(shape, F32), jax.ShapeDtypeStruct(shape, BF16)),
        compiler_params=pltpu.CompilerParams(vmem_limit_bytes=8 * MIB),
        cost_estimate=cost(FOLD),
        name="gather",
    )(held(keep), *got)


def fold_kernel(keep, got, *outs, fan, bit):
    outs = outs[-fan:]
    rest = keep.shape[0] // fan
    at = (lax.axis_index("dom") // (1 << bit)) % fan
    for m, out in enumerate(outs):
        for i in range(rest):
            b = i * fan + jnp.bitwise_xor(at, m)
            value = keep[b] + got[b].astype(F32)
            out[i] = value.astype(out.dtype)


def fold(keep, got, after, fan, bit):
    rest = (keep.shape[0] // fan,) + keep.shape[1:]
    return pl.pallas_call(
        functools.partial(fold_kernel, fan=fan, bit=bit),
        in_specs=[pl.BlockSpec(memory_space=pltpu.VMEM)] * 2
        + [pl.BlockSpec(memory_space=pl.ANY)] * len(after),
        out_shape=(pinned(rest, F32),) + (jax.ShapeDtypeStruct(rest, BF16),) * (fan - 1),
        compiler_params=pltpu.CompilerParams(vmem_limit_bytes=8 * MIB),
        cost_estimate=cost(FOLD),
        name="fold",
    )(held(keep), got, *after)


def finish_kernel(*args, counts, classes):
    out = args[-1]
    block_rows = sum(rows for rows, _ in counts)
    at = 0
    row = 0
    for rows, pieces in counts:
        for r in range(rows):
            cut = slice(r * classes, (r + 1) * classes)
            value = args[at][0, cut]
            for other in args[at + 1 : at + pieces]:
                value = value + other[0, cut].astype(F32)
            out[pl.ds(row, classes, stride=block_rows)] = value
            row += 1
        at += pieces


def finish(done, classes):
    counts = tuple((pieces[0].shape[1] // classes, len(pieces)) for pieces in done)
    width = done[0][0].shape[2]
    block_rows = sum(rows for rows, _ in counts)
    flat = [held(p) if i == 0 else p for pieces in done for i, p in enumerate(pieces)]
    out = pl.pallas_call(
        functools.partial(finish_kernel, counts=counts, classes=classes),
        out_shape=jax.ShapeDtypeStruct((classes * block_rows, width), F32),
        compiler_params=pltpu.CompilerParams(vmem_limit_bytes=8 * MIB),
        cost_estimate=cost(1),
        name="finish",
    )(*flat)
    return out.reshape(classes, block_rows, width)


def y_pieces(particles):
    last = GROUP
    middle = particles // 3 // GROUP * GROUP
    return ((particles - middle - last, GROUP), (middle, GROUP // 2), (last, last))


def row_pieces(rows, dom):
    if rows < 4 or dom > 8:
        return (rows, 0)
    outer = rows * 3 // 8
    return (rows - outer, outer)


def local(
    images, defocus_bin, ctf_kernels, band_kernel, references, rot_index, class_mask, noise_var
):
    dom = lax.axis_size("dom")
    particles, half, width = images.shape
    classes = rot_index.shape[0]
    padded = -(-classes // GROUP) * GROUP
    swap = [(0, 1), (1, 0)]
    over_cls = functools.partial(lax.ppermute, axis_name="cls", perm=swap)
    over_section = functools.partial(lax.ppermute, axis_name="section", perm=swap)

    sizes, steps = zip(*y_pieces(particles))
    starts = [sum(sizes[:i]) for i in range(len(sizes))]
    slices = [images[a : a + n] for a, n in zip(starts, sizes)]
    slices[0] = cut(images, sizes[0])
    remote = [over_cls(x) for x in slices]
    other_bins = over_cls(defocus_bin)
    own_sibs = [over_section(images)]

    refs, norm = lay_refs(references, padded)
    left, right, mask, noise, rot = prepare(
        ctf_kernels, band_kernel, class_mask, noise_var, rot_index.T, norm, padded
    )
    total = 2 * particles
    *buffers, token = filter_chunk(
        defocus_bin, images, own_sibs, left, right, (), total, 0, 0, 1
    )
    chosen = pick(other_bins, left, right, token, starts[-1], sizes[-1])
    tokens = [chosen[0]]
    for i, a in enumerate(starts):
        piece = gate(remote[i], *tokens)
        step = steps[i]
        sibs = [over_section(piece[b : b + step]) for b in range(0, sizes[i], step)]
        last = i + 1 == len(starts)
        filters = (None, piece, sibs, *chosen) if last else (other_bins, piece, sibs, left, right)
        made = filter_chunk(*filters, buffers, total, a, particles + a, int(not last))
        buffers = made[:2]
        tokens = made[2:]
    plain, turned = buffers

    scaled, stats = score(plain, refs, norm, mask, noise)
    inputs = (held(scaled), held(stats), over_cls(stats), held(rot))

    def along(x, mask):
        return lax.ppermute(x, "dom", [(i, i ^ mask) for i in range(dom)])

    def spread(sends, bit):
        far_first = sorted(range(len(sends)), key=lambda m: m == 0)
        return [along(sends[m], (m + 1) << bit) for m in far_first]

    inner, outer = row_pieces(half // dom, dom)
    keep, send, weights = sums(inputs, plain, turned, (), False, dom, 0, inner, classes)
    got = along(send, 1)
    if outer:
        keep_b, *sends_b = sums(
            (held(weights),), plain, turned, (send,), True, dom, inner, outer, classes
        )
        got_b = spread(sends_b, 1)
    bit = 1
    while keep.shape[0] > 4:
        keep, send = fold(keep, got, (), 2, bit)
        got = along(send, 1 << bit)
        bit += 1
    keep, *sends = fold(keep, got, (), keep.shape[0], bit)
    done = [[keep] + spread(sends, bit)]
    if outer:
        keep_b, send_b = gather(keep_b, got_b)
        done.append([keep_b, along(send_b, 1)])
    return finish(done, classes)


def solution(mesh):
    return jax.shard_map(
        local,
        mesh=mesh,
        in_specs=(
            P(("dom", "cls"), "section", None),
            P(("dom", "cls")),
            P(),
            P(),
            P("cls", None, None, None),
            P("cls", None),
            P("dom", "cls"),
            P("dom"),
        ),
        out_specs=P("cls", ("section", "dom"), None),
        check_vma=False,
    )
```

```python
import functools

import jax
import jax.numpy as jnp
from jax import lax
from jax.experimental import pallas as pl
from jax.experimental.pallas import tpu as pltpu
from jax.sharding import PartitionSpec as P

F32 = jnp.float32
BF16 = jnp.bfloat16
LOW = -1e30
GROUP = 16
PAD = 8
DEEP = 128
SUMS = 0.8
SCALE = 0.1
FOLD = 1
MIB = 1 << 20


def nt(a, b, precision=None):
    return lax.dot_general(
        a, b, (((1,), (1,)), ((), ())), preferred_element_type=F32, precision=precision
    )


def nn(a, b):
    return lax.dot_general(a, b, (((1,), (0,)), ((), ())), preferred_element_type=F32)


def cost(microseconds):
    return pl.CostEstimate(
        flops=int(microseconds * SCALE * 1e9), transcendentals=0, bytes_accessed=int(microseconds * SCALE * 3e6)
    )


def pinned(shape, dtype):
    return pltpu.VMEM(shape, dtype)


def held(x):
    return pltpu.with_memory_space_constraint(x, pltpu.VMEM)


def prepare_kernel(ctf, band, mask, noise, rot, after, left, right, mask_out, noise_out, rot_out, scr):
    del after
    bins, width = ctf.shape
    rots, classes = rot.shape
    padded = rot_out.shape[1]
    total = mask.shape[0]
    count = total // 2

    def negated(v):
        at = (width - lax.broadcasted_iota(jnp.int32, v.shape, 1)) % width
        return jnp.take_along_axis(v, at, axis=1)

    def rolled(row):
        return pltpu.roll(jnp.broadcast_to(row, (width, width)), 0, 1, stride=1, stride_axis=0)

    def with_delta(v):
        return v + jnp.where(lax.broadcasted_iota(jnp.int32, v.shape, 1) == 0, 1.0, 0.0)

    highest = lax.Precision.HIGHEST
    kernels = with_delta(ctf[...])
    bands = with_delta(jnp.broadcast_to(band[...], (8, width)))
    forward = nt(kernels, rolled(negated(bands)[:1]), highest)
    backward = nt(negated(kernels), rolled(bands[:1]), highest)
    for b in range(bins):
        left[b] = rolled(backward[b : b + 1]).astype(BF16)
        right[b] = rolled(forward[b : b + 1]).astype(BF16)

    scr[...] = jnp.zeros_like(scr)
    group = lax.axis_index("cls")
    for half in range(2):
        come = group if half == 0 else 1 - group
        start = pl.multiple_of(come * count, 8)
        scr[half * count : (half + 1) * count, :classes] = mask[pl.ds(start, count)].astype(F32)
    mask_out[...] = scr[...].T[:padded, :total]
    n = noise[...]
    other = jnp.concatenate([n[:, count:], n[:, :count]], axis=1)
    noise_out[...] = jnp.where(group == 0, n, other)
    square = scr.shape[1]
    scr[:square] = jnp.zeros((square, square), F32)
    scr[:rots, :classes] = rot[...].astype(F32)
    turned = scr[:square].T
    for j in range(rots):
        rot_out[j] = jnp.broadcast_to(turned[:padded, j : j + 1], (padded, square))


def prepare(ctf, band, mask, noise, rot, after, padded):
    bins, width = ctf.shape
    total = noise.shape[0]
    lanes = max(128, -(-padded // 128) * 128)
    tall = -(-max(total, lanes) // 128) * 128
    return pl.pallas_call(
        prepare_kernel,
        out_shape=(
            pinned((bins, width, width), BF16),
            pinned((bins, width, width), BF16),
            pinned((padded, total), F32),
            pinned((1, total), F32),
            pinned((rot.shape[0], padded, lanes), F32),
        ),
        scratch_shapes=[pltpu.VMEM((tall, lanes), F32)],
        compiler_params=pltpu.CompilerParams(vmem_limit_bytes=4 * MIB),
        cost_estimate=cost(3),
        name="prepare",
    )(ctf, band.reshape(1, width), mask, noise.reshape(1, total), rot, held(after))


def gate_kernel(*refs):
    del refs


def gate(piece, *tokens):
    anywhere = pl.BlockSpec(memory_space=pl.ANY)
    return pl.pallas_call(
        gate_kernel,
        in_specs=[anywhere] * (1 + len(tokens)),
        out_specs=anywhere,
        out_shape=jax.ShapeDtypeStruct(piece.shape, piece.dtype),
        input_output_aliases={0: 0},
        compiler_params=pltpu.CompilerParams(vmem_limit_bytes=MIB),
        cost_estimate=cost(0.1),
        name="gate",
    )(piece, *tokens)


def refs_kernel(refs, out, norm, scratch, *, padded):
    classes, _, rows, width = refs.shape
    pitch = rows + PAD
    j = pl.program_id(0)

    def block(start, count):
        for k in range(GROUP):
            if k < count:
                scratch[pl.ds(k * pitch, rows)] = refs[start + k, 0].astype(F32)
            else:
                scratch[pl.ds(k * pitch, rows)] = jnp.zeros((rows, width), F32)
        at = pl.multiple_of(j * padded + start, GROUP)

        def step(r, acc):
            v = scratch[pl.ds(r, GROUP, stride=pitch)]
            out[r, pl.ds(at, GROUP)] = v.astype(BF16)
            return acc + v * v

        acc = lax.fori_loop(0, rows, step, jnp.zeros((GROUP, width), F32), unroll=32)
        total = 0.5 * jnp.sum(acc, axis=1, keepdims=True)
        norm[pl.ds(at, GROUP)] = jnp.broadcast_to(total, (GROUP, width))

    full = classes // GROUP

    @pl.loop(0, full)
    def _(i):
        block(i * GROUP, GROUP)

    if classes % GROUP:
        block(full * GROUP, classes % GROUP)


def lay_refs(refs, padded):
    classes, rots, rows, width = refs.shape
    vmem = pl.BlockSpec(memory_space=pltpu.VMEM)
    return pl.pallas_call(
        functools.partial(refs_kernel, padded=padded),
        grid=(rots,),
        in_specs=[pl.BlockSpec((classes, 1, rows, width), lambda j: (0, j, 0, 0))],
        out_specs=(vmem, vmem),
        out_shape=(
            pinned((rows, rots * padded, width), BF16),
            pinned((rots * padded, width), F32),
        ),
        scratch_shapes=[pltpu.VMEM((GROUP * (rows + PAD), width), F32)],
        compiler_params=pltpu.CompilerParams(vmem_limit_bytes=12 * MIB),
        cost_estimate=cost(9),
        name="refs",
    )(pltpu.with_memory_space_constraint(refs, pltpu.HBM))


def filter_kernel(*args, picked, parts, skip, at, chained):
    bins = None if picked else args[0]
    mine, left, right, *rest = args[0 if picked else 1 :]
    sibs = rest[:parts]
    plain, turned, *token = rest[-6 - chained : -4]
    scratch = rest[-4:]
    for t in token:
        t[...] = jnp.zeros_like(t)
    width = mine.shape[2]
    top = lax.axis_index("section") == 0
    pitch = width + PAD

    def group(base, source, turn):
        scr, scr_t = scratch[2 * turn : 2 * turn + 2]
        for i in range(GROUP):
            b = base + i if picked else bins[skip + base + i]
            a = mine[base + i]
            o = source(i)
            x = jnp.concatenate([jnp.where(top, a, o), jnp.where(top, o, a)], axis=0)
            f = nn(left[b], nn(x, right[b]).astype(BF16))
            scr[pl.ds(i * pitch, width)] = f
            scr_t[pl.ds(i * pitch, width)] = f.T
        to = pl.multiple_of(at + base, GROUP)
        for r in range(width):
            plain[r, pl.ds(to, GROUP)] = scr[pl.ds(r, GROUP, stride=pitch)].astype(BF16)
            turned[r, pl.ds(to, GROUP)] = scr_t[pl.ds(r, GROUP, stride=pitch)].astype(BF16)

    groups = mine.shape[0] // GROUP
    if parts > 1 or groups <= 2:
        places = [(sib, i) for sib in sibs for i in range(sib.shape[0])]
        for g in range(groups):

            def source(i, g=g):
                sib, place = places[g * GROUP + i]
                return sib[place]

            group(g * GROUP, source, g % 2)
    else:

        @pl.loop(0, groups)
        def _(g):
            base = pl.multiple_of(g * GROUP, GROUP)
            group(base, lambda i: sibs[0][base + i], 0)


def filter_chunk(bins, mine, sibs, left, right, buffers, total, skip, at, chained):
    count, half, width = mine.shape
    smem = pl.BlockSpec(memory_space=pltpu.SMEM)
    vmem = pl.BlockSpec(memory_space=pltpu.VMEM)
    parts = len(sibs)
    picked = bins is None
    head = [] if picked else [bins]
    return pl.pallas_call(
        functools.partial(
            filter_kernel, picked=picked, parts=parts, skip=skip, at=at, chained=chained
        ),
        in_specs=[smem] * len(head) + [vmem] * (3 + parts + len(buffers)),
        out_specs=(vmem,) * (2 + chained),
        out_shape=(pinned((2 * half, total, width), BF16),) * 2
        + (pinned((8, width), F32),) * chained,
        scratch_shapes=[pltpu.VMEM((GROUP * (2 * half + PAD), width), F32)] * 4,
        input_output_aliases={len(head) + 3 + parts + i: i for i in range(len(buffers))},
        compiler_params=pltpu.CompilerParams(vmem_limit_bytes=8 * MIB),
        cost_estimate=cost(count * 0.1),
        name="filter",
    )(*head, mine, held(left), held(right), *sibs, *[held(b) for b in buffers])


def pick_kernel(bins, left, right, after, left_out, right_out, *, skip):
    del after
    for i in range(left_out.shape[0]):
        left_out[i] = left[bins[skip + i]]
        right_out[i] = right[bins[skip + i]]


def pick(bins, left, right, after, skip, count):
    vmem = pl.BlockSpec(memory_space=pltpu.VMEM)
    return pl.pallas_call(
        functools.partial(pick_kernel, skip=skip),
        in_specs=[pl.BlockSpec(memory_space=pltpu.SMEM), vmem, vmem, vmem],
        out_shape=(pinned((count,) + left.shape[1:], BF16),) * 2,
        compiler_params=pltpu.CompilerParams(vmem_limit_bytes=4 * MIB),
        cost_estimate=cost(1),
        name="pick",
    )(bins, held(left), held(right), held(after))


def score_kernel(plain, refs, norm, mask, noise, scaled, stats):
    rows, height, width = refs.shape
    count = mask.shape[1]

    def step(i, acc):
        at = [DEEP * i + a for a in range(DEEP)]
        lhs = jnp.concatenate([refs[r] for r in at], axis=1)
        rhs = jnp.concatenate([plain[r] for r in at], axis=1)
        return acc + nt(lhs, rhs)

    inner = lax.fori_loop(0, rows // DEEP, step, jnp.zeros((height, count), F32))
    rots = height // mask.shape[0]
    allowed = jnp.concatenate([mask[...]] * rots, axis=0) > 0
    s = jnp.where(allowed, (inner - norm[:, :1]) / noise[...], LOW)
    scaled[...] = s
    peak = jnp.max(s, axis=0, keepdims=True)
    total = jnp.sum(jnp.exp(s - peak), axis=0, keepdims=True)
    stats[0:1] = peak
    stats[1:2] = total
    stats[2:] = jnp.zeros((stats.shape[0] - 2, count), F32)


def score(plain, refs, norm, mask, noise):
    count = mask.shape[1]
    height = refs.shape[1]
    return pl.pallas_call(
        score_kernel,
        out_shape=(
            pinned((height, count), F32),
            pinned((8, count), F32),
        ),
        compiler_params=pltpu.CompilerParams(vmem_limit_bytes=8 * MIB),
        cost_estimate=cost(5),
        name="score",
    )(held(plain), held(refs), held(norm), held(mask), held(noise))


def weigh(scaled, mine, other, rot, out):
    rots, padded, _ = rot.shape
    count = scaled.shape[1]
    theirs = jnp.concatenate([other[:, count // 2 :], other[:, : count // 2]], axis=1)
    peak = jnp.maximum(mine[0:1], theirs[0:1])
    total = mine[1:2] * jnp.exp(mine[0:1] - peak) + theirs[1:2] * jnp.exp(theirs[0:1] - peak)
    w = (jnp.exp(scaled[...] - peak) / total).astype(BF16).astype(F32)
    quarters = []
    for q in range(4):
        acc = jnp.zeros((padded, count), F32)
        for j in range(rots):
            acc = acc + jnp.where(rot[j][:, :1] == q, w[j * padded : (j + 1) * padded], 0.0)
        quarters.append(acc)
    for row, pair in enumerate(((0, 3), (2, 1))):
        out[row] = jnp.concatenate([quarters[q] for q in pair], axis=1).astype(BF16)


def row_pair(weights, plain, turned, both, classes):
    height, _, width = plain.shape
    direct = jnp.concatenate(
        [jnp.concatenate([plain[i], turned[height - 1 - i]], axis=0) for i in both], axis=1
    )
    mirror = jnp.concatenate(
        [jnp.concatenate([plain[height - 1 - i], turned[i]], axis=0) for i in both], axis=1
    )
    direct = nn(weights[0], direct)
    mirror = nn(weights[1], mirror)
    padded = weights.shape[1]
    flip = width - 1 - lax.broadcasted_iota(jnp.int32, (padded, width), 1)
    return [
        (
            direct[:, at : at + width]
            + jnp.take_along_axis(mirror[:, at : at + width], flip, axis=1)
        )[:classes]
        for at in (0, width)
    ]


def row_place(plain, dom, start):
    half = plain.shape[0] // 2
    first = lax.axis_index("section") * half + start
    return lambda block, r: first + block * (half // dom) + r


def one_side(weights, plain, turned, out, side, dom, start, rows, classes):
    place = row_place(plain, dom, start)
    count = dom // 2

    def pair(g, h):
        for r in range(rows):
            both = [place(2 * k + side, r) for k in (g, h)]
            for k, value in zip((g, h), row_pair(weights, plain, turned, both, classes)):
                out[k, r * classes : (r + 1) * classes] = value.astype(out.dtype)

    if count == 1:
        pair(0, 0)
    else:

        @pl.loop(0, count // 2)
        def _(g):
            pair(2 * g, 2 * g + 1)


def both_sides(weights, plain, turned, out, z, dom, start, rows, classes):
    place = row_place(plain, dom, start)
    for r in range(rows):
        both = [place(2 * z + side, r) for side in range(2)]
        for side, value in enumerate(row_pair(weights, plain, turned, both, classes)):
            out[side, r * classes : (r + 1) * classes] = value.astype(out.dtype)


def inner_kernel(scaled, mine, other, rot, plain, turned, send, weights, *, dom, **sizes):
    weigh(scaled, mine, other, rot, weights)
    away = 1 - lax.axis_index("dom") % 2
    one_side(weights, plain, turned, send, away, dom, **sizes)


def outer_kernel(weights, plain, turned, after, *outs, dom, **sizes):
    del after
    z = lax.axis_index("dom") // 2
    for m, out in enumerate(outs):
        both_sides(weights, plain, turned, out, jnp.bitwise_xor(z, m + 1), dom, **sizes)


def keep_kernel(weights, plain, turned, after, *outs, dom, classes, inner, outer):
    del after
    own = lax.axis_index("dom")
    one_side(weights, plain, turned, outs[0], own % 2, dom, 0, inner, classes)
    if outer:
        both_sides(weights, plain, turned, outs[1], own // 2, dom, inner, outer, classes)


def call_sums(kernel, args, after, out_shape, rows):
    vmem = pl.BlockSpec(memory_space=pltpu.VMEM)
    return pl.pallas_call(
        kernel,
        in_specs=[vmem] * len(args) + [pl.BlockSpec(memory_space=pl.ANY)] * len(after),
        out_shape=out_shape,
        compiler_params=pltpu.CompilerParams(vmem_limit_bytes=8 * MIB),
        cost_estimate=cost(SUMS * rows),
        name="sums",
    )(*args, *after)


def gather_kernel(keep, *rest, came):
    got = rest[:came]
    here, away = rest[-2:]
    parity = lax.axis_index("dom") % 2
    for out, side in ((here, parity), (away, 1 - parity)):
        value = keep[side]
        for other in got:
            value = value + other[side].astype(F32)
        out[0] = value.astype(out.dtype)


def gather(keep, got):
    shape = (1,) + keep.shape[1:]
    return pl.pallas_call(
        functools.partial(gather_kernel, came=len(got)),
        out_shape=(pinned(shape, F32), jax.ShapeDtypeStruct(shape, BF16)),
        compiler_params=pltpu.CompilerParams(vmem_limit_bytes=8 * MIB),
        cost_estimate=cost(FOLD),
        name="gather",
    )(held(keep), *got)


def fold_kernel(keep, got, *outs, fan, bit):
    outs = outs[-fan:]
    rest = keep.shape[0] // fan
    at = (lax.axis_index("dom") // (1 << bit)) % fan
    for m, out in enumerate(outs):
        for i in range(rest):
            b = i * fan + jnp.bitwise_xor(at, m)
            value = keep[b] + got[b].astype(F32)
            out[i] = value.astype(out.dtype)


def fold(keep, got, after, fan, bit):
    rest = (keep.shape[0] // fan,) + keep.shape[1:]
    return pl.pallas_call(
        functools.partial(fold_kernel, fan=fan, bit=bit),
        in_specs=[pl.BlockSpec(memory_space=pltpu.VMEM)] * 2
        + [pl.BlockSpec(memory_space=pl.ANY)] * len(after),
        out_shape=(pinned(rest, F32),) + (jax.ShapeDtypeStruct(rest, BF16),) * (fan - 1),
        compiler_params=pltpu.CompilerParams(vmem_limit_bytes=8 * MIB),
        cost_estimate=cost(FOLD),
        name="fold",
    )(held(keep), got, *after)


def finish_kernel(*args, counts, classes):
    out = args[-1]
    block_rows = sum(rows for rows, _ in counts)
    at = 0
    row = 0
    for rows, pieces in counts:
        for r in range(rows):
            cut = slice(r * classes, (r + 1) * classes)
            value = args[at][0, cut]
            for other in args[at + 1 : at + pieces]:
                value = value + other[0, cut].astype(F32)
            out[pl.ds(row, classes, stride=block_rows)] = value
            row += 1
        at += pieces


def finish(done, classes):
    counts = tuple((pieces[0].shape[1] // classes, len(pieces)) for pieces in done)
    width = done[0][0].shape[2]
    block_rows = sum(rows for rows, _ in counts)
    flat = [held(p) if i == 0 else p for pieces in done for i, p in enumerate(pieces)]
    out = pl.pallas_call(
        functools.partial(finish_kernel, counts=counts, classes=classes),
        out_shape=jax.ShapeDtypeStruct((classes * block_rows, width), F32),
        compiler_params=pltpu.CompilerParams(vmem_limit_bytes=8 * MIB),
        cost_estimate=cost(1),
        name="finish",
    )(*flat)
    return out.reshape(classes, block_rows, width)


def y_pieces(particles):
    last = GROUP
    middle = particles // 3 // GROUP * GROUP
    return ((particles - middle - last, GROUP), (middle, GROUP // 2), (last, last))


def row_pieces(rows, dom):
    if rows < 4 or dom > 8:
        return (rows, 0)
    outer = rows * 3 // 8
    return (rows - outer, outer)


def local(
    images, defocus_bin, ctf_kernels, band_kernel, references, rot_index, class_mask, noise_var
):
    dom = lax.axis_size("dom")
    particles, half, width = images.shape
    classes = rot_index.shape[0]
    padded = -(-classes // GROUP) * GROUP
    swap = [(0, 1), (1, 0)]
    over_cls = functools.partial(lax.ppermute, axis_name="cls", perm=swap)
    over_section = functools.partial(lax.ppermute, axis_name="section", perm=swap)

    sizes, steps = zip(*y_pieces(particles))
    starts = [sum(sizes[:i]) for i in range(len(sizes))]
    remote = [over_cls(images[a : a + n]) for a, n in zip(starts, sizes)]
    other_bins = over_cls(defocus_bin)
    own_sib = over_section(images)

    refs, norm = lay_refs(references, padded)
    left, right, mask, noise, rot = prepare(
        ctf_kernels, band_kernel, class_mask, noise_var, rot_index.T, norm, padded
    )
    total = 2 * particles
    *buffers, token = filter_chunk(
        defocus_bin, images, [own_sib], left, right, (), total, 0, 0, 1
    )
    chosen = pick(other_bins, left, right, token, starts[-1], sizes[-1])
    tokens = [chosen[0]]
    for i, a in enumerate(starts):
        piece = gate(remote[i], *tokens)
        step = steps[i]
        sibs = [over_section(piece[b : b + step]) for b in range(0, sizes[i], step)]
        last = i + 1 == len(starts)
        filters = (None, piece, sibs, *chosen) if last else (other_bins, piece, sibs, left, right)
        made = filter_chunk(*filters, buffers, total, a, particles + a, int(not last))
        buffers = made[:2]
        tokens = made[2:]
    plain, turned = buffers

    scaled, stats = score(plain, refs, norm, mask, noise)
    inputs = (held(scaled), held(stats), over_cls(stats), held(rot))

    def along(x, mask):
        return lax.ppermute(x, "dom", [(i, i ^ mask) for i in range(dom)])

    def spread(sends, bit):
        far_first = sorted(range(len(sends)), key=lambda m: m == 0)
        return [along(sends[m], (m + 1) << bit) for m in far_first]

    inner, outer = row_pieces(half // dom, dom)
    images_in = (held(plain), held(turned))
    count = dom // 2
    send, weights = call_sums(
        functools.partial(
            inner_kernel, dom=dom, start=0, rows=inner, classes=classes
        ),
        inputs + images_in,
        (),
        (
            jax.ShapeDtypeStruct((count, inner * classes, width), BF16),
            pinned((2, rot.shape[1], 2 * total), BF16),
        ),
        inner,
    )
    got = along(send, 1)
    weighted = (held(weights),) + images_in
    keep_shape = (pinned((count, inner * classes, width), F32),)
    after = send
    if outer:
        shape = (2, outer * classes, width)
        sends_b = call_sums(
            functools.partial(
                outer_kernel, dom=dom, start=inner, rows=outer, classes=classes
            ),
            weighted,
            (send,),
            (jax.ShapeDtypeStruct(shape, BF16),) * (count - 1),
            outer,
        )
        got_b = spread(sends_b, 1)
        keep_shape += (pinned(shape, F32),)
        after = sends_b[0]
    keep, *keep_b = call_sums(
        functools.partial(keep_kernel, dom=dom, classes=classes, inner=inner, outer=outer),
        weighted,
        (after,),
        keep_shape,
        inner,
    )
    bit = 1
    while keep.shape[0] > 4:
        keep, send = fold(keep, got, (), 2, bit)
        got = along(send, 1 << bit)
        bit += 1
    keep, *sends = fold(keep, got, (), keep.shape[0], bit)
    done = [[keep] + spread(sends, bit)]
    if outer:
        keep_b, send_b = gather(keep_b[0], got_b)
        done.append([keep_b, along(send_b, 1)])
    return finish(done, classes)


def solution(mesh):
    return jax.shard_map(
        local,
        mesh=mesh,
        in_specs=(
            P(("dom", "cls"), "section", None),
            P(("dom", "cls")),
            P(),
            P(),
            P("cls", None, None, None),
            P("cls", None),
            P("dom", "cls"),
            P("dom"),
        ),
        out_specs=P("cls", ("section", "dom"), None),
        check_vma=False,
    )
```

```python
import functools

import jax
import jax.numpy as jnp
from jax import lax
from jax.experimental import pallas as pl
from jax.experimental.pallas import tpu as pltpu
from jax.sharding import PartitionSpec as P

F32 = jnp.float32
BF16 = jnp.bfloat16
LOW = -1e30
GROUP = 16
PAD = 8
DEEP = 128
SUMS = 0.8
SCALE = 0.1
FOLD = 1
MIB = 1 << 20


def nt(a, b, precision=None):
    return lax.dot_general(
        a, b, (((1,), (1,)), ((), ())), preferred_element_type=F32, precision=precision
    )


def nn(a, b):
    return lax.dot_general(a, b, (((1,), (0,)), ((), ())), preferred_element_type=F32)


def cost(microseconds):
    return pl.CostEstimate(
        flops=int(microseconds * SCALE * 1e9), transcendentals=0, bytes_accessed=int(microseconds * SCALE * 3e6)
    )


def pinned(shape, dtype):
    return pltpu.VMEM(shape, dtype)


def held(x):
    return pltpu.with_memory_space_constraint(x, pltpu.VMEM)


def prepare_kernel(ctf, band, mask, noise, rot, after, left, right, mask_out, noise_out, rot_out, scr):
    del after
    bins, width = ctf.shape
    rots, classes = rot.shape
    padded = rot_out.shape[1]
    total = mask.shape[0]
    count = total // 2

    def negated(v):
        at = (width - lax.broadcasted_iota(jnp.int32, v.shape, 1)) % width
        return jnp.take_along_axis(v, at, axis=1)

    def rolled(row):
        return pltpu.roll(jnp.broadcast_to(row, (width, width)), 0, 1, stride=1, stride_axis=0)

    def with_delta(v):
        return v + jnp.where(lax.broadcasted_iota(jnp.int32, v.shape, 1) == 0, 1.0, 0.0)

    highest = lax.Precision.HIGHEST
    kernels = with_delta(ctf[...])
    bands = with_delta(jnp.broadcast_to(band[...], (8, width)))
    forward = nt(kernels, rolled(negated(bands)[:1]), highest)
    backward = nt(negated(kernels), rolled(bands[:1]), highest)
    for b in range(bins):
        left[b] = rolled(backward[b : b + 1]).astype(BF16)
        right[b] = rolled(forward[b : b + 1]).astype(BF16)

    scr[...] = jnp.zeros_like(scr)
    group = lax.axis_index("cls")
    for half in range(2):
        come = group if half == 0 else 1 - group
        start = pl.multiple_of(come * count, 8)
        scr[half * count : (half + 1) * count, :classes] = mask[pl.ds(start, count)].astype(F32)
    mask_out[...] = scr[...].T[:padded, :total]
    n = noise[...]
    other = jnp.concatenate([n[:, count:], n[:, :count]], axis=1)
    noise_out[...] = jnp.where(group == 0, n, other)
    square = scr.shape[1]
    scr[:square] = jnp.zeros((square, square), F32)
    scr[:rots, :classes] = rot[...].astype(F32)
    turned = scr[:square].T
    for j in range(rots):
        rot_out[j] = jnp.broadcast_to(turned[:padded, j : j + 1], (padded, square))


def prepare(ctf, band, mask, noise, rot, after, padded):
    bins, width = ctf.shape
    total = noise.shape[0]
    lanes = max(128, -(-padded // 128) * 128)
    tall = -(-max(total, lanes) // 128) * 128
    return pl.pallas_call(
        prepare_kernel,
        out_shape=(
            pinned((bins, width, width), BF16),
            pinned((bins, width, width), BF16),
            pinned((padded, total), F32),
            pinned((1, total), F32),
            pinned((rot.shape[0], padded, lanes), F32),
        ),
        scratch_shapes=[pltpu.VMEM((tall, lanes), F32)],
        compiler_params=pltpu.CompilerParams(vmem_limit_bytes=4 * MIB),
        cost_estimate=cost(3),
        name="prepare",
    )(ctf, band.reshape(1, width), mask, noise.reshape(1, total), rot, held(after))


def gate_kernel(*refs):
    del refs


def gate(piece, *tokens):
    anywhere = pl.BlockSpec(memory_space=pl.ANY)
    return pl.pallas_call(
        gate_kernel,
        in_specs=[anywhere] * (1 + len(tokens)),
        out_specs=anywhere,
        out_shape=jax.ShapeDtypeStruct(piece.shape, piece.dtype),
        input_output_aliases={0: 0},
        compiler_params=pltpu.CompilerParams(vmem_limit_bytes=MIB),
        cost_estimate=cost(0.1),
        name="gate",
    )(piece, *tokens)


def refs_kernel(refs, out, norm, scratch, *, padded):
    classes, _, rows, width = refs.shape
    pitch = rows + PAD
    j = pl.program_id(0)

    def block(start, count):
        for k in range(GROUP):
            if k < count:
                scratch[pl.ds(k * pitch, rows)] = refs[start + k, 0].astype(F32)
            else:
                scratch[pl.ds(k * pitch, rows)] = jnp.zeros((rows, width), F32)
        at = pl.multiple_of(j * padded + start, GROUP)

        def step(r, acc):
            v = scratch[pl.ds(r, GROUP, stride=pitch)]
            out[r, pl.ds(at, GROUP)] = v.astype(BF16)
            return acc + v * v

        acc = lax.fori_loop(0, rows, step, jnp.zeros((GROUP, width), F32), unroll=32)
        total = 0.5 * jnp.sum(acc, axis=1, keepdims=True)
        norm[pl.ds(at, GROUP)] = jnp.broadcast_to(total, (GROUP, width))

    full = classes // GROUP

    @pl.loop(0, full)
    def _(i):
        block(i * GROUP, GROUP)

    if classes % GROUP:
        block(full * GROUP, classes % GROUP)


def lay_refs(refs, padded):
    classes, rots, rows, width = refs.shape
    vmem = pl.BlockSpec(memory_space=pltpu.VMEM)
    return pl.pallas_call(
        functools.partial(refs_kernel, padded=padded),
        grid=(rots,),
        in_specs=[pl.BlockSpec((classes, 1, rows, width), lambda j: (0, j, 0, 0))],
        out_specs=(vmem, vmem),
        out_shape=(
            pinned((rows, rots * padded, width), BF16),
            pinned((rots * padded, width), F32),
        ),
        scratch_shapes=[pltpu.VMEM((GROUP * (rows + PAD), width), F32)],
        compiler_params=pltpu.CompilerParams(vmem_limit_bytes=12 * MIB),
        cost_estimate=cost(9),
        name="refs",
    )(pltpu.with_memory_space_constraint(refs, pltpu.HBM))


def filter_kernel(*args, picked, parts, skip, at, chained):
    bins = None if picked else args[0]
    mine, left, right, *rest = args[0 if picked else 1 :]
    sibs = rest[:parts]
    plain, turned, *token = rest[-6 - chained : -4]
    scratch = rest[-4:]
    for t in token:
        t[...] = jnp.zeros_like(t)
    width = mine.shape[2]
    top = lax.axis_index("section") == 0
    pitch = width + PAD

    def group(base, source, turn):
        scr, scr_t = scratch[2 * turn : 2 * turn + 2]
        for i in range(GROUP):
            b = base + i if picked else bins[skip + base + i]
            a = mine[base + i]
            o = source(i)
            x = jnp.concatenate([jnp.where(top, a, o), jnp.where(top, o, a)], axis=0)
            f = nn(left[b], nn(x, right[b]).astype(BF16))
            scr[pl.ds(i * pitch, width)] = f
            scr_t[pl.ds(i * pitch, width)] = f.T
        to = pl.multiple_of(at + base, GROUP)
        for r in range(width):
            plain[r, pl.ds(to, GROUP)] = scr[pl.ds(r, GROUP, stride=pitch)].astype(BF16)
            turned[r, pl.ds(to, GROUP)] = scr_t[pl.ds(r, GROUP, stride=pitch)].astype(BF16)

    groups = mine.shape[0] // GROUP
    if parts > 1 or groups <= 2:
        places = [(sib, i) for sib in sibs for i in range(sib.shape[0])]
        for g in range(groups):

            def source(i, g=g):
                sib, place = places[g * GROUP + i]
                return sib[place]

            group(g * GROUP, source, g % 2)
    else:

        @pl.loop(0, groups)
        def _(g):
            base = pl.multiple_of(g * GROUP, GROUP)
            group(base, lambda i: sibs[0][base + i], 0)


def filter_chunk(bins, mine, sibs, left, right, buffers, total, skip, at, chained):
    count, half, width = mine.shape
    smem = pl.BlockSpec(memory_space=pltpu.SMEM)
    vmem = pl.BlockSpec(memory_space=pltpu.VMEM)
    parts = len(sibs)
    picked = bins is None
    head = [] if picked else [bins]
    return pl.pallas_call(
        functools.partial(
            filter_kernel, picked=picked, parts=parts, skip=skip, at=at, chained=chained
        ),
        in_specs=[smem] * len(head) + [vmem] * (3 + parts + len(buffers)),
        out_specs=(vmem,) * (2 + chained),
        out_shape=(pinned((2 * half, total, width), BF16),) * 2
        + (pinned((8, width), F32),) * chained,
        scratch_shapes=[pltpu.VMEM((GROUP * (2 * half + PAD), width), F32)] * 4,
        input_output_aliases={len(head) + 3 + parts + i: i for i in range(len(buffers))},
        compiler_params=pltpu.CompilerParams(vmem_limit_bytes=8 * MIB),
        cost_estimate=cost(count * 0.1),
        name="filter",
    )(*head, mine, held(left), held(right), *sibs, *[held(b) for b in buffers])


def pick_kernel(bins, left, right, after, left_out, right_out, *, skip):
    del after
    for i in range(left_out.shape[0]):
        left_out[i] = left[bins[skip + i]]
        right_out[i] = right[bins[skip + i]]


def pick(bins, left, right, after, skip, count):
    vmem = pl.BlockSpec(memory_space=pltpu.VMEM)
    return pl.pallas_call(
        functools.partial(pick_kernel, skip=skip),
        in_specs=[pl.BlockSpec(memory_space=pltpu.SMEM), vmem, vmem, vmem],
        out_shape=(pinned((count,) + left.shape[1:], BF16),) * 2,
        compiler_params=pltpu.CompilerParams(vmem_limit_bytes=4 * MIB),
        cost_estimate=cost(1),
        name="pick",
    )(bins, held(left), held(right), held(after))


def score_kernel(plain, refs, norm, mask, noise, scaled, stats):
    rows, height, width = refs.shape
    count = mask.shape[1]

    def step(i, acc):
        at = [DEEP * i + a for a in range(DEEP)]
        lhs = jnp.concatenate([refs[r] for r in at], axis=1)
        rhs = jnp.concatenate([plain[r] for r in at], axis=1)
        return acc + nt(lhs, rhs)

    inner = lax.fori_loop(0, rows // DEEP, step, jnp.zeros((height, count), F32))
    rots = height // mask.shape[0]
    allowed = jnp.concatenate([mask[...]] * rots, axis=0) > 0
    s = jnp.where(allowed, (inner - norm[:, :1]) / noise[...], LOW)
    scaled[...] = s
    peak = jnp.max(s, axis=0, keepdims=True)
    total = jnp.sum(jnp.exp(s - peak), axis=0, keepdims=True)
    stats[0:1] = peak
    stats[1:2] = total
    stats[2:] = jnp.zeros((stats.shape[0] - 2, count), F32)


def score(plain, refs, norm, mask, noise):
    count = mask.shape[1]
    height = refs.shape[1]
    return pl.pallas_call(
        score_kernel,
        out_shape=(
            pinned((height, count), F32),
            pinned((8, count), F32),
        ),
        compiler_params=pltpu.CompilerParams(vmem_limit_bytes=8 * MIB),
        cost_estimate=cost(5),
        name="score",
    )(held(plain), held(refs), held(norm), held(mask), held(noise))


def shares_kernel(scaled, mine, rot, out):
    rots, padded, _ = rot.shape
    e = jnp.exp(scaled[...] - mine[0:1])
    for q in range(4):
        acc = jnp.zeros((padded, scaled.shape[1]), F32)
        for j in range(rots):
            acc = acc + jnp.where(rot[j][:, :1] == q, e[j * padded : (j + 1) * padded], 0.0)
        out[q] = acc


def make_shares(scaled, mine, rot):
    return pl.pallas_call(
        shares_kernel,
        out_shape=pinned((4, rot.shape[1], scaled.shape[1]), F32),
        compiler_params=pltpu.CompilerParams(vmem_limit_bytes=8 * MIB),
        cost_estimate=cost(1),
        name="shares",
    )(held(scaled), held(mine), held(rot))


def weigh(shares, mine, other, out):
    count = shares.shape[2]
    theirs = jnp.concatenate([other[:, count // 2 :], other[:, : count // 2]], axis=1)
    peak = jnp.maximum(mine[0:1], theirs[0:1])
    near = jnp.exp(mine[0:1] - peak)
    total = mine[1:2] * near + theirs[1:2] * jnp.exp(theirs[0:1] - peak)
    factor = near / total
    for row, pair in enumerate(((0, 3), (2, 1))):
        out[row] = jnp.concatenate([shares[q] * factor for q in pair], axis=1).astype(BF16)


def row_pair(weights, plain, turned, both, classes):
    height, _, width = plain.shape
    direct = jnp.concatenate(
        [jnp.concatenate([plain[i], turned[height - 1 - i]], axis=0) for i in both], axis=1
    )
    mirror = jnp.concatenate(
        [jnp.concatenate([plain[height - 1 - i], turned[i]], axis=0) for i in both], axis=1
    )
    direct = nn(weights[0], direct)
    mirror = nn(weights[1], mirror)
    padded = weights.shape[1]
    flip = width - 1 - lax.broadcasted_iota(jnp.int32, (padded, width), 1)
    return [
        (
            direct[:, at : at + width]
            + jnp.take_along_axis(mirror[:, at : at + width], flip, axis=1)
        )[:classes]
        for at in (0, width)
    ]


def row_place(plain, dom, start):
    half = plain.shape[0] // 2
    first = lax.axis_index("section") * half + start
    return lambda block, r: first + block * (half // dom) + r


def one_side(weights, plain, turned, out, side, dom, start, rows, classes):
    place = row_place(plain, dom, start)
    count = dom // 2

    def pair(g, h):
        for r in range(rows):
            both = [place(2 * k + side, r) for k in (g, h)]
            for k, value in zip((g, h), row_pair(weights, plain, turned, both, classes)):
                out[k, r * classes : (r + 1) * classes] = value.astype(out.dtype)

    if count == 1:
        pair(0, 0)
    else:

        @pl.loop(0, count // 2)
        def _(g):
            pair(2 * g, 2 * g + 1)


def both_sides(weights, plain, turned, out, z, dom, start, rows, classes):
    place = row_place(plain, dom, start)
    for r in range(rows):
        both = [place(2 * z + side, r) for side in range(2)]
        for side, value in enumerate(row_pair(weights, plain, turned, both, classes)):
            out[side, r * classes : (r + 1) * classes] = value.astype(out.dtype)


def inner_kernel(shares, mine, other, plain, turned, send, weights, *, dom, **sizes):
    weigh(shares, mine, other, weights)
    away = 1 - lax.axis_index("dom") % 2
    one_side(weights, plain, turned, send, away, dom, **sizes)


def outer_kernel(weights, plain, turned, after, *outs, dom, **sizes):
    del after
    z = lax.axis_index("dom") // 2
    for m, out in enumerate(outs):
        both_sides(weights, plain, turned, out, jnp.bitwise_xor(z, m + 1), dom, **sizes)


def keep_kernel(weights, plain, turned, after, *outs, dom, classes, inner, outer):
    del after
    own = lax.axis_index("dom")
    one_side(weights, plain, turned, outs[0], own % 2, dom, 0, inner, classes)
    if outer:
        both_sides(weights, plain, turned, outs[1], own // 2, dom, inner, outer, classes)


def call_sums(kernel, args, after, out_shape, rows):
    vmem = pl.BlockSpec(memory_space=pltpu.VMEM)
    return pl.pallas_call(
        kernel,
        in_specs=[vmem] * len(args) + [pl.BlockSpec(memory_space=pl.ANY)] * len(after),
        out_shape=out_shape,
        compiler_params=pltpu.CompilerParams(vmem_limit_bytes=8 * MIB),
        cost_estimate=cost(SUMS * rows),
        name="sums",
    )(*args, *after)


def gather_kernel(keep, *rest, came):
    got = rest[:came]
    here, away = rest[-2:]
    parity = lax.axis_index("dom") % 2
    for out, side in ((here, parity), (away, 1 - parity)):
        value = keep[side]
        for other in got:
            value = value + other[side].astype(F32)
        out[0] = value.astype(out.dtype)


def gather(keep, got):
    shape = (1,) + keep.shape[1:]
    return pl.pallas_call(
        functools.partial(gather_kernel, came=len(got)),
        out_shape=(pinned(shape, F32), jax.ShapeDtypeStruct(shape, BF16)),
        compiler_params=pltpu.CompilerParams(vmem_limit_bytes=8 * MIB),
        cost_estimate=cost(FOLD),
        name="gather",
    )(held(keep), *got)


def fold_kernel(keep, got, *outs, fan, bit):
    outs = outs[-fan:]
    rest = keep.shape[0] // fan
    at = (lax.axis_index("dom") // (1 << bit)) % fan
    for m, out in enumerate(outs):
        for i in range(rest):
            b = i * fan + jnp.bitwise_xor(at, m)
            value = keep[b] + got[b].astype(F32)
            out[i] = value.astype(out.dtype)


def fold(keep, got, after, fan, bit):
    rest = (keep.shape[0] // fan,) + keep.shape[1:]
    return pl.pallas_call(
        functools.partial(fold_kernel, fan=fan, bit=bit),
        in_specs=[pl.BlockSpec(memory_space=pltpu.VMEM)] * 2
        + [pl.BlockSpec(memory_space=pl.ANY)] * len(after),
        out_shape=(pinned(rest, F32),) + (jax.ShapeDtypeStruct(rest, BF16),) * (fan - 1),
        compiler_params=pltpu.CompilerParams(vmem_limit_bytes=8 * MIB),
        cost_estimate=cost(FOLD),
        name="fold",
    )(held(keep), got, *after)


def finish_kernel(*args, counts, classes):
    out = args[-1]
    block_rows = sum(rows for rows, _ in counts)
    at = 0
    row = 0
    for rows, pieces in counts:
        for r in range(rows):
            cut = slice(r * classes, (r + 1) * classes)
            value = args[at][0, cut]
            for other in args[at + 1 : at + pieces]:
                value = value + other[0, cut].astype(F32)
            out[pl.ds(row, classes, stride=block_rows)] = value
            row += 1
        at += pieces


def finish(done, classes):
    counts = tuple((pieces[0].shape[1] // classes, len(pieces)) for pieces in done)
    width = done[0][0].shape[2]
    block_rows = sum(rows for rows, _ in counts)
    flat = [held(p) if i == 0 else p for pieces in done for i, p in enumerate(pieces)]
    out = pl.pallas_call(
        functools.partial(finish_kernel, counts=counts, classes=classes),
        out_shape=jax.ShapeDtypeStruct((classes * block_rows, width), F32),
        compiler_params=pltpu.CompilerParams(vmem_limit_bytes=8 * MIB),
        cost_estimate=cost(1),
        name="finish",
    )(*flat)
    return out.reshape(classes, block_rows, width)


def y_pieces(particles):
    last = GROUP
    middle = particles // 3 // GROUP * GROUP
    return ((particles - middle - last, GROUP), (middle, GROUP // 2), (last, last))


def row_pieces(rows, dom):
    if rows < 4 or dom > 8:
        return (rows, 0)
    outer = rows * 3 // 8
    return (rows - outer, outer)


def local(
    images, defocus_bin, ctf_kernels, band_kernel, references, rot_index, class_mask, noise_var
):
    dom = lax.axis_size("dom")
    particles, half, width = images.shape
    classes = rot_index.shape[0]
    padded = -(-classes // GROUP) * GROUP
    swap = [(0, 1), (1, 0)]
    over_cls = functools.partial(lax.ppermute, axis_name="cls", perm=swap)
    over_section = functools.partial(lax.ppermute, axis_name="section", perm=swap)

    sizes, steps = zip(*y_pieces(particles))
    starts = [sum(sizes[:i]) for i in range(len(sizes))]
    remote = [over_cls(images[a : a + n]) for a, n in zip(starts, sizes)]
    other_bins = over_cls(defocus_bin)
    own_sib = over_section(images)

    refs, norm = lay_refs(references, padded)
    left, right, mask, noise, rot = prepare(
        ctf_kernels, band_kernel, class_mask, noise_var, rot_index.T, norm, padded
    )
    total = 2 * particles
    *buffers, token = filter_chunk(
        defocus_bin, images, [own_sib], left, right, (), total, 0, 0, 1
    )
    chosen = pick(other_bins, left, right, token, starts[-1], sizes[-1])
    tokens = [chosen[0]]
    for i, a in enumerate(starts):
        piece = gate(remote[i], *tokens)
        step = steps[i]
        sibs = [over_section(piece[b : b + step]) for b in range(0, sizes[i], step)]
        last = i + 1 == len(starts)
        filters = (None, piece, sibs, *chosen) if last else (other_bins, piece, sibs, left, right)
        made = filter_chunk(*filters, buffers, total, a, particles + a, int(not last))
        buffers = made[:2]
        tokens = made[2:]
    plain, turned = buffers

    scaled, stats = score(plain, refs, norm, mask, noise)
    theirs = over_cls(stats)
    inputs = (held(make_shares(scaled, stats, rot)), held(stats), theirs)

    def along(x, mask):
        return lax.ppermute(x, "dom", [(i, i ^ mask) for i in range(dom)])

    def spread(sends, bit):
        far_first = sorted(range(len(sends)), key=lambda m: m == 0)
        return [along(sends[m], (m + 1) << bit) for m in far_first]

    inner, outer = row_pieces(half // dom, dom)
    images_in = (held(plain), held(turned))
    count = dom // 2
    send, weights = call_sums(
        functools.partial(
            inner_kernel, dom=dom, start=0, rows=inner, classes=classes
        ),
        inputs + images_in,
        (),
        (
            jax.ShapeDtypeStruct((count, inner * classes, width), BF16),
            pinned((2, rot.shape[1], 2 * total), BF16),
        ),
        inner,
    )
    got = along(send, 1)
    weighted = (held(weights),) + images_in
    keep_shape = (pinned((count, inner * classes, width), F32),)
    after = send
    if outer:
        shape = (2, outer * classes, width)
        sends_b = call_sums(
            functools.partial(
                outer_kernel, dom=dom, start=inner, rows=outer, classes=classes
            ),
            weighted,
            (send,),
            (jax.ShapeDtypeStruct(shape, BF16),) * (count - 1),
            outer,
        )
        got_b = spread(sends_b, 1)
        keep_shape += (pinned(shape, F32),)
        after = sends_b[0]
    keep, *keep_b = call_sums(
        functools.partial(keep_kernel, dom=dom, classes=classes, inner=inner, outer=outer),
        weighted,
        (after,),
        keep_shape,
        inner,
    )
    bit = 1
    while keep.shape[0] > 4:
        keep, send = fold(keep, got, (), 2, bit)
        got = along(send, 1 << bit)
        bit += 1
    keep, *sends = fold(keep, got, (), keep.shape[0], bit)
    done = [[keep] + spread(sends, bit)]
    if outer:
        keep_b, send_b = gather(keep_b[0], got_b)
        done.append([keep_b, along(send_b, 1)])
    return finish(done, classes)


def solution(mesh):
    return jax.shard_map(
        local,
        mesh=mesh,
        in_specs=(
            P(("dom", "cls"), "section", None),
            P(("dom", "cls")),
            P(),
            P(),
            P("cls", None, None, None),
            P("cls", None),
            P("dom", "cls"),
            P("dom"),
        ),
        out_specs=P("cls", ("section", "dom"), None),
        check_vma=False,
    )
```

```python
import functools

import jax
import jax.numpy as jnp
from jax import lax
from jax.experimental import pallas as pl
from jax.experimental.pallas import tpu as pltpu
from jax.sharding import PartitionSpec as P

F32 = jnp.float32
BF16 = jnp.bfloat16
LOW = -1e30
GROUP = 16
PAD = 8
DEEP = 128
SUMS = 0.8
SCALE = 0.1
FOLD = 1
MIB = 1 << 20


def nt(a, b, precision=None):
    return lax.dot_general(
        a, b, (((1,), (1,)), ((), ())), preferred_element_type=F32, precision=precision
    )


def nn(a, b):
    return lax.dot_general(a, b, (((1,), (0,)), ((), ())), preferred_element_type=F32)


def cost(microseconds):
    return pl.CostEstimate(
        flops=int(microseconds * SCALE * 1e9), transcendentals=0, bytes_accessed=int(microseconds * SCALE * 3e6)
    )


def pinned(shape, dtype):
    return pltpu.VMEM(shape, dtype)


def held(x):
    return pltpu.with_memory_space_constraint(x, pltpu.VMEM)


def prepare_kernel(ctf, band, mask, noise, rot, after, left, right, mask_out, noise_out, rot_out, scr):
    del after
    bins, width = ctf.shape
    rots, classes = rot.shape
    padded = rot_out.shape[1]
    total = mask.shape[0]
    count = total // 2

    def negated(v):
        at = (width - lax.broadcasted_iota(jnp.int32, v.shape, 1)) % width
        return jnp.take_along_axis(v, at, axis=1)

    def rolled(row):
        return pltpu.roll(jnp.broadcast_to(row, (width, width)), 0, 1, stride=1, stride_axis=0)

    def with_delta(v):
        return v + jnp.where(lax.broadcasted_iota(jnp.int32, v.shape, 1) == 0, 1.0, 0.0)

    highest = lax.Precision.HIGHEST
    kernels = with_delta(ctf[...])
    bands = with_delta(jnp.broadcast_to(band[...], (8, width)))
    forward = nt(kernels, rolled(negated(bands)[:1]), highest)
    backward = nt(negated(kernels), rolled(bands[:1]), highest)
    for b in range(bins):
        left[b] = rolled(backward[b : b + 1]).astype(BF16)
        right[b] = rolled(forward[b : b + 1]).astype(BF16)

    scr[...] = jnp.zeros_like(scr)
    group = lax.axis_index("cls")
    for half in range(2):
        come = group if half == 0 else 1 - group
        start = pl.multiple_of(come * count, 8)
        scr[half * count : (half + 1) * count, :classes] = mask[pl.ds(start, count)].astype(F32)
    mask_out[...] = scr[...].T[:padded, :total]
    n = noise[...]
    other = jnp.concatenate([n[:, count:], n[:, :count]], axis=1)
    noise_out[...] = jnp.where(group == 0, n, other)
    square = scr.shape[1]
    scr[:square] = jnp.zeros((square, square), F32)
    scr[:rots, :classes] = rot[...].astype(F32)
    turned = scr[:square].T
    for j in range(rots):
        rot_out[j] = jnp.broadcast_to(turned[:padded, j : j + 1], (padded, square))


def prepare(ctf, band, mask, noise, rot, after, padded):
    bins, width = ctf.shape
    total = noise.shape[0]
    lanes = max(128, -(-padded // 128) * 128)
    tall = -(-max(total, lanes) // 128) * 128
    return pl.pallas_call(
        prepare_kernel,
        out_shape=(
            pinned((bins, width, width), BF16),
            pinned((bins, width, width), BF16),
            pinned((padded, total), F32),
            pinned((1, total), F32),
            pinned((rot.shape[0], padded, lanes), F32),
        ),
        scratch_shapes=[pltpu.VMEM((tall, lanes), F32)],
        compiler_params=pltpu.CompilerParams(vmem_limit_bytes=4 * MIB),
        cost_estimate=cost(3),
        name="prepare",
    )(ctf, band.reshape(1, width), mask, noise.reshape(1, total), rot, held(after))


def gate_kernel(*refs):
    del refs


def gate(piece, *tokens):
    anywhere = pl.BlockSpec(memory_space=pl.ANY)
    return pl.pallas_call(
        gate_kernel,
        in_specs=[anywhere] * (1 + len(tokens)),
        out_specs=anywhere,
        out_shape=jax.ShapeDtypeStruct(piece.shape, piece.dtype),
        input_output_aliases={0: 0},
        compiler_params=pltpu.CompilerParams(vmem_limit_bytes=MIB),
        cost_estimate=cost(0.1),
        name="gate",
    )(piece, *tokens)


def refs_kernel(refs, out, norm, scratch, *, padded):
    classes, _, rows, width = refs.shape
    pitch = rows + PAD
    j = pl.program_id(0)

    def block(start, count):
        for k in range(GROUP):
            if k < count:
                scratch[pl.ds(k * pitch, rows)] = refs[start + k, 0].astype(F32)
            else:
                scratch[pl.ds(k * pitch, rows)] = jnp.zeros((rows, width), F32)
        at = pl.multiple_of(j * padded + start, GROUP)

        def step(r, acc):
            v = scratch[pl.ds(r, GROUP, stride=pitch)]
            out[r, pl.ds(at, GROUP)] = v.astype(BF16)
            return acc + v * v

        acc = lax.fori_loop(0, rows, step, jnp.zeros((GROUP, width), F32), unroll=32)
        total = 0.5 * jnp.sum(acc, axis=1, keepdims=True)
        norm[pl.ds(at, GROUP)] = jnp.broadcast_to(total, (GROUP, width))

    full = classes // GROUP

    @pl.loop(0, full)
    def _(i):
        block(i * GROUP, GROUP)

    if classes % GROUP:
        block(full * GROUP, classes % GROUP)


def lay_refs(refs, padded):
    classes, rots, rows, width = refs.shape
    vmem = pl.BlockSpec(memory_space=pltpu.VMEM)
    return pl.pallas_call(
        functools.partial(refs_kernel, padded=padded),
        grid=(rots,),
        in_specs=[pl.BlockSpec((classes, 1, rows, width), lambda j: (0, j, 0, 0))],
        out_specs=(vmem, vmem),
        out_shape=(
            pinned((rows, rots * padded, width), BF16),
            pinned((rots * padded, width), F32),
        ),
        scratch_shapes=[pltpu.VMEM((GROUP * (rows + PAD), width), F32)],
        compiler_params=pltpu.CompilerParams(vmem_limit_bytes=12 * MIB),
        cost_estimate=cost(9),
        name="refs",
    )(pltpu.with_memory_space_constraint(refs, pltpu.HBM))


def filter_kernel(*args, picked, parts, skip, at, chained):
    bins = None if picked else args[0]
    mine, left, right, *rest = args[0 if picked else 1 :]
    sibs = rest[:parts]
    plain, turned, *token = rest[-6 - chained : -4]
    scratch = rest[-4:]
    for t in token:
        t[...] = jnp.zeros_like(t)
    width = mine.shape[2]
    top = lax.axis_index("section") == 0
    pitch = width + PAD

    def group(base, source, turn):
        scr, scr_t = scratch[2 * turn : 2 * turn + 2]
        for i in range(GROUP):
            b = base + i if picked else bins[skip + base + i]
            a = mine[base + i]
            o = source(i)
            x = jnp.concatenate([jnp.where(top, a, o), jnp.where(top, o, a)], axis=0)
            f = nn(left[b], nn(x, right[b]).astype(BF16))
            scr[pl.ds(i * pitch, width)] = f
            scr_t[pl.ds(i * pitch, width)] = f.T
        to = pl.multiple_of(at + base, GROUP)
        for r in range(width):
            plain[r, pl.ds(to, GROUP)] = scr[pl.ds(r, GROUP, stride=pitch)].astype(BF16)
            turned[r, pl.ds(to, GROUP)] = scr_t[pl.ds(r, GROUP, stride=pitch)].astype(BF16)

    groups = mine.shape[0] // GROUP
    if parts > 1 or groups <= 2:
        places = [(sib, i) for sib in sibs for i in range(sib.shape[0])]
        for g in range(groups):

            def source(i, g=g):
                sib, place = places[g * GROUP + i]
                return sib[place]

            group(g * GROUP, source, g % 2)
    else:

        @pl.loop(0, groups)
        def _(g):
            base = pl.multiple_of(g * GROUP, GROUP)
            group(base, lambda i: sibs[0][base + i], 0)


def filter_chunk(bins, mine, sibs, left, right, buffers, total, skip, at, chained):
    count, half, width = mine.shape
    smem = pl.BlockSpec(memory_space=pltpu.SMEM)
    vmem = pl.BlockSpec(memory_space=pltpu.VMEM)
    parts = len(sibs)
    picked = bins is None
    head = [] if picked else [bins]
    return pl.pallas_call(
        functools.partial(
            filter_kernel, picked=picked, parts=parts, skip=skip, at=at, chained=chained
        ),
        in_specs=[smem] * len(head) + [vmem] * (3 + parts + len(buffers)),
        out_specs=(vmem,) * (2 + chained),
        out_shape=(pinned((2 * half, total, width), BF16),) * 2
        + (pinned((8, width), F32),) * chained,
        scratch_shapes=[pltpu.VMEM((GROUP * (2 * half + PAD), width), F32)] * 4,
        input_output_aliases={len(head) + 3 + parts + i: i for i in range(len(buffers))},
        compiler_params=pltpu.CompilerParams(vmem_limit_bytes=8 * MIB),
        cost_estimate=cost(count * 0.1),
        name="filter",
    )(*head, mine, held(left), held(right), *sibs, *[held(b) for b in buffers])


def pick_kernel(bins, left, right, after, left_out, right_out, *, skip):
    del after
    for i in range(left_out.shape[0]):
        left_out[i] = left[bins[skip + i]]
        right_out[i] = right[bins[skip + i]]


def pick(bins, left, right, after, skip, count):
    vmem = pl.BlockSpec(memory_space=pltpu.VMEM)
    return pl.pallas_call(
        functools.partial(pick_kernel, skip=skip),
        in_specs=[pl.BlockSpec(memory_space=pltpu.SMEM), vmem, vmem, vmem],
        out_shape=(pinned((count,) + left.shape[1:], BF16),) * 2,
        compiler_params=pltpu.CompilerParams(vmem_limit_bytes=4 * MIB),
        cost_estimate=cost(1),
        name="pick",
    )(bins, held(left), held(right), held(after))


def score_kernel(plain, refs, norm, mask, noise, scaled, stats):
    rows, height, width = refs.shape
    count = mask.shape[1]

    def step(i, acc):
        at = [DEEP * i + a for a in range(DEEP)]
        lhs = jnp.concatenate([refs[r] for r in at], axis=1)
        rhs = jnp.concatenate([plain[r] for r in at], axis=1)
        return acc + nt(lhs, rhs)

    inner = lax.fori_loop(0, rows // DEEP, step, jnp.zeros((height, count), F32))
    rots = height // mask.shape[0]
    allowed = jnp.concatenate([mask[...]] * rots, axis=0) > 0
    s = jnp.where(allowed, (inner - norm[:, :1]) / noise[...], LOW)
    scaled[...] = s
    peak = jnp.max(s, axis=0, keepdims=True)
    total = jnp.sum(jnp.exp(s - peak), axis=0, keepdims=True)
    stats[0:1] = peak
    stats[1:2] = total
    stats[2:] = jnp.zeros((stats.shape[0] - 2, count), F32)


def score(plain, refs, norm, mask, noise):
    count = mask.shape[1]
    height = refs.shape[1]
    return pl.pallas_call(
        score_kernel,
        out_shape=(
            pinned((height, count), F32),
            pinned((8, count), F32),
        ),
        compiler_params=pltpu.CompilerParams(vmem_limit_bytes=8 * MIB),
        cost_estimate=cost(5),
        name="score",
    )(held(plain), held(refs), held(norm), held(mask), held(noise))


def shares_kernel(scaled, mine, rot, out):
    rots, padded, _ = rot.shape
    e = jnp.exp(scaled[...] - mine[0:1])
    for q in range(4):
        acc = jnp.zeros((padded, scaled.shape[1]), F32)
        for j in range(rots):
            acc = acc + jnp.where(rot[j][:, :1] == q, e[j * padded : (j + 1) * padded], 0.0)
        out[q] = acc


def make_shares(scaled, mine, rot):
    return pl.pallas_call(
        shares_kernel,
        out_shape=pinned((4, rot.shape[1], scaled.shape[1]), F32),
        compiler_params=pltpu.CompilerParams(vmem_limit_bytes=8 * MIB),
        cost_estimate=cost(1),
        name="shares",
    )(held(scaled), held(mine), held(rot))


def weigh(shares, mine, other, out):
    count = shares.shape[2]
    theirs = jnp.concatenate([other[:, count // 2 :], other[:, : count // 2]], axis=1)
    peak = jnp.maximum(mine[0:1], theirs[0:1])
    near = jnp.exp(mine[0:1] - peak)
    total = mine[1:2] * near + theirs[1:2] * jnp.exp(theirs[0:1] - peak)
    factor = near / total
    for row, pair in enumerate(((0, 3), (2, 1))):
        out[row] = jnp.concatenate([shares[q] * factor for q in pair], axis=1).astype(BF16)


def row_pair(weights, plain, turned, both, classes):
    height, _, width = plain.shape
    direct = jnp.concatenate(
        [jnp.concatenate([plain[i], turned[height - 1 - i]], axis=0) for i in both], axis=1
    )
    mirror = jnp.concatenate(
        [jnp.concatenate([plain[height - 1 - i], turned[i]], axis=0) for i in both], axis=1
    )
    direct = nn(weights[0], direct)
    mirror = nn(weights[1], mirror)
    padded = weights.shape[1]
    flip = width - 1 - lax.broadcasted_iota(jnp.int32, (padded, width), 1)
    return [
        (
            direct[:, at : at + width]
            + jnp.take_along_axis(mirror[:, at : at + width], flip, axis=1)
        )[:classes]
        for at in (0, width)
    ]


def row_place(plain, dom, start):
    half = plain.shape[0] // 2
    first = lax.axis_index("section") * half + start
    return lambda block, r: first + block * (half // dom) + r


def one_side(weights, plain, turned, out, side, dom, start, rows, classes):
    place = row_place(plain, dom, start)
    count = dom // 2

    def pair(g, h):
        for r in range(rows):
            both = [place(2 * k + side, r) for k in (g, h)]
            for k, value in zip((g, h), row_pair(weights, plain, turned, both, classes)):
                out[k, r * classes : (r + 1) * classes] = value.astype(out.dtype)

    if count == 1:
        pair(0, 0)
    else:

        @pl.loop(0, count // 2)
        def _(g):
            pair(2 * g, 2 * g + 1)


def both_sides(weights, plain, turned, out, z, dom, start, rows, classes):
    place = row_place(plain, dom, start)
    for r in range(rows):
        both = [place(2 * z + side, r) for side in range(2)]
        for side, value in enumerate(row_pair(weights, plain, turned, both, classes)):
            out[side, r * classes : (r + 1) * classes] = value.astype(out.dtype)


def inner_kernel(shares, mine, other, plain, turned, send, weights, *, dom, **sizes):
    weigh(shares, mine, other, weights)
    away = 1 - lax.axis_index("dom") % 2
    one_side(weights, plain, turned, send, away, dom, **sizes)


def outer_kernel(weights, plain, turned, after, *outs, dom, **sizes):
    del after
    z = lax.axis_index("dom") // 2
    for m, out in enumerate(outs):
        both_sides(weights, plain, turned, out, jnp.bitwise_xor(z, m + 1), dom, **sizes)


def keep_kernel(weights, plain, turned, after, *outs, dom, classes, inner, outer):
    del after
    own = lax.axis_index("dom")
    one_side(weights, plain, turned, outs[0], own % 2, dom, 0, inner, classes)
    if outer:
        both_sides(weights, plain, turned, outs[1], own // 2, dom, inner, outer, classes)


def call_sums(kernel, args, after, out_shape, rows):
    vmem = pl.BlockSpec(memory_space=pltpu.VMEM)
    return pl.pallas_call(
        kernel,
        in_specs=[vmem] * len(args) + [pl.BlockSpec(memory_space=pl.ANY)] * len(after),
        out_shape=out_shape,
        compiler_params=pltpu.CompilerParams(vmem_limit_bytes=8 * MIB),
        cost_estimate=cost(SUMS * rows),
        name="sums",
    )(*args, *after)


def gather_kernel(keep, *rest, came):
    got = rest[:came]
    here, away = rest[-2:]
    parity = lax.axis_index("dom") % 2
    for out, side in ((here, parity), (away, 1 - parity)):
        value = keep[side]
        for other in got:
            value = value + other[side].astype(F32)
        out[0] = value.astype(out.dtype)


def gather(keep, got):
    shape = (1,) + keep.shape[1:]
    return pl.pallas_call(
        functools.partial(gather_kernel, came=len(got)),
        out_shape=(pinned(shape, F32), jax.ShapeDtypeStruct(shape, BF16)),
        compiler_params=pltpu.CompilerParams(vmem_limit_bytes=8 * MIB),
        cost_estimate=cost(FOLD),
        name="gather",
    )(held(keep), *got)


def fold_kernel(keep, got, *outs, fan, bit):
    outs = outs[-fan:]
    rest = keep.shape[0] // fan
    at = (lax.axis_index("dom") // (1 << bit)) % fan
    for m, out in enumerate(outs):
        for i in range(rest):
            b = i * fan + jnp.bitwise_xor(at, m)
            value = keep[b] + got[b].astype(F32)
            out[i] = value.astype(out.dtype)


def fold(keep, got, after, fan, bit):
    rest = (keep.shape[0] // fan,) + keep.shape[1:]
    return pl.pallas_call(
        functools.partial(fold_kernel, fan=fan, bit=bit),
        in_specs=[pl.BlockSpec(memory_space=pltpu.VMEM)] * 2
        + [pl.BlockSpec(memory_space=pl.ANY)] * len(after),
        out_shape=(pinned(rest, F32),) + (jax.ShapeDtypeStruct(rest, BF16),) * (fan - 1),
        compiler_params=pltpu.CompilerParams(vmem_limit_bytes=8 * MIB),
        cost_estimate=cost(FOLD),
        name="fold",
    )(held(keep), got, *after)


def finish_kernel(*args, counts, classes):
    out = args[-1]
    block_rows = sum(rows for rows, _ in counts)
    at = 0
    row = 0
    for rows, pieces in counts:
        for r in range(rows):
            cut = slice(r * classes, (r + 1) * classes)
            value = args[at][0, cut]
            for other in args[at + 1 : at + pieces]:
                value = value + other[0, cut].astype(F32)
            out[pl.ds(row, classes, stride=block_rows)] = value
            row += 1
        at += pieces


def finish(done, classes):
    counts = tuple((pieces[0].shape[1] // classes, len(pieces)) for pieces in done)
    width = done[0][0].shape[2]
    block_rows = sum(rows for rows, _ in counts)
    flat = [held(p) if i == 0 else p for pieces in done for i, p in enumerate(pieces)]
    out = pl.pallas_call(
        functools.partial(finish_kernel, counts=counts, classes=classes),
        out_shape=jax.ShapeDtypeStruct((classes * block_rows, width), F32),
        compiler_params=pltpu.CompilerParams(vmem_limit_bytes=8 * MIB),
        cost_estimate=cost(1),
        name="finish",
    )(*flat)
    return out.reshape(classes, block_rows, width)


def y_pieces(particles):
    last = GROUP
    middle = particles // 3 // GROUP * GROUP
    return ((particles - middle - last, GROUP), (middle, GROUP // 2), (last, last))


def row_pieces(rows, dom):
    if rows < 4 or dom > 8:
        return (rows, 0)
    outer = rows * 3 // 8
    return (rows - outer, outer)


def local(
    images, defocus_bin, ctf_kernels, band_kernel, references, rot_index, class_mask, noise_var
):
    dom = lax.axis_size("dom")
    particles, half, width = images.shape
    classes = rot_index.shape[0]
    padded = -(-classes // GROUP) * GROUP
    swap = [(0, 1), (1, 0)]
    over_cls = functools.partial(lax.ppermute, axis_name="cls", perm=swap)
    over_section = functools.partial(lax.ppermute, axis_name="section", perm=swap)

    sizes, steps = zip(*y_pieces(particles))
    starts = [sum(sizes[:i]) for i in range(len(sizes))]
    remote = [over_cls(images[a : a + n]) for a, n in zip(starts, sizes)]
    other_bins = over_cls(defocus_bin)
    own_sib = over_section(images)

    refs, norm = lay_refs(references, padded)
    left, right, mask, noise, rot = prepare(
        ctf_kernels, band_kernel, class_mask, noise_var, rot_index.T, norm, padded
    )
    total = 2 * particles
    *buffers, token = filter_chunk(
        defocus_bin, images, [own_sib], left, right, (), total, 0, 0, 1
    )
    chosen = pick(other_bins, left, right, token, starts[-1], sizes[-1])
    tokens = [chosen[0]]
    for i, a in enumerate(starts):
        piece = gate(remote[i], *tokens)
        step = steps[i]
        sibs = [over_section(piece[b : b + step]) for b in range(0, sizes[i], step)]
        last = i + 1 == len(starts)
        filters = (None, piece, sibs, *chosen) if last else (other_bins, piece, sibs, left, right)
        made = filter_chunk(*filters, buffers, total, a, particles + a, int(not last))
        buffers = made[:2]
        tokens = made[2:]
    plain, turned = buffers

    scaled, stats = score(plain, refs, norm, mask, noise)
    theirs = over_cls(stats)
    inputs = (held(make_shares(scaled, stats, rot)), held(stats), theirs)

    def along(x, mask):
        return lax.ppermute(x, "dom", [(i, i ^ mask) for i in range(dom)])

    def spread(sends, bit, order):
        order = [m for m in order if m < len(sends)]
        return [along(sends[m], (m + 1) << bit) for m in order]

    inner, outer = row_pieces(half // dom, dom)
    images_in = (held(plain), held(turned))
    count = dom // 2
    send, weights = call_sums(
        functools.partial(
            inner_kernel, dom=dom, start=0, rows=inner, classes=classes
        ),
        inputs + images_in,
        (),
        (
            jax.ShapeDtypeStruct((count, inner * classes, width), BF16),
            pinned((2, rot.shape[1], 2 * total), BF16),
        ),
        inner,
    )
    got = along(send, 1)
    weighted = (held(weights),) + images_in
    keep_shape = (pinned((count, inner * classes, width), F32),)
    after = send
    if outer:
        shape = (2, outer * classes, width)
        sends_b = call_sums(
            functools.partial(
                outer_kernel, dom=dom, start=inner, rows=outer, classes=classes
            ),
            weighted,
            (send,),
            (jax.ShapeDtypeStruct(shape, BF16),) * (count - 1),
            outer,
        )
        got_b = spread(sends_b, 1, (1, 2, 0))
        keep_shape += (pinned(shape, F32),)
        after = sends_b[0]
    keep, *keep_b = call_sums(
        functools.partial(keep_kernel, dom=dom, classes=classes, inner=inner, outer=outer),
        weighted,
        (after,),
        keep_shape,
        inner,
    )
    bit = 1
    while keep.shape[0] > 4:
        keep, send = fold(keep, got, (), 2, bit)
        got = along(send, 1 << bit)
        bit += 1
    keep, *sends = fold(keep, got, (), keep.shape[0], bit)
    done = [[keep] + spread(sends, bit, (2, 0, 1))]
    if outer:
        keep_b, send_b = gather(keep_b[0], got_b)
        done.append([keep_b, along(send_b, 1)])
    return finish(done, classes)


def solution(mesh):
    return jax.shard_map(
        local,
        mesh=mesh,
        in_specs=(
            P(("dom", "cls"), "section", None),
            P(("dom", "cls")),
            P(),
            P(),
            P("cls", None, None, None),
            P("cls", None),
            P("dom", "cls"),
            P("dom"),
        ),
        out_specs=P("cls", ("section", "dom"), None),
        check_vma=False,
    )
```

```python
import functools

import jax
import jax.numpy as jnp
from jax import lax
from jax.experimental import pallas as pl
from jax.experimental.pallas import tpu as pltpu
from jax.sharding import PartitionSpec as P

F32 = jnp.float32
BF16 = jnp.bfloat16
LOW = -1e30
GROUP = 16
PAD = 8
DEEP = 128
SUMS = 0.8
SCALE = 0.1
FOLD = 1
MIB = 1 << 20


def nt(a, b, precision=None):
    return lax.dot_general(
        a, b, (((1,), (1,)), ((), ())), preferred_element_type=F32, precision=precision
    )


def nn(a, b):
    return lax.dot_general(a, b, (((1,), (0,)), ((), ())), preferred_element_type=F32)


def cost(microseconds):
    return pl.CostEstimate(
        flops=int(microseconds * SCALE * 1e9), transcendentals=0, bytes_accessed=int(microseconds * SCALE * 3e6)
    )


def pinned(shape, dtype):
    return pltpu.VMEM(shape, dtype)


def held(x):
    return pltpu.with_memory_space_constraint(x, pltpu.VMEM)


def prepare_kernel(ctf, band, mask, noise, rot, after, left, right, mask_out, noise_out, rot_out, scr):
    del after
    bins, width = ctf.shape
    rots, classes = rot.shape
    padded = rot_out.shape[1]
    total = mask.shape[0]
    count = total // 2

    def negated(v):
        at = (width - lax.broadcasted_iota(jnp.int32, v.shape, 1)) % width
        return jnp.take_along_axis(v, at, axis=1)

    def rolled(row):
        return pltpu.roll(jnp.broadcast_to(row, (width, width)), 0, 1, stride=1, stride_axis=0)

    def with_delta(v):
        return v + jnp.where(lax.broadcasted_iota(jnp.int32, v.shape, 1) == 0, 1.0, 0.0)

    highest = lax.Precision.HIGHEST
    kernels = with_delta(ctf[...])
    bands = with_delta(jnp.broadcast_to(band[...], (8, width)))
    forward = nt(kernels, rolled(negated(bands)[:1]), highest)
    backward = nt(negated(kernels), rolled(bands[:1]), highest)
    for b in range(bins):
        left[b] = rolled(backward[b : b + 1]).astype(BF16)
        right[b] = rolled(forward[b : b + 1]).astype(BF16)

    scr[...] = jnp.zeros_like(scr)
    group = lax.axis_index("cls")
    for half in range(2):
        come = group if half == 0 else 1 - group
        start = pl.multiple_of(come * count, 8)
        scr[half * count : (half + 1) * count, :classes] = mask[pl.ds(start, count)].astype(F32)
    mask_out[...] = scr[...].T[:padded, :total]
    n = noise[...]
    other = jnp.concatenate([n[:, count:], n[:, :count]], axis=1)
    noise_out[...] = jnp.where(group == 0, n, other)
    square = scr.shape[1]
    scr[:square] = jnp.zeros((square, square), F32)
    scr[:rots, :classes] = rot[...].astype(F32)
    turned = scr[:square].T
    for j in range(rots):
        rot_out[j] = jnp.broadcast_to(turned[:padded, j : j + 1], (padded, square))


def prepare(ctf, band, mask, noise, rot, after, padded):
    bins, width = ctf.shape
    total = noise.shape[0]
    lanes = max(128, -(-padded // 128) * 128)
    tall = -(-max(total, lanes) // 128) * 128
    return pl.pallas_call(
        prepare_kernel,
        out_shape=(
            pinned((bins, width, width), BF16),
            pinned((bins, width, width), BF16),
            pinned((padded, total), F32),
            pinned((1, total), F32),
            pinned((rot.shape[0], padded, lanes), F32),
        ),
        scratch_shapes=[pltpu.VMEM((tall, lanes), F32)],
        compiler_params=pltpu.CompilerParams(vmem_limit_bytes=4 * MIB),
        cost_estimate=cost(3),
        name="prepare",
    )(ctf, band.reshape(1, width), mask, noise.reshape(1, total), rot, held(after))


def gate_kernel(*refs):
    del refs


def gate(piece, *tokens):
    anywhere = pl.BlockSpec(memory_space=pl.ANY)
    return pl.pallas_call(
        gate_kernel,
        in_specs=[anywhere] * (1 + len(tokens)),
        out_specs=anywhere,
        out_shape=jax.ShapeDtypeStruct(piece.shape, piece.dtype),
        input_output_aliases={0: 0},
        compiler_params=pltpu.CompilerParams(vmem_limit_bytes=MIB),
        cost_estimate=cost(0.1),
        name="gate",
    )(piece, *tokens)


def refs_kernel(refs, out, norm, scratch, *, padded):
    classes, _, rows, width = refs.shape
    pitch = rows + PAD
    j = pl.program_id(0)

    def block(start, count):
        for k in range(GROUP):
            if k < count:
                scratch[pl.ds(k * pitch, rows)] = refs[start + k, 0].astype(F32)
            else:
                scratch[pl.ds(k * pitch, rows)] = jnp.zeros((rows, width), F32)
        at = pl.multiple_of(j * padded + start, GROUP)

        def step(r, acc):
            v = scratch[pl.ds(r, GROUP, stride=pitch)]
            out[r, pl.ds(at, GROUP)] = v.astype(BF16)
            return acc + v * v

        acc = lax.fori_loop(0, rows, step, jnp.zeros((GROUP, width), F32), unroll=32)
        total = 0.5 * jnp.sum(acc, axis=1, keepdims=True)
        norm[pl.ds(at, GROUP)] = jnp.broadcast_to(total, (GROUP, width))

    full = classes // GROUP

    @pl.loop(0, full)
    def _(i):
        block(i * GROUP, GROUP)

    if classes % GROUP:
        block(full * GROUP, classes % GROUP)


def lay_refs(refs, padded):
    classes, rots, rows, width = refs.shape
    vmem = pl.BlockSpec(memory_space=pltpu.VMEM)
    return pl.pallas_call(
        functools.partial(refs_kernel, padded=padded),
        grid=(rots,),
        in_specs=[pl.BlockSpec((classes, 1, rows, width), lambda j: (0, j, 0, 0))],
        out_specs=(vmem, vmem),
        out_shape=(
            pinned((rows, rots * padded, width), BF16),
            pinned((rots * padded, width), F32),
        ),
        scratch_shapes=[pltpu.VMEM((GROUP * (rows + PAD), width), F32)],
        compiler_params=pltpu.CompilerParams(vmem_limit_bytes=12 * MIB),
        cost_estimate=cost(9),
        name="refs",
    )(pltpu.with_memory_space_constraint(refs, pltpu.HBM))


def filter_kernel(*args, picked, parts, skip, at, chained):
    bins = None if picked else args[0]
    mine, left, right, *rest = args[0 if picked else 1 :]
    sibs = rest[:parts]
    plain, turned, *token = rest[-6 - chained : -4]
    scratch = rest[-4:]
    for t in token:
        t[...] = jnp.zeros_like(t)
    width = mine.shape[2]
    top = lax.axis_index("section") == 0
    pitch = width + PAD

    def group(base, source, turn):
        scr, scr_t = scratch[2 * turn : 2 * turn + 2]
        for i in range(GROUP):
            b = base + i if picked else bins[skip + base + i]
            a = mine[base + i]
            o = source(i)
            x = jnp.concatenate([jnp.where(top, a, o), jnp.where(top, o, a)], axis=0)
            f = nn(left[b], nn(x, right[b]).astype(BF16))
            scr[pl.ds(i * pitch, width)] = f
            scr_t[pl.ds(i * pitch, width)] = f.T
        to = pl.multiple_of(at + base, GROUP)
        for r in range(width):
            plain[r, pl.ds(to, GROUP)] = scr[pl.ds(r, GROUP, stride=pitch)].astype(BF16)
            turned[r, pl.ds(to, GROUP)] = scr_t[pl.ds(r, GROUP, stride=pitch)].astype(BF16)

    groups = mine.shape[0] // GROUP
    if parts > 1 or groups <= 2:
        places = [(sib, i) for sib in sibs for i in range(sib.shape[0])]
        for g in range(groups):

            def source(i, g=g):
                sib, place = places[g * GROUP + i]
                return sib[place]

            group(g * GROUP, source, g % 2)
    else:

        @pl.loop(0, groups)
        def _(g):
            base = pl.multiple_of(g * GROUP, GROUP)
            group(base, lambda i: sibs[0][base + i], 0)


def filter_chunk(bins, mine, sibs, left, right, buffers, total, skip, at, chained):
    count, half, width = mine.shape
    smem = pl.BlockSpec(memory_space=pltpu.SMEM)
    vmem = pl.BlockSpec(memory_space=pltpu.VMEM)
    parts = len(sibs)
    picked = bins is None
    head = [] if picked else [bins]
    return pl.pallas_call(
        functools.partial(
            filter_kernel, picked=picked, parts=parts, skip=skip, at=at, chained=chained
        ),
        in_specs=[smem] * len(head) + [vmem] * (3 + parts + len(buffers)),
        out_specs=(vmem,) * (2 + chained),
        out_shape=(pinned((2 * half, total, width), BF16),) * 2
        + (pinned((8, width), F32),) * chained,
        scratch_shapes=[pltpu.VMEM((GROUP * (2 * half + PAD), width), F32)] * 4,
        input_output_aliases={len(head) + 3 + parts + i: i for i in range(len(buffers))},
        compiler_params=pltpu.CompilerParams(vmem_limit_bytes=8 * MIB),
        cost_estimate=cost(count * 0.1),
        name="filter",
    )(*head, mine, held(left), held(right), *sibs, *[held(b) for b in buffers])


def pick_kernel(bins, left, right, after, left_out, right_out, *, skip):
    del after
    for i in range(left_out.shape[0]):
        left_out[i] = left[bins[skip + i]]
        right_out[i] = right[bins[skip + i]]


def pick(bins, left, right, after, skip, count):
    vmem = pl.BlockSpec(memory_space=pltpu.VMEM)
    return pl.pallas_call(
        functools.partial(pick_kernel, skip=skip),
        in_specs=[pl.BlockSpec(memory_space=pltpu.SMEM), vmem, vmem, vmem],
        out_shape=(pinned((count,) + left.shape[1:], BF16),) * 2,
        compiler_params=pltpu.CompilerParams(vmem_limit_bytes=4 * MIB),
        cost_estimate=cost(1),
        name="pick",
    )(bins, held(left), held(right), held(after))


def score_kernel(plain, refs, norm, mask, noise, scaled, stats):
    rows, height, width = refs.shape
    count = mask.shape[1]

    def step(i, acc):
        at = [DEEP * i + a for a in range(DEEP)]
        lhs = jnp.concatenate([refs[r] for r in at], axis=1)
        rhs = jnp.concatenate([plain[r] for r in at], axis=1)
        return acc + nt(lhs, rhs)

    inner = lax.fori_loop(0, rows // DEEP, step, jnp.zeros((height, count), F32))
    rots = height // mask.shape[0]
    allowed = jnp.concatenate([mask[...]] * rots, axis=0) > 0
    s = jnp.where(allowed, (inner - norm[:, :1]) / noise[...], LOW)
    scaled[...] = s
    peak = jnp.max(s, axis=0, keepdims=True)
    total = jnp.sum(jnp.exp(s - peak), axis=0, keepdims=True)
    stats[0:1] = peak
    stats[1:2] = total
    stats[2:] = jnp.zeros((stats.shape[0] - 2, count), F32)


def score(plain, refs, norm, mask, noise):
    count = mask.shape[1]
    height = refs.shape[1]
    return pl.pallas_call(
        score_kernel,
        out_shape=(
            pinned((height, count), F32),
            pinned((8, count), F32),
        ),
        compiler_params=pltpu.CompilerParams(vmem_limit_bytes=8 * MIB),
        cost_estimate=cost(5),
        name="score",
    )(held(plain), held(refs), held(norm), held(mask), held(noise))


def shares_kernel(scaled, mine, rot, out):
    rots, padded, _ = rot.shape
    e = jnp.exp(scaled[...] - mine[0:1])
    for q in range(4):
        acc = jnp.zeros((padded, scaled.shape[1]), F32)
        for j in range(rots):
            acc = acc + jnp.where(rot[j][:, :1] == q, e[j * padded : (j + 1) * padded], 0.0)
        out[q] = acc


def make_shares(scaled, mine, rot):
    return pl.pallas_call(
        shares_kernel,
        out_shape=pinned((4, rot.shape[1], scaled.shape[1]), F32),
        compiler_params=pltpu.CompilerParams(vmem_limit_bytes=8 * MIB),
        cost_estimate=cost(1),
        name="shares",
    )(held(scaled), held(mine), held(rot))


def weigh(shares, mine, other, out):
    count = shares.shape[2]
    theirs = jnp.concatenate([other[:, count // 2 :], other[:, : count // 2]], axis=1)
    peak = jnp.maximum(mine[0:1], theirs[0:1])
    near = jnp.exp(mine[0:1] - peak)
    total = mine[1:2] * near + theirs[1:2] * jnp.exp(theirs[0:1] - peak)
    factor = near / total
    for row, pair in enumerate(((0, 3), (2, 1))):
        out[row] = jnp.concatenate([shares[q] * factor for q in pair], axis=1).astype(BF16)


def row_pair(weights, plain, turned, both, classes):
    height, _, width = plain.shape
    direct = jnp.concatenate(
        [jnp.concatenate([plain[i], turned[height - 1 - i]], axis=0) for i in both], axis=1
    )
    mirror = jnp.concatenate(
        [jnp.concatenate([plain[height - 1 - i], turned[i]], axis=0) for i in both], axis=1
    )
    direct = nn(weights[0], direct)
    mirror = nn(weights[1], mirror)
    padded = weights.shape[1]
    flip = width - 1 - lax.broadcasted_iota(jnp.int32, (padded, width), 1)
    return [
        (
            direct[:, at : at + width]
            + jnp.take_along_axis(mirror[:, at : at + width], flip, axis=1)
        )[:classes]
        for at in (0, width)
    ]


def row_place(plain, dom, start):
    half = plain.shape[0] // 2
    first = lax.axis_index("section") * half + start
    return lambda block, r: first + block * (half // dom) + r


def one_side(weights, plain, turned, out, side, dom, start, rows, classes):
    place = row_place(plain, dom, start)
    count = dom // 2

    def pair(g, h):
        for r in range(rows):
            both = [place(2 * k + side, r) for k in (g, h)]
            for k, value in zip((g, h), row_pair(weights, plain, turned, both, classes)):
                out[k, r * classes : (r + 1) * classes] = value.astype(out.dtype)

    if count == 1:
        pair(0, 0)
    else:

        @pl.loop(0, count // 2)
        def _(g):
            pair(2 * g, 2 * g + 1)


def both_sides(weights, plain, turned, out, z, dom, start, rows, classes):
    place = row_place(plain, dom, start)
    for r in range(rows):
        both = [place(2 * z + side, r) for side in range(2)]
        for side, value in enumerate(row_pair(weights, plain, turned, both, classes)):
            out[side, r * classes : (r + 1) * classes] = value.astype(out.dtype)


def inner_kernel(shares, mine, other, plain, turned, send, weights, *, dom, **sizes):
    weigh(shares, mine, other, weights)
    away = 1 - lax.axis_index("dom") % 2
    one_side(weights, plain, turned, send, away, dom, **sizes)


def outer_kernel(weights, plain, turned, after, *outs, dom, **sizes):
    del after
    z = lax.axis_index("dom") // 2
    for m, out in enumerate(outs):
        both_sides(weights, plain, turned, out, jnp.bitwise_xor(z, m + 1), dom, **sizes)


def keep_kernel(weights, plain, turned, after, *outs, dom, classes, inner, outer):
    del after
    own = lax.axis_index("dom")
    one_side(weights, plain, turned, outs[0], own % 2, dom, 0, inner, classes)
    if outer:
        both_sides(weights, plain, turned, outs[1], own // 2, dom, inner, outer, classes)


def call_sums(kernel, args, after, out_shape, rows):
    vmem = pl.BlockSpec(memory_space=pltpu.VMEM)
    return pl.pallas_call(
        kernel,
        in_specs=[vmem] * len(args) + [pl.BlockSpec(memory_space=pl.ANY)] * len(after),
        out_shape=out_shape,
        compiler_params=pltpu.CompilerParams(vmem_limit_bytes=8 * MIB),
        cost_estimate=cost(SUMS * rows),
        name="sums",
    )(*args, *after)


def gather_kernel(keep, *rest, came):
    got = rest[:came]
    here, away = rest[-2:]
    parity = lax.axis_index("dom") % 2
    for out, side in ((here, parity), (away, 1 - parity)):
        value = keep[side]
        for other in got:
            value = value + other[side].astype(F32)
        out[0] = value.astype(out.dtype)


def gather(keep, got):
    shape = (1,) + keep.shape[1:]
    return pl.pallas_call(
        functools.partial(gather_kernel, came=len(got)),
        out_shape=(pinned(shape, F32), jax.ShapeDtypeStruct(shape, BF16)),
        compiler_params=pltpu.CompilerParams(vmem_limit_bytes=8 * MIB),
        cost_estimate=cost(FOLD),
        name="gather",
    )(held(keep), *got)


def fold_kernel(keep, got, *outs, fan, bit):
    outs = outs[-fan:]
    rest = keep.shape[0] // fan
    at = (lax.axis_index("dom") // (1 << bit)) % fan
    for m, out in enumerate(outs):
        for i in range(rest):
            b = i * fan + jnp.bitwise_xor(at, m)
            value = keep[b] + got[b].astype(F32)
            out[i] = value.astype(out.dtype)


def fold(keep, got, after, fan, bit):
    rest = (keep.shape[0] // fan,) + keep.shape[1:]
    return pl.pallas_call(
        functools.partial(fold_kernel, fan=fan, bit=bit),
        in_specs=[pl.BlockSpec(memory_space=pltpu.VMEM)] * 2
        + [pl.BlockSpec(memory_space=pl.ANY)] * len(after),
        out_shape=(pinned(rest, F32),) + (jax.ShapeDtypeStruct(rest, BF16),) * (fan - 1),
        compiler_params=pltpu.CompilerParams(vmem_limit_bytes=8 * MIB),
        cost_estimate=cost(FOLD),
        name="fold",
    )(held(keep), got, *after)


def finish_kernel(*args, counts, classes):
    out = args[-1]
    block_rows = sum(rows for rows, _ in counts)
    at = 0
    row = 0
    for rows, pieces in counts:
        for r in range(rows):
            cut = slice(r * classes, (r + 1) * classes)
            value = args[at][0, cut]
            for other in args[at + 1 : at + pieces]:
                value = value + other[0, cut].astype(F32)
            out[pl.ds(row, classes, stride=block_rows)] = value
            row += 1
        at += pieces


def finish(done, classes):
    counts = tuple((pieces[0].shape[1] // classes, len(pieces)) for pieces in done)
    width = done[0][0].shape[2]
    block_rows = sum(rows for rows, _ in counts)
    flat = [held(p) if i == 0 else p for pieces in done for i, p in enumerate(pieces)]
    out = pl.pallas_call(
        functools.partial(finish_kernel, counts=counts, classes=classes),
        out_shape=jax.ShapeDtypeStruct((classes * block_rows, width), F32),
        compiler_params=pltpu.CompilerParams(vmem_limit_bytes=8 * MIB),
        cost_estimate=cost(1),
        name="finish",
    )(*flat)
    return out.reshape(classes, block_rows, width)


def y_pieces(particles):
    last = GROUP
    middle = particles // 3 // GROUP * GROUP
    return ((particles - middle - last, GROUP), (middle, GROUP // 2), (last, last))


def row_pieces(rows, dom):
    if rows < 4 or dom > 8:
        return (rows, 0)
    outer = rows * 3 // 8
    return (rows - outer, outer)


def local(
    images, defocus_bin, ctf_kernels, band_kernel, references, rot_index, class_mask, noise_var
):
    dom = lax.axis_size("dom")
    particles, half, width = images.shape
    classes = rot_index.shape[0]
    padded = -(-classes // GROUP) * GROUP
    swap = [(0, 1), (1, 0)]
    over_cls = functools.partial(lax.ppermute, axis_name="cls", perm=swap)
    over_section = functools.partial(lax.ppermute, axis_name="section", perm=swap)

    sizes, steps = zip(*y_pieces(particles))
    starts = [sum(sizes[:i]) for i in range(len(sizes))]
    remote = [over_cls(images[a : a + n]) for a, n in zip(starts, sizes)]
    other_bins = over_cls(defocus_bin)
    own_sib = over_section(images)

    refs, norm = lay_refs(references, padded)
    left, right, mask, noise, rot = prepare(
        ctf_kernels, band_kernel, class_mask, noise_var, rot_index.T, norm, padded
    )
    total = 2 * particles
    *buffers, token = filter_chunk(
        defocus_bin, images, [own_sib], left, right, (), total, 0, 0, 1
    )
    chosen = pick(other_bins, left, right, token, starts[-1], sizes[-1])
    tokens = [chosen[0]]
    for i, a in enumerate(starts):
        piece = gate(remote[i], *tokens)
        step = steps[i]
        sibs = [over_section(piece[b : b + step]) for b in range(0, sizes[i], step)]
        last = i + 1 == len(starts)
        filters = (None, piece, sibs, *chosen) if last else (other_bins, piece, sibs, left, right)
        made = filter_chunk(*filters, buffers, total, a, particles + a, int(not last))
        buffers = made[:2]
        tokens = made[2:]
    plain, turned = buffers

    scaled, stats = score(plain, refs, norm, mask, noise)
    theirs = over_cls(stats)
    inputs = (held(make_shares(scaled, stats, rot)), held(stats), theirs)

    def along(x, mask):
        return lax.ppermute(x, "dom", [(i, i ^ mask) for i in range(dom)])

    def spread(sends, bit):
        far_first = sorted(range(len(sends)), reverse=True)
        return [along(sends[m], (m + 1) << bit) for m in far_first]

    inner, outer = row_pieces(half // dom, dom)
    images_in = (held(plain), held(turned))
    count = dom // 2
    send, weights = call_sums(
        functools.partial(
            inner_kernel, dom=dom, start=0, rows=inner, classes=classes
        ),
        inputs + images_in,
        (),
        (
            jax.ShapeDtypeStruct((count, inner * classes, width), BF16),
            pinned((2, rot.shape[1], 2 * total), BF16),
        ),
        inner,
    )
    got = along(send, 1)
    weighted = (held(weights),) + images_in
    keep_shape = (pinned((count, inner * classes, width), F32),)
    after = send
    if outer:
        shape = (2, outer * classes, width)
        sends_b = call_sums(
            functools.partial(
                outer_kernel, dom=dom, start=inner, rows=outer, classes=classes
            ),
            weighted,
            (send,),
            (jax.ShapeDtypeStruct(shape, BF16),) * (count - 1),
            outer,
        )
        got_b = spread(sends_b, 1)
        keep_shape += (pinned(shape, F32),)
        after = sends_b[0]
    keep, *keep_b = call_sums(
        functools.partial(keep_kernel, dom=dom, classes=classes, inner=inner, outer=outer),
        weighted,
        (after,),
        keep_shape,
        inner,
    )
    bit = 1
    while keep.shape[0] > 4:
        keep, send = fold(keep, got, (), 2, bit)
        got = along(send, 1 << bit)
        bit += 1
    keep, *sends = fold(keep, got, (), keep.shape[0], bit)
    done = [[keep] + spread(sends, bit)]
    if outer:
        keep_b, send_b = gather(keep_b[0], got_b)
        done.append([keep_b, along(send_b, 1)])
    return finish(done, classes)


def solution(mesh):
    return jax.shard_map(
        local,
        mesh=mesh,
        in_specs=(
            P(("dom", "cls"), "section", None),
            P(("dom", "cls")),
            P(),
            P(),
            P("cls", None, None, None),
            P("cls", None),
            P("dom", "cls"),
            P("dom"),
        ),
        out_specs=P("cls", ("section", "dom"), None),
        check_vma=False,
    )
```
